32 devices in a mesh: row: 8 (over y, x, core), col: 4 (over z).
Axes of the slice: x: 2, y: 2, z: 4, core: 2. Of those that a mesh axis runs over, the one named last changes fastest.
Arguments:
- chol: float32 [12288, 640], P(('row', 'col')), may hold values from -6 to 6
- eps_occ: float32 [48], replicated, may hold values from -2 to -0.5
- eps_vir: float32 [256], replicated, may hold values from 0.3 to 3
Outputs:
- work: float32 [12288, 640], P(('row', 'col'))
- energies: float32 [2], replicated
The draws below stay inside these ranges and needn't reach their ends.
All inputs are finite; a program needn't handle non-finite values.
Results may differ from the reference program's by a relative error of at most 0.00013.
Values sent between devices are 32-bit elements; how exact they have to be, the bound alone decides.
A program may use at most 192 MiB of HBM per device.

```python
import jax
import jax.numpy as jnp
from jax import lax

NO = 48
NV = 256
NAUX = 640
ITERS = 2
OV = 12288


def block_scale(own_key, shape, shards, least, top_value):
    loudness = 1.0
    for position, parts in shards:
        heights = jax.random.uniform(jax.random.fold_in(jax.random.fold_in(own_key, 6), position), (parts,), jnp.float32, least / len(shards), top_value / len(shards))
        loudness = loudness * jnp.repeat(jnp.exp(heights), shape[position] // parts).reshape((-1,) + (1,) * (len(shape) - 1 - position))
    return loudness


def normal_values(own_key, extent, scale, bound, split=(), kind=jnp.bfloat16):
    entries = jax.random.normal(own_key, extent, jnp.float32) * scale
    if len(split) > 0:
        entries = block_scale(own_key, extent, split, -0.22, 0.18) * entries
    return jnp.clip(entries, min=-bound, max=bound).astype(kind)


def setup_inputs(seed: int = 0) -> dict:
    splits = jax.random.split(jax.random.key(seed), 4)
    return {
        "chol": normal_values(splits[0], (OV, NAUX), 1.0, 6.0, ((0, 32),), jnp.float32),
        "eps_occ": jnp.clip(jax.random.uniform(splits[1], (NO,), jnp.float32, -2.0, -0.5), -2.0, -0.5),
        "eps_vir": jnp.clip(jax.random.uniform(splits[2], (NV,), jnp.float32, 0.3, 3.0), 0.3, 3.0),
    }


def reference(chol, eps_occ, eps_vir):
    total = NV * NO
    pair = (eps_vir[:, None] - eps_occ[None, :]).reshape(total)
    height = 8
    blocks = NV // height
    block_rows = height * NO
    work = jnp.zeros_like(chol)
    energies = []
    for step in range(ITERS):
        factor = chol + work

        def one_block(index):
            rows = lax.dynamic_slice_in_dim(factor, index * block_rows, block_rows, 0)
            row_pair = lax.dynamic_slice_in_dim(pair, index * block_rows, block_rows, 0)
            product = lax.dot_general(rows, factor, (((1,), (1,)), ((), ())), precision=lax.Precision.HIGHEST, preferred_element_type=jnp.float32)
            direct = product.reshape(height, NO, NV, NO)
            numerator = 2.0 * direct - jnp.transpose(direct, (0, 3, 2, 1))
            denominator = row_pair.reshape(height, NO, 1, 1) + pair.reshape(1, 1, NV, NO)
            tile = (-numerator / (jnp.float32(total) * denominator)).reshape(block_rows, total)
            return jnp.dot(tile, chol, precision=lax.Precision.HIGHEST, preferred_element_type=jnp.float32)

        work = lax.map(one_block, jnp.arange(blocks, dtype=jnp.int32)).reshape(total, NAUX)
        energies.append(jnp.sum(chol * work))
    return work, jnp.stack(energies) / jnp.float32(total)
```

```python
import functools

import jax
import jax.numpy as jnp
from jax import lax
from jax.experimental import pallas as pl
from jax.experimental.pallas import tpu as pltpu
from jax.sharding import PartitionSpec as P

ITERS = 2
LANES = 128
NT = (((1,), (1,)), ((), ()))


def split(x):
    high = x.astype(jnp.bfloat16)
    low = (x - high.astype(jnp.float32)).astype(jnp.bfloat16)
    return high, low


def flat(ref, index, turn=None):
    parts = range(ref.shape[0])
    pieces = [ref[part if turn is None else (part + turn) % len(parts), index] for part in parts]
    return pieces[0] if len(pieces) == 1 else jnp.concatenate(pieces, axis=0)


def kernel(steps, turn_ref, rows_ref, cols_ref, chol_ref, rpair_ref, cpair_ref, out_ref, rows, cols, chol, direct, high_tile, low_tile):
    step = pl.program_id(0)
    parts, occupied, shard_virtuals, width = rows_ref.shape
    height = parts * shard_virtuals
    block = occupied // steps
    breadth = cols_ref.shape[0] * cols_ref.shape[2]
    span = block * breadth
    group = LANES // breadth

    @pl.when(step == 0)
    def _():
        def one(index, carry):
            high, low = split(flat(rows_ref, index, turn_ref[0]))
            at = pl.ds(pl.multiple_of(index * height, height), height)
            rows[at, :width] = high
            rows[at, width:] = low
            return carry

        lax.fori_loop(0, occupied, one, 0)

    @pl.when(step < steps)
    def _():
        for index in range(block):
            high, low = split(flat(cols_ref, index))
            cols[index * breadth : (index + 1) * breadth, :width] = low
            cols[index * breadth : (index + 1) * breadth, width:] = high
            high, low = split(flat(chol_ref, index))
            at = pl.ds(pl.multiple_of(step * span + index * breadth, breadth), breadth)
            chol[at, :width] = high
            chol[at, width:] = low

        def one(index, carry):
            at = pl.ds(pl.multiple_of(index * block * height, block * height), block * height)
            value = lax.dot_general(rows[at, :], cols[...], NT, preferred_element_type=jnp.float32)
            value += lax.dot_general(rows[at, :width], cols[:, width:], NT, preferred_element_type=jnp.float32)
            direct[at, pl.ds(pl.multiple_of(step * span, span), span)] = value
            return carry

        lax.fori_loop(0, steps, one, 0)

    @pl.when(step >= steps)
    def _():
        first = (step - steps) * block
        lane = lax.broadcasted_iota(jnp.int32, (height, LANES), 1) // breadth

        def one(index, carry):
            lead = first + index * group
            columns = pl.ds(pl.multiple_of(lead * breadth, LANES), LANES)
            bottoms = [rpair_ref[lead + own] for own in range(group)]
            for other in range(occupied // group):
                swapped = [direct[pl.ds((other * group + m) * height, height), columns] for m in range(group)]
                to = slice(other * LANES, (other + 1) * LANES)
                tops = cpair_ref[other : other + 1, :]
                for own in range(group):
                    exchange = swapped[0] if own == 0 else pltpu.roll(swapped[0], (LANES - own * breadth) % LANES, 1)
                    for m in range(1, group):
                        shift = ((m - own) * breadth) % LANES
                        moved = pltpu.roll(swapped[m], shift, 1) if shift else swapped[m]
                        exchange = jnp.where(lane == m, moved, exchange)
                    at = pl.ds(pl.multiple_of((lead + own) * height, height), height)
                    value = (exchange - 2.0 * direct[at, to]) / (bottoms[own] + tops)
                    high, low = split(value)
                    put = pl.ds(pl.multiple_of((index * group + own) * height, height), height)
                    high_tile[put, to] = high
                    low_tile[put, to] = low
            return carry

        lax.fori_loop(0, block // group, one, 0)
        both = jnp.dot(high_tile[...], chol[...], preferred_element_type=jnp.float32)
        value = both[:, :width] + both[:, width:]
        value += jnp.dot(low_tile[...], chol[:, :width], preferred_element_type=jnp.float32)
        value = value.reshape(block, parts, shard_virtuals, width)
        for part in range(parts):
            out_ref[part] = value[:, part]


def update(turn, rows, cols, chol, rpair, cpair):
    parts, occupied, shard_virtuals, width = rows.shape
    height = parts * shard_virtuals
    breadth = cols.shape[0] * cols.shape[2]
    steps = 6
    block = occupied // steps
    pair_columns = occupied * breadth
    column_block = (cols.shape[0], block, cols.shape[2], width)

    def of_columns(step):
        return (0, jnp.minimum(step, steps - 1), 0, 0)

    return pl.pallas_call(
        functools.partial(kernel, steps),
        grid=(2 * steps,),
        out_shape=jax.ShapeDtypeStruct(rows.shape, jnp.float32),
        in_specs=[
            pl.BlockSpec(memory_space=pltpu.SMEM),
            pl.BlockSpec(rows.shape, lambda step: (0, 0, 0, 0)),
            pl.BlockSpec(column_block, of_columns),
            pl.BlockSpec(column_block, of_columns),
            pl.BlockSpec(rpair.shape, lambda step: (0, 0, 0)),
            pl.BlockSpec(cpair.shape, lambda step: (0, 0)),
        ],
        out_specs=pl.BlockSpec((parts, block, shard_virtuals, width), lambda step: (0, jnp.maximum(step - steps, 0), 0, 0)),
        scratch_shapes=[
            pltpu.VMEM((occupied * height, 2 * width), jnp.bfloat16),
            pltpu.VMEM((block * breadth, 2 * width), jnp.bfloat16),
            pltpu.VMEM((pair_columns, 2 * width), jnp.bfloat16),
            pltpu.VMEM((occupied * height, pair_columns), jnp.float32),
            pltpu.VMEM((block * height, pair_columns), jnp.bfloat16),
            pltpu.VMEM((block * height, pair_columns), jnp.bfloat16),
        ],
        compiler_params=pltpu.CompilerParams(
            dimension_semantics=("arbitrary",), vmem_limit_bytes=66 * 1000 * 1000
        ),
        cost_estimate=pl.CostEstimate(
            flops=12 * occupied * height * pair_columns * width, bytes_accessed=4 * width * (2 * occupied * height + 2 * pair_columns), transcendentals=0
        ),
    )(turn, rows, cols, chol, rpair, cpair)


def gather(x, axis):
    parts = lax.all_gather(x, axis, axis=0)
    if x.shape[1] % 8:
        parts = jnp.transpose(parts, (1, 0, 2, 3)).reshape(1, x.shape[0], -1, x.shape[2])
    return parts


def passed(x, axis):
    n = lax.axis_size(axis)
    blocks = [x]
    for k in range(1, n):
        blocks.append(lax.ppermute(x, axis, [(j, (j - k) % n) for j in range(n)]))
    return jnp.stack(blocks)


PIECES = 4
CORE, ACROSS, UP, DOWN = 0, 1, 2, 3
MESH = pl.DeviceIdType.MESH


def place():
    row = lax.axis_index("row")
    core = lax.rem(row, 2)
    side = lax.rem(lax.div(row, 2), 2)
    half = lax.div(row, 4)
    return row, half, side, core, lax.axis_index("col")


def nearest(col, n_col, order):
    near = jnp.minimum(col, n_col - 1 - col)
    far = order - near
    away = jnp.where(col < n_col - 1 - col, far, -far)
    turn = lax.div(order + 1, 2) * (2 * lax.rem(order, 2) - 1)
    return col + jnp.where(order <= 2 * near, turn, away)


def fused_kernel(
    n_col, chol_ref, rpair_ref, cpair_ref, out_ref, energy_ref, land, held, back, factor, rows, fresh, kept, direct, high_tile, low_tile, total,
    mine, around, along, local_sem, send_sem, recv_sem, held_send, held_recv, back_send, back_recv, ring_send, ring_recv, line_send, line_recv, credit,
):
    row, half, side, core, col = place()
    n_row = 8
    occupied, width = chol_ref.shape[0], chol_ref.shape[2]
    virtuals = chol_ref.shape[1]
    size = occupied * virtuals
    span = occupied * 2 * virtuals
    part = occupied // PIECES
    chunks = 2 * n_col
    group = LANES // (2 * virtuals)
    blocks = occupied // group
    tall = group * virtuals
    partner = (row + 1 - 2 * core, col)
    beside = (row + 2 - 4 * side, col)
    across = (row + 4 - 8 * half, col)
    above = (row, col + 1)
    below = (row, col - 1)
    own_chunk = 2 * col + half

    def slot(chunk, owner, piece):
        return land.at[chunk, pl.ds(piece * part, part), pl.ds(pl.multiple_of(owner * virtuals, virtuals), virtuals), :]

    def move(source, chunk, target, piece, device):
        return pltpu.make_async_remote_copy(
            src_ref=source,
            dst_ref=slot(chunk, core, piece),
            send_sem=send_sem.at[chunk, target, piece],
            recv_sem=recv_sem.at[chunk, core, piece],
            device_id=device,
            device_id_type=MESH,
        )

    def landed(chunk, owner, piece):
        pltpu.make_async_remote_copy(
            src_ref=slot(chunk, owner, piece),
            dst_ref=slot(chunk, owner, piece),
            send_sem=send_sem.at[chunk, CORE, piece],
            recv_sem=recv_sem.at[chunk, owner, piece],
            device_id=partner,
            device_id_type=MESH,
        ).wait_recv()

    def pieces_of(ref, piece):
        return ref.at[pl.ds(piece * part, part), :, :]

    def lend(source, piece):
        return pltpu.make_async_remote_copy(
            src_ref=pieces_of(source, piece), dst_ref=pieces_of(held, piece), send_sem=held_send.at[piece], recv_sem=held_recv.at[piece], device_id=beside, device_id_type=MESH
        )

    def give(piece):
        return pltpu.make_async_remote_copy(
            src_ref=pieces_of(total.at[0], piece), dst_ref=pieces_of(back, piece), send_sem=back_send.at[piece], recv_sem=back_recv.at[piece], device_id=beside, device_id_type=MESH
        )

    def stay(source, piece):
        return pltpu.make_async_copy(pieces_of(source, piece), slot(own_chunk, core, piece), local_sem.at[piece])

    def take(value, start):
        high, low = split(value.reshape(-1, width))
        at = slice(start, start + high.shape[0])
        rows[at, :width] = low
        rows[at, width:] = high

    def publish(source, piece):
        @pl.when(col < n_col - 1)
        def _():
            move(pieces_of(source, piece), own_chunk, UP, piece, above).start()

        @pl.when(col > 0)
        def _():
            move(pieces_of(source, piece), own_chunk, DOWN, piece, below).start()

        lend(source, piece).start()
        move(pieces_of(source, piece), own_chunk, ACROSS, piece, across).start()
        move(pieces_of(source, piece), own_chunk, CORE, piece, partner).start()
        stay(source, piece).start()
        take(source[piece * part : (piece + 1) * part], size + piece * part * virtuals)

    def relay(distance):
        def of(position, target, device, more):
            chunk = 2 * position + half

            def one(piece, carry):
                landed(chunk, core, piece)

                @pl.when(more)
                def _():
                    move(slot(chunk, core, piece), chunk, target, piece, device).start()

                move(slot(chunk, core, piece), chunk, ACROSS, piece, across).start()
                move(slot(chunk, core, piece), chunk, CORE, piece, partner).start()
                return carry

            lax.fori_loop(0, PIECES, one, 0)

        @pl.when(col + distance < n_col)
        def _():
            of(col + distance, DOWN, below, col > 0)

        @pl.when(col >= distance)
        def _():
            of(col - distance, UP, above, col < n_col - 1)

    def cross(chunk):
        def one(piece, carry):
            landed(chunk, core, piece)
            move(slot(chunk, core, piece), chunk, CORE, piece, partner).start()
            return carry

        lax.fori_loop(0, PIECES, one, 0)

    def settle():
        def one(position, carry):
            def each(piece, carry):
                near = 2 * position + half
                source = slot(near, core, piece)
                move(source, near, CORE, piece, partner).wait_send()
                move(source, near, ACROSS, piece, across).wait_send()

                @pl.when((position >= col) & (col > 0))
                def _():
                    move(source, near, DOWN, piece, below).wait_send()

                @pl.when((position <= col) & (col < n_col - 1))
                def _():
                    move(source, near, UP, piece, above).wait_send()

                move(source, 2 * position + 1 - half, CORE, piece, partner).wait_send()
                return carry

            return lax.fori_loop(0, PIECES, each, carry)

        lax.fori_loop(0, n_col, one, 0)
        for piece in range(PIECES):
            lend(factor, piece).wait_send()

    barrier = pltpu.get_barrier_semaphore()

    def greet_row(other, carry):
        pl.semaphore_signal(barrier, inc=1, device_id=(lax.rem(row + other, n_row), col), device_id_type=MESH)
        return carry

    def greet_col(other, carry):
        pl.semaphore_signal(barrier, inc=1, device_id=(row, lax.rem(col + other, n_col)), device_id_type=MESH)
        return carry

    lax.fori_loop(1, n_row, greet_row, 0)
    lax.fori_loop(1, n_col, greet_col, 0)
    pl.semaphore_wait(barrier, n_row + n_col - 2)

    for piece in range(PIECES):
        publish(chol_ref, piece)

    def contract(step, order, chunk, last):
        def convert(index, carry):
            high, low = split(land[chunk, index])
            at = pl.ds(pl.multiple_of(index * 2 * virtuals, 2 * virtuals), 2 * virtuals)
            fresh[at, :width] = high
            fresh[at, width:] = low

            @pl.when(step == 0)
            def _():
                kept[chunk, at, :width] = high
                kept[chunk, at, width:] = low

            return carry

        lax.fori_loop(0, occupied, convert, 0)

        def product(index, carry):
            at = pl.ds(pl.multiple_of(index * 2 * LANES, 2 * LANES), 2 * LANES)
            value = lax.dot_general(rows[...], fresh[at, :], NT, preferred_element_type=jnp.float32)
            value += lax.dot_general(rows[:, width:], fresh[at, :width], NT, preferred_element_type=jnp.float32)
            direct[:, at] = value
            return carry

        lax.fori_loop(0, span // (2 * LANES), product, 0)
        lane = lax.broadcasted_iota(jnp.int32, (virtuals, LANES), 1) // (2 * virtuals)

        def amplitude(index, carry):
            which = lax.div(index, blocks * blocks)
            rest = lax.rem(index, blocks * blocks)
            first, second = lax.div(rest, blocks), lax.rem(rest, blocks)
            at = pl.ds(pl.multiple_of(which * size + first * tall, tall), tall)
            to = pl.ds(pl.multiple_of(second * LANES, LANES), LANES)
            plain = direct[at, to]
            turned = direct[pl.ds(pl.multiple_of(which * size + second * tall, tall), tall), pl.ds(pl.multiple_of(first * LANES, LANES), LANES)]
            turned = [turned[m * virtuals : (m + 1) * virtuals] for m in range(group)]
            stride = group // 2
            while stride:
                lower = (lane & stride) == 0
                shift = stride * 2 * virtuals
                for m in range(group):
                    if not m & stride:
                        one, two = turned[m], turned[m + stride]
                        turned[m] = jnp.where(lower, one, pltpu.roll(two, shift, 1))
                        turned[m + stride] = jnp.where(lower, pltpu.roll(one, LANES - shift, 1), two)
                stride //= 2
            top = cpair_ref[chunk, pl.ds(second, 1), :]
            values = []
            for m in range(group):
                bottom = rpair_ref[which, first * group + m]
                values.append((turned[m] - 2.0 * plain[m * virtuals : (m + 1) * virtuals]) / (bottom + top))
            high, low = split(jnp.concatenate(values, axis=0))
            high_tile[at, to] = high
            low_tile[at, to] = low
            return carry

        lax.fori_loop(0, 2 * blocks * blocks, amplitude, 0)

        def collect(which, carry):
            at = pl.ds(pl.multiple_of(which * size, size), size)
            both = jnp.dot(high_tile[at, :], kept[chunk], preferred_element_type=jnp.float32)
            value = both[:, :width] + both[:, width:]
            value += jnp.dot(low_tile[at, :], kept[chunk, :, :width], preferred_element_type=jnp.float32)
            total[which] += value.reshape(occupied, virtuals, width)

            @pl.when(last & (which == 0))
            def _():
                for piece in range(PIECES):
                    give(piece).start()

            return carry

        lax.fori_loop(0, 2, collect, 0)

    def iterate(step, carry):
        total[...] = jnp.zeros_like(total)
        relay(1)
        for piece in range(PIECES):
            lend(factor, piece).wait_recv()
        take(held[...], 0)
        for piece in range(PIECES):
            stay(factor, piece).wait()

        def one(index, carry):
            order = lax.div(index, 2)
            odd = lax.rem(index, 2)
            position = nearest(col, n_col, order)
            chunk = 2 * position + half + odd * (1 - 2 * half)

            @pl.when((odd == 1) & (order > 0) & (order < n_col - 1))
            def _():
                relay(order + 1)

            @pl.when(odd == 1)
            def _():
                cross(chunk)

            def there(piece, carry):
                landed(chunk, 1 - core, piece)
                return carry

            lax.fori_loop(0, PIECES, there, 0)
            contract(step, order, chunk, index == chunks - 1)
            return carry

        lax.fori_loop(0, chunks, one, 0)
        settle()

        @pl.when(step == 0)
        def _():
            def thank(device):
                pl.semaphore_signal(credit, inc=1, device_id=device, device_id_type=MESH)

            thank(partner)
            thank(beside)
            thank(across)

            @pl.when(col < n_col - 1)
            def _():
                thank(above)

            @pl.when(col > 0)
            def _():
                thank(below)

            pl.semaphore_wait(credit, 3 + jnp.minimum(col, 1) + jnp.minimum(n_col - 1 - col, 1))

        energy = jnp.zeros((virtuals, width), jnp.float32)
        for piece in range(PIECES):
            give(piece).wait_recv()
            at = slice(piece * part, (piece + 1) * part)
            value = total[1, at] + back[at]
            energy += jnp.sum(chol_ref[at] * value, axis=0)

            @pl.when(step == 0)
            def _():
                factor[at] = chol_ref[at] + value
                publish(factor, piece)

            @pl.when(step == ITERS - 1)
            def _():
                out_ref[at] = value

        folded = energy[:, :LANES]
        for index in range(1, width // LANES):
            folded += energy[:, index * LANES : (index + 1) * LANES]
        mine[step] = folded
        for piece in range(PIECES):
            give(piece).wait_send()
        return carry

    lax.fori_loop(0, ITERS, iterate, 0)

    def to_ring(other):
        return pltpu.make_async_remote_copy(
            src_ref=mine, dst_ref=around.at[row], send_sem=ring_send.at[other], recv_sem=ring_recv.at[row], device_id=(lax.rem(row + other, n_row), col), device_id_type=MESH
        )

    def from_ring(other):
        source = lax.rem(row + other, n_row)
        return pltpu.make_async_remote_copy(
            src_ref=mine, dst_ref=around.at[source], send_sem=ring_send.at[other], recv_sem=ring_recv.at[source], device_id=(source, col), device_id_type=MESH
        )

    for other in range(1, n_row):
        to_ring(other).start()
    around[row] = mine[...]
    for other in range(1, n_row):
        from_ring(other).wait_recv()
    for other in range(1, n_row):
        to_ring(other).wait_send()
    mine[...] = sum(around[index] for index in range(n_row))

    def to_line(other):
        return pltpu.make_async_remote_copy(
            src_ref=mine, dst_ref=along.at[col], send_sem=line_send.at[other], recv_sem=line_recv.at[col], device_id=(row, lax.rem(col + other, n_col)), device_id_type=MESH
        )

    def from_line(other):
        source = lax.rem(col + other, n_col)
        return pltpu.make_async_remote_copy(
            src_ref=mine, dst_ref=along.at[source], send_sem=line_send.at[other], recv_sem=line_recv.at[source], device_id=(row, source), device_id_type=MESH
        )

    for other in range(1, n_col):
        to_line(other).start()
    along[col] = mine[...]
    for other in range(1, n_col):
        from_line(other).wait_recv()
    for other in range(1, n_col):
        to_line(other).wait_send()
    energy_ref[...] = sum(along[index] for index in range(n_col))


def fused(chol, eps_occ, eps_vir):
    n_col = lax.axis_size("col")
    n_row = lax.axis_size("row")
    row, half, side, core, col = place()
    shard, width = chol.shape
    occupied = eps_occ.shape[0]
    virtuals = shard // occupied
    scale = jnp.float32(eps_vir.shape[0] * occupied)
    size, span = shard, 2 * shard
    by_place = eps_vir.reshape(n_row // 4, 2, 2, n_col, virtuals)
    own = lax.dynamic_index_in_dim(by_place, side, 1, False)
    columns = jnp.transpose(own, (2, 0, 1, 3)).reshape(2 * n_col, 1, 2 * virtuals)
    cpair = (scale * (columns - eps_occ[None, :, None])).reshape(2 * n_col, span // LANES, LANES)
    by_device = eps_vir.reshape(n_row, n_col, virtuals)
    pair = jnp.stack([by_device[row + 2 - 4 * side, col], by_device[row, col]])
    rpair = scale * (pair[:, None, :] - eps_occ[None, :, None])
    rpair = jnp.broadcast_to(rpair[:, :, :, None], (2, occupied, virtuals, LANES))
    chol_t = jnp.transpose(chol.reshape(virtuals, occupied, width), (1, 0, 2))
    shape = (occupied, virtuals, width)
    dma = pltpu.SemaphoreType.DMA
    work, energies = pl.pallas_call(
        functools.partial(fused_kernel, n_col),
        out_shape=(jax.ShapeDtypeStruct(shape, jnp.float32), jax.ShapeDtypeStruct((ITERS, virtuals, LANES), jnp.float32)),
        in_specs=[pl.BlockSpec(memory_space=pltpu.VMEM)] * 3,
        out_specs=(pl.BlockSpec(memory_space=pltpu.VMEM), pl.BlockSpec(memory_space=pltpu.VMEM)),
        scratch_shapes=[
            pltpu.VMEM((2 * n_col, occupied, 2 * virtuals, width), jnp.float32),
            pltpu.VMEM(shape, jnp.float32),
            pltpu.VMEM(shape, jnp.float32),
            pltpu.VMEM(shape, jnp.float32),
            pltpu.VMEM((2 * size, 2 * width), jnp.bfloat16),
            pltpu.VMEM((span, 2 * width), jnp.bfloat16),
            pltpu.VMEM((2 * n_col, span, 2 * width), jnp.bfloat16),
            pltpu.VMEM((2 * size, span), jnp.float32),
            pltpu.VMEM((2 * size, span), jnp.bfloat16),
            pltpu.VMEM((2 * size, span), jnp.bfloat16),
            pltpu.VMEM((2,) + shape, jnp.float32),
            pltpu.VMEM((ITERS, virtuals, LANES), jnp.float32),
            pltpu.VMEM((n_row, ITERS, virtuals, LANES), jnp.float32),
            pltpu.VMEM((n_col, ITERS, virtuals, LANES), jnp.float32),
            dma((PIECES,)),
            dma((2 * n_col, 4, PIECES)),
            dma((2 * n_col, 2, PIECES)),
            dma((PIECES,)),
            dma((PIECES,)),
            dma((PIECES,)),
            dma((PIECES,)),
            dma((n_row,)),
            dma((n_row,)),
            dma((n_col,)),
            dma((n_col,)),
            pltpu.SemaphoreType.REGULAR,
        ],
        compiler_params=pltpu.CompilerParams(collective_id=0, has_side_effects=True, vmem_limit_bytes=66 * 1000 * 1000),
    )(chol_t, rpair, cpair)
    return jnp.transpose(work, (1, 0, 2)).reshape(shard, width), jnp.sum(energies, axis=(1, 2)) / scale


def shards(chol, eps_occ, eps_vir):
    if lax.axis_size("row") == 8 and chol.shape[0] == 8 * eps_occ.shape[0]:
        return fused(chol, eps_occ, eps_vir)
    n_row = lax.axis_size("row")
    n_col = lax.axis_size("col")
    row_index = lax.axis_index("row")
    col_index = lax.axis_index("col")
    shard, width = chol.shape
    occupied = eps_occ.shape[0]
    virtual = eps_vir.shape[0]
    shard_virtuals = shard // occupied
    block_virtuals = n_col * shard_virtuals
    total = virtual * occupied
    scale = jnp.float32(total)
    row_vir = lax.dynamic_slice_in_dim(eps_vir, row_index * block_virtuals, block_virtuals, 0)
    col_vir = lax.dynamic_slice_in_dim(
        eps_vir.reshape(n_row, block_virtuals), col_index * shard_virtuals, shard_virtuals, 1
    ).reshape(n_row * shard_virtuals)
    rpair = scale * (row_vir[None, :] - eps_occ[:, None])
    rpair = jnp.broadcast_to(rpair[:, :, None], (occupied, block_virtuals, LANES))
    cpair = (scale * (col_vir[None, :] - eps_occ[:, None])).reshape(-1, LANES)
    chol_t = jnp.transpose(chol.reshape(shard_virtuals, occupied, width), (1, 0, 2))
    chol_cols = gather(chol_t, "row")
    factor = chol_t
    sums = []
    for step in range(ITERS):
        if shard_virtuals % 8:
            rows = gather(factor, "col")
            turn = jnp.zeros((1,), jnp.int32)
        else:
            rows = passed(factor, "col")
            turn = jnp.full((1,), n_col - col_index, jnp.int32)
        cols = chol_cols if step == 0 else gather(factor, "row")
        partial_value = update(turn, rows, cols, chol_cols, rpair, cpair)
        if shard_virtuals % 8:
            partial_value = jnp.transpose(
                partial_value.reshape(occupied, n_col, shard_virtuals, width), (1, 0, 2, 3)
            )
        work = lax.psum_scatter(partial_value, "col", scatter_dimension=0, tiled=False)
        factor = chol_t + work
        sums.append(jnp.sum(chol_t * work))
    energies = lax.psum(jnp.stack(sums), ("row", "col"))
    return jnp.transpose(work, (1, 0, 2)).reshape(shard, width), energies / scale


def solution(mesh):
    placed = (P(("row", "col"), None), P(), P())
    return jax.shard_map(
        shards,
        mesh=mesh,
        in_specs=placed,
        out_specs=(P(("row", "col"), None), P()),
        check_vma=False,
    )
```

```python
import functools

import jax
import jax.numpy as jnp
from jax import lax
from jax.experimental import pallas as pl
from jax.experimental.pallas import tpu as pltpu
from jax.sharding import PartitionSpec as P

ITERS = 2
LANES = 128
NT = (((1,), (1,)), ((), ()))


def split(x):
    high = x.astype(jnp.bfloat16)
    low = (x - high.astype(jnp.float32)).astype(jnp.bfloat16)
    return high, low


def flat(ref, index, turn=None):
    parts = range(ref.shape[0])
    pieces = [ref[part if turn is None else (part + turn) % len(parts), index] for part in parts]
    return pieces[0] if len(pieces) == 1 else jnp.concatenate(pieces, axis=0)


def kernel(steps, turn_ref, rows_ref, cols_ref, chol_ref, rpair_ref, cpair_ref, out_ref, rows, cols, chol, direct, high_tile, low_tile):
    step = pl.program_id(0)
    parts, occupied, shard_virtuals, width = rows_ref.shape
    height = parts * shard_virtuals
    block = occupied // steps
    breadth = cols_ref.shape[0] * cols_ref.shape[2]
    span = block * breadth
    group = LANES // breadth

    @pl.when(step == 0)
    def _():
        def one(index, carry):
            high, low = split(flat(rows_ref, index, turn_ref[0]))
            at = pl.ds(pl.multiple_of(index * height, height), height)
            rows[at, :width] = high
            rows[at, width:] = low
            return carry

        lax.fori_loop(0, occupied, one, 0)

    @pl.when(step < steps)
    def _():
        for index in range(block):
            high, low = split(flat(cols_ref, index))
            cols[index * breadth : (index + 1) * breadth, :width] = low
            cols[index * breadth : (index + 1) * breadth, width:] = high
            high, low = split(flat(chol_ref, index))
            at = pl.ds(pl.multiple_of(step * span + index * breadth, breadth), breadth)
            chol[at, :width] = high
            chol[at, width:] = low

        def one(index, carry):
            at = pl.ds(pl.multiple_of(index * block * height, block * height), block * height)
            value = lax.dot_general(rows[at, :], cols[...], NT, preferred_element_type=jnp.float32)
            value += lax.dot_general(rows[at, :width], cols[:, width:], NT, preferred_element_type=jnp.float32)
            direct[at, pl.ds(pl.multiple_of(step * span, span), span)] = value
            return carry

        lax.fori_loop(0, steps, one, 0)

    @pl.when(step >= steps)
    def _():
        first = (step - steps) * block
        lane = lax.broadcasted_iota(jnp.int32, (height, LANES), 1) // breadth

        def one(index, carry):
            lead = first + index * group
            columns = pl.ds(pl.multiple_of(lead * breadth, LANES), LANES)
            bottoms = [rpair_ref[lead + own] for own in range(group)]
            for other in range(occupied // group):
                swapped = [direct[pl.ds((other * group + m) * height, height), columns] for m in range(group)]
                to = slice(other * LANES, (other + 1) * LANES)
                tops = cpair_ref[other : other + 1, :]
                for own in range(group):
                    exchange = swapped[0] if own == 0 else pltpu.roll(swapped[0], (LANES - own * breadth) % LANES, 1)
                    for m in range(1, group):
                        shift = ((m - own) * breadth) % LANES
                        moved = pltpu.roll(swapped[m], shift, 1) if shift else swapped[m]
                        exchange = jnp.where(lane == m, moved, exchange)
                    at = pl.ds(pl.multiple_of((lead + own) * height, height), height)
                    value = (exchange - 2.0 * direct[at, to]) / (bottoms[own] + tops)
                    high, low = split(value)
                    put = pl.ds(pl.multiple_of((index * group + own) * height, height), height)
                    high_tile[put, to] = high
                    low_tile[put, to] = low
            return carry

        lax.fori_loop(0, block // group, one, 0)
        both = jnp.dot(high_tile[...], chol[...], preferred_element_type=jnp.float32)
        value = both[:, :width] + both[:, width:]
        value += jnp.dot(low_tile[...], chol[:, :width], preferred_element_type=jnp.float32)
        value = value.reshape(block, parts, shard_virtuals, width)
        for part in range(parts):
            out_ref[part] = value[:, part]


def update(turn, rows, cols, chol, rpair, cpair):
    parts, occupied, shard_virtuals, width = rows.shape
    height = parts * shard_virtuals
    breadth = cols.shape[0] * cols.shape[2]
    steps = 6
    block = occupied // steps
    pair_columns = occupied * breadth
    column_block = (cols.shape[0], block, cols.shape[2], width)

    def of_columns(step):
        return (0, jnp.minimum(step, steps - 1), 0, 0)

    return pl.pallas_call(
        functools.partial(kernel, steps),
        grid=(2 * steps,),
        out_shape=jax.ShapeDtypeStruct(rows.shape, jnp.float32),
        in_specs=[
            pl.BlockSpec(memory_space=pltpu.SMEM),
            pl.BlockSpec(rows.shape, lambda step: (0, 0, 0, 0)),
            pl.BlockSpec(column_block, of_columns),
            pl.BlockSpec(column_block, of_columns),
            pl.BlockSpec(rpair.shape, lambda step: (0, 0, 0)),
            pl.BlockSpec(cpair.shape, lambda step: (0, 0)),
        ],
        out_specs=pl.BlockSpec((parts, block, shard_virtuals, width), lambda step: (0, jnp.maximum(step - steps, 0), 0, 0)),
        scratch_shapes=[
            pltpu.VMEM((occupied * height, 2 * width), jnp.bfloat16),
            pltpu.VMEM((block * breadth, 2 * width), jnp.bfloat16),
            pltpu.VMEM((pair_columns, 2 * width), jnp.bfloat16),
            pltpu.VMEM((occupied * height, pair_columns), jnp.float32),
            pltpu.VMEM((block * height, pair_columns), jnp.bfloat16),
            pltpu.VMEM((block * height, pair_columns), jnp.bfloat16),
        ],
        compiler_params=pltpu.CompilerParams(
            dimension_semantics=("arbitrary",), vmem_limit_bytes=66 * 1000 * 1000
        ),
        cost_estimate=pl.CostEstimate(
            flops=12 * occupied * height * pair_columns * width, bytes_accessed=4 * width * (2 * occupied * height + 2 * pair_columns), transcendentals=0
        ),
    )(turn, rows, cols, chol, rpair, cpair)


def gather(x, axis):
    parts = lax.all_gather(x, axis, axis=0)
    if x.shape[1] % 8:
        parts = jnp.transpose(parts, (1, 0, 2, 3)).reshape(1, x.shape[0], -1, x.shape[2])
    return parts


def passed(x, axis):
    n = lax.axis_size(axis)
    blocks = [x]
    for k in range(1, n):
        blocks.append(lax.ppermute(x, axis, [(j, (j - k) % n) for j in range(n)]))
    return jnp.stack(blocks)


PIECES = 4
CORE, ACROSS, UP, DOWN = 0, 1, 2, 3
MESH = pl.DeviceIdType.MESH


def place():
    row = lax.axis_index("row")
    core = lax.rem(row, 2)
    side = lax.rem(lax.div(row, 2), 2)
    half = lax.div(row, 4)
    return row, half, side, core, lax.axis_index("col")


def nearest(col, n_col, order):
    near = jnp.minimum(col, n_col - 1 - col)
    far = order - near
    away = jnp.where(col < n_col - 1 - col, far, -far)
    turn = lax.div(order + 1, 2) * (2 * lax.rem(order, 2) - 1)
    return col + jnp.where(order <= 2 * near, turn, away)


def fused_kernel(
    n_col, chol_ref, rpair_ref, cpair_ref, out_ref, energy_ref, land, held, back, factor, rows, fresh, kept, direct, high_tile, low_tile, total,
    mine, around, along, local_sem, send_sem, recv_sem, held_send, held_recv, back_send, back_recv, ring_send, ring_recv, line_send, line_recv, credit,
):
    row, half, side, core, col = place()
    n_row = 8
    occupied, width = chol_ref.shape[0], chol_ref.shape[2]
    virtuals = chol_ref.shape[1]
    size = occupied * virtuals
    span = occupied * 2 * virtuals
    part = occupied // PIECES
    chunks = 2 * n_col
    group = LANES // (2 * virtuals)
    blocks = occupied // group
    tall = group * virtuals
    partner = (row + 1 - 2 * core, col)
    beside = (row + 2 - 4 * side, col)
    across = (row + 4 - 8 * half, col)
    above = (row, col + 1)
    below = (row, col - 1)
    own_chunk = 2 * col + half

    def slot(chunk, owner, piece):
        return land.at[chunk, pl.ds(piece * part, part), pl.ds(pl.multiple_of(owner * virtuals, virtuals), virtuals), :]

    def move(source, chunk, target, piece, device):
        return pltpu.make_async_remote_copy(
            src_ref=source,
            dst_ref=slot(chunk, core, piece),
            send_sem=send_sem.at[chunk, target, piece],
            recv_sem=recv_sem.at[chunk, core, piece],
            device_id=device,
            device_id_type=MESH,
        )

    def landed(chunk, owner, piece):
        pltpu.make_async_remote_copy(
            src_ref=slot(chunk, owner, piece),
            dst_ref=slot(chunk, owner, piece),
            send_sem=send_sem.at[chunk, CORE, piece],
            recv_sem=recv_sem.at[chunk, owner, piece],
            device_id=partner,
            device_id_type=MESH,
        ).wait_recv()

    def pieces_of(ref, piece):
        return ref.at[pl.ds(piece * part, part), :, :]

    def lend(source, piece):
        return pltpu.make_async_remote_copy(
            src_ref=pieces_of(source, piece), dst_ref=pieces_of(held, piece), send_sem=held_send.at[piece], recv_sem=held_recv.at[piece], device_id=beside, device_id_type=MESH
        )

    def give(piece):
        return pltpu.make_async_remote_copy(
            src_ref=pieces_of(total.at[0], piece), dst_ref=pieces_of(back, piece), send_sem=back_send.at[piece], recv_sem=back_recv.at[piece], device_id=beside, device_id_type=MESH
        )

    def stay(source, piece):
        return pltpu.make_async_copy(pieces_of(source, piece), slot(own_chunk, core, piece), local_sem.at[piece])

    def take(value, start):
        high, low = split(value.reshape(-1, width))
        at = slice(start, start + high.shape[0])
        rows[at, :width] = low
        rows[at, width:] = high

    def publish(source, piece):
        @pl.when(col < n_col - 1)
        def _():
            move(pieces_of(source, piece), own_chunk, UP, piece, above).start()

        @pl.when(col > 0)
        def _():
            move(pieces_of(source, piece), own_chunk, DOWN, piece, below).start()

        lend(source, piece).start()
        move(pieces_of(source, piece), own_chunk, ACROSS, piece, across).start()
        move(pieces_of(source, piece), own_chunk, CORE, piece, partner).start()
        stay(source, piece).start()
        take(source[piece * part : (piece + 1) * part], size + piece * part * virtuals)

    def relay(distance):
        def of(position, target, device, more):
            chunk = 2 * position + half

            def one(piece, carry):
                landed(chunk, core, piece)

                @pl.when(more)
                def _():
                    move(slot(chunk, core, piece), chunk, target, piece, device).start()

                move(slot(chunk, core, piece), chunk, ACROSS, piece, across).start()
                move(slot(chunk, core, piece), chunk, CORE, piece, partner).start()
                return carry

            lax.fori_loop(0, PIECES, one, 0)

        @pl.when(col + distance < n_col)
        def _():
            of(col + distance, DOWN, below, col > 0)

        @pl.when(col >= distance)
        def _():
            of(col - distance, UP, above, col < n_col - 1)

    def cross(chunk):
        def one(piece, carry):
            landed(chunk, core, piece)
            move(slot(chunk, core, piece), chunk, CORE, piece, partner).start()
            return carry

        lax.fori_loop(0, PIECES, one, 0)

    def settle():
        def one(position, carry):
            def each(piece, carry):
                near = 2 * position + half
                source = slot(near, core, piece)
                move(source, near, CORE, piece, partner).wait_send()
                move(source, near, ACROSS, piece, across).wait_send()

                @pl.when((position >= col) & (col > 0))
                def _():
                    move(source, near, DOWN, piece, below).wait_send()

                @pl.when((position <= col) & (col < n_col - 1))
                def _():
                    move(source, near, UP, piece, above).wait_send()

                move(source, 2 * position + 1 - half, CORE, piece, partner).wait_send()
                return carry

            return lax.fori_loop(0, PIECES, each, carry)

        lax.fori_loop(0, n_col, one, 0)
        for piece in range(PIECES):
            lend(factor, piece).wait_send()

    barrier = pltpu.get_barrier_semaphore()

    def greet_row(other, carry):
        pl.semaphore_signal(barrier, inc=1, device_id=(lax.rem(row + other, n_row), col), device_id_type=MESH)
        return carry

    def greet_col(other, carry):
        pl.semaphore_signal(barrier, inc=1, device_id=(row, lax.rem(col + other, n_col)), device_id_type=MESH)
        return carry

    lax.fori_loop(1, n_row, greet_row, 0)
    lax.fori_loop(1, n_col, greet_col, 0)
    pl.semaphore_wait(barrier, n_row + n_col - 2)

    for piece in range(PIECES):
        publish(chol_ref, piece)

    def contract(step, order, chunk, last):
        def convert(index, carry):
            high, low = split(land[chunk, index])
            at = pl.ds(pl.multiple_of(index * 2 * virtuals, 2 * virtuals), 2 * virtuals)
            fresh[at, :width] = high
            fresh[at, width:] = low

            @pl.when(step == 0)
            def _():
                kept[chunk, at, :width] = high
                kept[chunk, at, width:] = low

            return carry

        lax.fori_loop(0, occupied, convert, 0, unroll=8)

        value = lax.dot_general(rows[...], fresh[...], NT, preferred_element_type=jnp.float32)
        value += lax.dot_general(rows[:, width:], fresh[:, :width], NT, preferred_element_type=jnp.float32)
        direct[...] = value
        lane = lax.broadcasted_iota(jnp.int32, (virtuals, LANES), 1) // (2 * virtuals)

        def amplitude(index, carry):
            which = lax.div(index, blocks * blocks)
            rest = lax.rem(index, blocks * blocks)
            first, second = lax.div(rest, blocks), lax.rem(rest, blocks)
            at = pl.ds(pl.multiple_of(which * size + first * tall, tall), tall)
            to = pl.ds(pl.multiple_of(second * LANES, LANES), LANES)
            plain = direct[at, to]
            turned = direct[pl.ds(pl.multiple_of(which * size + second * tall, tall), tall), pl.ds(pl.multiple_of(first * LANES, LANES), LANES)]
            turned = [turned[m * virtuals : (m + 1) * virtuals] for m in range(group)]
            stride = group // 2
            while stride:
                lower = (lane & stride) == 0
                shift = stride * 2 * virtuals
                for m in range(group):
                    if not m & stride:
                        one, two = turned[m], turned[m + stride]
                        turned[m] = jnp.where(lower, one, pltpu.roll(two, shift, 1))
                        turned[m + stride] = jnp.where(lower, pltpu.roll(one, LANES - shift, 1), two)
                stride //= 2
            top = cpair_ref[chunk, pl.ds(second, 1), :]
            values = []
            for m in range(group):
                bottom = rpair_ref[which, first * group + m]
                values.append((turned[m] - 2.0 * plain[m * virtuals : (m + 1) * virtuals]) / (bottom + top))
            high, low = split(jnp.concatenate(values, axis=0))
            high_tile[at, to] = high
            low_tile[at, to] = low
            return carry

        lax.fori_loop(0, 2 * blocks * blocks, amplitude, 0, unroll=9)

        def collect(which, carry):
            at = pl.ds(pl.multiple_of(which * size, size), size)
            both = jnp.dot(high_tile[at, :], kept[chunk], preferred_element_type=jnp.float32)
            value = both[:, :width] + both[:, width:]
            value += jnp.dot(low_tile[at, :], kept[chunk, :, :width], preferred_element_type=jnp.float32)
            total[which] += value.reshape(occupied, virtuals, width)

            @pl.when(last & (which == 0))
            def _():
                for piece in range(PIECES):
                    give(piece).start()

            return carry

        lax.fori_loop(0, 2, collect, 0)

    def iterate(step, carry):
        total[...] = jnp.zeros_like(total)
        relay(1)
        for piece in range(PIECES):
            lend(factor, piece).wait_recv()
        take(held[...], 0)
        for piece in range(PIECES):
            stay(factor, piece).wait()

        def one(index, carry):
            order = lax.div(index, 2)
            odd = lax.rem(index, 2)
            position = nearest(col, n_col, order)
            chunk = 2 * position + half + odd * (1 - 2 * half)

            @pl.when((odd == 1) & (order > 0) & (order < n_col - 1))
            def _():
                relay(order + 1)

            @pl.when(odd == 1)
            def _():
                cross(chunk)

            def there(piece, carry):
                landed(chunk, 1 - core, piece)
                return carry

            lax.fori_loop(0, PIECES, there, 0)
            contract(step, order, chunk, index == chunks - 1)
            return carry

        lax.fori_loop(0, chunks, one, 0)
        settle()

        @pl.when(step == 0)
        def _():
            def thank(device):
                pl.semaphore_signal(credit, inc=1, device_id=device, device_id_type=MESH)

            thank(partner)
            thank(beside)
            thank(across)

            @pl.when(col < n_col - 1)
            def _():
                thank(above)

            @pl.when(col > 0)
            def _():
                thank(below)

            pl.semaphore_wait(credit, 3 + jnp.minimum(col, 1) + jnp.minimum(n_col - 1 - col, 1))

        energy = jnp.zeros((virtuals, width), jnp.float32)
        for piece in range(PIECES):
            give(piece).wait_recv()
            at = slice(piece * part, (piece + 1) * part)
            value = total[1, at] + back[at]
            energy += jnp.sum(chol_ref[at] * value, axis=0)

            @pl.when(step == 0)
            def _():
                factor[at] = chol_ref[at] + value
                publish(factor, piece)

            @pl.when(step == ITERS - 1)
            def _():
                out_ref[at] = value

        folded = energy[:, :LANES]
        for index in range(1, width // LANES):
            folded += energy[:, index * LANES : (index + 1) * LANES]
        mine[step] = folded
        for piece in range(PIECES):
            give(piece).wait_send()
        return carry

    lax.fori_loop(0, ITERS, iterate, 0)

    def to_ring(other):
        return pltpu.make_async_remote_copy(
            src_ref=mine, dst_ref=around.at[row], send_sem=ring_send.at[other], recv_sem=ring_recv.at[row], device_id=(lax.rem(row + other, n_row), col), device_id_type=MESH
        )

    def from_ring(other):
        source = lax.rem(row + other, n_row)
        return pltpu.make_async_remote_copy(
            src_ref=mine, dst_ref=around.at[source], send_sem=ring_send.at[other], recv_sem=ring_recv.at[source], device_id=(source, col), device_id_type=MESH
        )

    for other in range(1, n_row):
        to_ring(other).start()
    around[row] = mine[...]
    for other in range(1, n_row):
        from_ring(other).wait_recv()
    for other in range(1, n_row):
        to_ring(other).wait_send()
    mine[...] = sum(around[index] for index in range(n_row))

    def to_line(other):
        return pltpu.make_async_remote_copy(
            src_ref=mine, dst_ref=along.at[col], send_sem=line_send.at[other], recv_sem=line_recv.at[col], device_id=(row, lax.rem(col + other, n_col)), device_id_type=MESH
        )

    def from_line(other):
        source = lax.rem(col + other, n_col)
        return pltpu.make_async_remote_copy(
            src_ref=mine, dst_ref=along.at[source], send_sem=line_send.at[other], recv_sem=line_recv.at[source], device_id=(row, source), device_id_type=MESH
        )

    for other in range(1, n_col):
        to_line(other).start()
    along[col] = mine[...]
    for other in range(1, n_col):
        from_line(other).wait_recv()
    for other in range(1, n_col):
        to_line(other).wait_send()
    energy_ref[...] = sum(along[index] for index in range(n_col))


def fused(chol, eps_occ, eps_vir):
    n_col = lax.axis_size("col")
    n_row = lax.axis_size("row")
    row, half, side, core, col = place()
    shard, width = chol.shape
    occupied = eps_occ.shape[0]
    virtuals = shard // occupied
    scale = jnp.float32(eps_vir.shape[0] * occupied)
    size, span = shard, 2 * shard
    by_place = eps_vir.reshape(n_row // 4, 2, 2, n_col, virtuals)
    own = lax.dynamic_index_in_dim(by_place, side, 1, False)
    columns = jnp.transpose(own, (2, 0, 1, 3)).reshape(2 * n_col, 1, 2 * virtuals)
    cpair = (scale * (columns - eps_occ[None, :, None])).reshape(2 * n_col, span // LANES, LANES)
    by_device = eps_vir.reshape(n_row, n_col, virtuals)
    pair = jnp.stack([by_device[row + 2 - 4 * side, col], by_device[row, col]])
    rpair = scale * (pair[:, None, :] - eps_occ[None, :, None])
    rpair = jnp.broadcast_to(rpair[:, :, :, None], (2, occupied, virtuals, LANES))
    chol_t = jnp.transpose(chol.reshape(virtuals, occupied, width), (1, 0, 2))
    shape = (occupied, virtuals, width)
    dma = pltpu.SemaphoreType.DMA
    work, energies = pl.pallas_call(
        functools.partial(fused_kernel, n_col),
        out_shape=(jax.ShapeDtypeStruct(shape, jnp.float32), jax.ShapeDtypeStruct((ITERS, virtuals, LANES), jnp.float32)),
        in_specs=[pl.BlockSpec(memory_space=pltpu.VMEM)] * 3,
        out_specs=(pl.BlockSpec(memory_space=pltpu.VMEM), pl.BlockSpec(memory_space=pltpu.VMEM)),
        scratch_shapes=[
            pltpu.VMEM((2 * n_col, occupied, 2 * virtuals, width), jnp.float32),
            pltpu.VMEM(shape, jnp.float32),
            pltpu.VMEM(shape, jnp.float32),
            pltpu.VMEM(shape, jnp.float32),
            pltpu.VMEM((2 * size, 2 * width), jnp.bfloat16),
            pltpu.VMEM((span, 2 * width), jnp.bfloat16),
            pltpu.VMEM((2 * n_col, span, 2 * width), jnp.bfloat16),
            pltpu.VMEM((2 * size, span), jnp.float32),
            pltpu.VMEM((2 * size, span), jnp.bfloat16),
            pltpu.VMEM((2 * size, span), jnp.bfloat16),
            pltpu.VMEM((2,) + shape, jnp.float32),
            pltpu.VMEM((ITERS, virtuals, LANES), jnp.float32),
            pltpu.VMEM((n_row, ITERS, virtuals, LANES), jnp.float32),
            pltpu.VMEM((n_col, ITERS, virtuals, LANES), jnp.float32),
            dma((PIECES,)),
            dma((2 * n_col, 4, PIECES)),
            dma((2 * n_col, 2, PIECES)),
            dma((PIECES,)),
            dma((PIECES,)),
            dma((PIECES,)),
            dma((PIECES,)),
            dma((n_row,)),
            dma((n_row,)),
            dma((n_col,)),
            dma((n_col,)),
            pltpu.SemaphoreType.REGULAR,
        ],
        compiler_params=pltpu.CompilerParams(collective_id=0, has_side_effects=True, vmem_limit_bytes=66 * 1000 * 1000),
    )(chol_t, rpair, cpair)
    return jnp.transpose(work, (1, 0, 2)).reshape(shard, width), jnp.sum(energies, axis=(1, 2)) / scale


def shards(chol, eps_occ, eps_vir):
    if lax.axis_size("row") == 8 and chol.shape[0] == 8 * eps_occ.shape[0]:
        return fused(chol, eps_occ, eps_vir)
    n_row = lax.axis_size("row")
    n_col = lax.axis_size("col")
    row_index = lax.axis_index("row")
    col_index = lax.axis_index("col")
    shard, width = chol.shape
    occupied = eps_occ.shape[0]
    virtual = eps_vir.shape[0]
    shard_virtuals = shard // occupied
    block_virtuals = n_col * shard_virtuals
    total = virtual * occupied
    scale = jnp.float32(total)
    row_vir = lax.dynamic_slice_in_dim(eps_vir, row_index * block_virtuals, block_virtuals, 0)
    col_vir = lax.dynamic_slice_in_dim(
        eps_vir.reshape(n_row, block_virtuals), col_index * shard_virtuals, shard_virtuals, 1
    ).reshape(n_row * shard_virtuals)
    rpair = scale * (row_vir[None, :] - eps_occ[:, None])
    rpair = jnp.broadcast_to(rpair[:, :, None], (occupied, block_virtuals, LANES))
    cpair = (scale * (col_vir[None, :] - eps_occ[:, None])).reshape(-1, LANES)
    chol_t = jnp.transpose(chol.reshape(shard_virtuals, occupied, width), (1, 0, 2))
    chol_cols = gather(chol_t, "row")
    factor = chol_t
    sums = []
    for step in range(ITERS):
        if shard_virtuals % 8:
            rows = gather(factor, "col")
            turn = jnp.zeros((1,), jnp.int32)
        else:
            rows = passed(factor, "col")
            turn = jnp.full((1,), n_col - col_index, jnp.int32)
        cols = chol_cols if step == 0 else gather(factor, "row")
        partial_value = update(turn, rows, cols, chol_cols, rpair, cpair)
        if shard_virtuals % 8:
            partial_value = jnp.transpose(
                partial_value.reshape(occupied, n_col, shard_virtuals, width), (1, 0, 2, 3)
            )
        work = lax.psum_scatter(partial_value, "col", scatter_dimension=0, tiled=False)
        factor = chol_t + work
        sums.append(jnp.sum(chol_t * work))
    energies = lax.psum(jnp.stack(sums), ("row", "col"))
    return jnp.transpose(work, (1, 0, 2)).reshape(shard, width), energies / scale


def solution(mesh):
    placed = (P(("row", "col"), None), P(), P())
    return jax.shard_map(
        shards,
        mesh=mesh,
        in_specs=placed,
        out_specs=(P(("row", "col"), None), P()),
        check_vma=False,
    )
```

```python
import functools

import jax
import jax.numpy as jnp
from jax import lax
from jax.experimental import pallas as pl
from jax.experimental.pallas import tpu as pltpu
from jax.sharding import PartitionSpec as P

ITERS = 2
LANES = 128
NT = (((1,), (1,)), ((), ()))


def split(x):
    high = x.astype(jnp.bfloat16)
    low = (x - high.astype(jnp.float32)).astype(jnp.bfloat16)
    return high, low


def flat(ref, index, turn=None):
    parts = range(ref.shape[0])
    pieces = [ref[part if turn is None else (part + turn) % len(parts), index] for part in parts]
    return pieces[0] if len(pieces) == 1 else jnp.concatenate(pieces, axis=0)


def kernel(steps, turn_ref, rows_ref, cols_ref, chol_ref, rpair_ref, cpair_ref, out_ref, rows, cols, chol, direct, high_tile, low_tile):
    step = pl.program_id(0)
    parts, occupied, shard_virtuals, width = rows_ref.shape
    height = parts * shard_virtuals
    block = occupied // steps
    breadth = cols_ref.shape[0] * cols_ref.shape[2]
    span = block * breadth
    group = LANES // breadth

    @pl.when(step == 0)
    def _():
        def one(index, carry):
            high, low = split(flat(rows_ref, index, turn_ref[0]))
            at = pl.ds(pl.multiple_of(index * height, height), height)
            rows[at, :width] = high
            rows[at, width:] = low
            return carry

        lax.fori_loop(0, occupied, one, 0)

    @pl.when(step < steps)
    def _():
        for index in range(block):
            high, low = split(flat(cols_ref, index))
            cols[index * breadth : (index + 1) * breadth, :width] = low
            cols[index * breadth : (index + 1) * breadth, width:] = high
            high, low = split(flat(chol_ref, index))
            at = pl.ds(pl.multiple_of(step * span + index * breadth, breadth), breadth)
            chol[at, :width] = high
            chol[at, width:] = low

        def one(index, carry):
            at = pl.ds(pl.multiple_of(index * block * height, block * height), block * height)
            value = lax.dot_general(rows[at, :], cols[...], NT, preferred_element_type=jnp.float32)
            value += lax.dot_general(rows[at, :width], cols[:, width:], NT, preferred_element_type=jnp.float32)
            direct[at, pl.ds(pl.multiple_of(step * span, span), span)] = value
            return carry

        lax.fori_loop(0, steps, one, 0)

    @pl.when(step >= steps)
    def _():
        first = (step - steps) * block
        lane = lax.broadcasted_iota(jnp.int32, (height, LANES), 1) // breadth

        def one(index, carry):
            lead = first + index * group
            columns = pl.ds(pl.multiple_of(lead * breadth, LANES), LANES)
            bottoms = [rpair_ref[lead + own] for own in range(group)]
            for other in range(occupied // group):
                swapped = [direct[pl.ds((other * group + m) * height, height), columns] for m in range(group)]
                to = slice(other * LANES, (other + 1) * LANES)
                tops = cpair_ref[other : other + 1, :]
                for own in range(group):
                    exchange = swapped[0] if own == 0 else pltpu.roll(swapped[0], (LANES - own * breadth) % LANES, 1)
                    for m in range(1, group):
                        shift = ((m - own) * breadth) % LANES
                        moved = pltpu.roll(swapped[m], shift, 1) if shift else swapped[m]
                        exchange = jnp.where(lane == m, moved, exchange)
                    at = pl.ds(pl.multiple_of((lead + own) * height, height), height)
                    value = (exchange - 2.0 * direct[at, to]) / (bottoms[own] + tops)
                    high, low = split(value)
                    put = pl.ds(pl.multiple_of((index * group + own) * height, height), height)
                    high_tile[put, to] = high
                    low_tile[put, to] = low
            return carry

        lax.fori_loop(0, block // group, one, 0)
        both = jnp.dot(high_tile[...], chol[...], preferred_element_type=jnp.float32)
        value = both[:, :width] + both[:, width:]
        value += jnp.dot(low_tile[...], chol[:, :width], preferred_element_type=jnp.float32)
        value = value.reshape(block, parts, shard_virtuals, width)
        for part in range(parts):
            out_ref[part] = value[:, part]


def update(turn, rows, cols, chol, rpair, cpair):
    parts, occupied, shard_virtuals, width = rows.shape
    height = parts * shard_virtuals
    breadth = cols.shape[0] * cols.shape[2]
    steps = 6
    block = occupied // steps
    pair_columns = occupied * breadth
    column_block = (cols.shape[0], block, cols.shape[2], width)

    def of_columns(step):
        return (0, jnp.minimum(step, steps - 1), 0, 0)

    return pl.pallas_call(
        functools.partial(kernel, steps),
        grid=(2 * steps,),
        out_shape=jax.ShapeDtypeStruct(rows.shape, jnp.float32),
        in_specs=[
            pl.BlockSpec(memory_space=pltpu.SMEM),
            pl.BlockSpec(rows.shape, lambda step: (0, 0, 0, 0)),
            pl.BlockSpec(column_block, of_columns),
            pl.BlockSpec(column_block, of_columns),
            pl.BlockSpec(rpair.shape, lambda step: (0, 0, 0)),
            pl.BlockSpec(cpair.shape, lambda step: (0, 0)),
        ],
        out_specs=pl.BlockSpec((parts, block, shard_virtuals, width), lambda step: (0, jnp.maximum(step - steps, 0), 0, 0)),
        scratch_shapes=[
            pltpu.VMEM((occupied * height, 2 * width), jnp.bfloat16),
            pltpu.VMEM((block * breadth, 2 * width), jnp.bfloat16),
            pltpu.VMEM((pair_columns, 2 * width), jnp.bfloat16),
            pltpu.VMEM((occupied * height, pair_columns), jnp.float32),
            pltpu.VMEM((block * height, pair_columns), jnp.bfloat16),
            pltpu.VMEM((block * height, pair_columns), jnp.bfloat16),
        ],
        compiler_params=pltpu.CompilerParams(
            dimension_semantics=("arbitrary",), vmem_limit_bytes=66 * 1000 * 1000
        ),
        cost_estimate=pl.CostEstimate(
            flops=12 * occupied * height * pair_columns * width, bytes_accessed=4 * width * (2 * occupied * height + 2 * pair_columns), transcendentals=0
        ),
    )(turn, rows, cols, chol, rpair, cpair)


def gather(x, axis):
    parts = lax.all_gather(x, axis, axis=0)
    if x.shape[1] % 8:
        parts = jnp.transpose(parts, (1, 0, 2, 3)).reshape(1, x.shape[0], -1, x.shape[2])
    return parts


def passed(x, axis):
    n = lax.axis_size(axis)
    blocks = [x]
    for k in range(1, n):
        blocks.append(lax.ppermute(x, axis, [(j, (j - k) % n) for j in range(n)]))
    return jnp.stack(blocks)


PIECES = 6
CORE, ACROSS, UP, DOWN = 0, 1, 2, 3
MESH = pl.DeviceIdType.MESH


def place():
    row = lax.axis_index("row")
    core = lax.rem(row, 2)
    side = lax.rem(lax.div(row, 2), 2)
    half = lax.div(row, 4)
    return row, half, side, core, lax.axis_index("col")


def nearest(col, n_col, order):
    near = jnp.minimum(col, n_col - 1 - col)
    far = order - near
    away = jnp.where(col < n_col - 1 - col, far, -far)
    turn = lax.div(order + 1, 2) * (2 * lax.rem(order, 2) - 1)
    return col + jnp.where(order <= 2 * near, turn, away)


def fused_kernel(
    n_col, chol_ref, occ_ref, vir_ref, out_ref, energy_ref, land, held, back, factor, rows, fresh, kept, direct, high_tile, low_tile, total, bottoms, tops,
    mine, around, along, local_sem, send_sem, recv_sem, held_send, held_recv, back_send, back_recv, ring_send, ring_recv, line_send, line_recv, credit,
):
    row, half, side, core, col = place()
    n_row = 8
    occupied, width = chol_ref.shape[0], chol_ref.shape[2]
    virtuals = chol_ref.shape[1]
    size = occupied * virtuals
    span = occupied * 2 * virtuals
    part = occupied // PIECES
    chunks = 2 * n_col
    group = LANES // (2 * virtuals)
    blocks = occupied // group
    tall = group * virtuals
    partner = (row + 1 - 2 * core, col)
    beside = (row + 2 - 4 * side, col)
    across = (row + 4 - 8 * half, col)
    above = (row, col + 1)
    below = (row, col - 1)
    own_chunk = 2 * col + half

    def slot(chunk, owner, piece):
        return land.at[chunk, pl.ds(piece * part, part), pl.ds(pl.multiple_of(owner * virtuals, virtuals), virtuals), :]

    def move(source, chunk, target, piece, device):
        return pltpu.make_async_remote_copy(
            src_ref=source,
            dst_ref=slot(chunk, core, piece),
            send_sem=send_sem.at[chunk, target, piece],
            recv_sem=recv_sem.at[chunk, core, piece],
            device_id=device,
            device_id_type=MESH,
        )

    def landed(chunk, owner, piece):
        pltpu.make_async_remote_copy(
            src_ref=slot(chunk, owner, piece),
            dst_ref=slot(chunk, owner, piece),
            send_sem=send_sem.at[chunk, CORE, piece],
            recv_sem=recv_sem.at[chunk, owner, piece],
            device_id=partner,
            device_id_type=MESH,
        ).wait_recv()

    def pieces_of(ref, piece):
        return ref.at[pl.ds(piece * part, part), :, :]

    def lend(source, piece):
        return pltpu.make_async_remote_copy(
            src_ref=pieces_of(source, piece), dst_ref=pieces_of(held, piece), send_sem=held_send.at[piece], recv_sem=held_recv.at[piece], device_id=beside, device_id_type=MESH
        )

    def give(piece):
        return pltpu.make_async_remote_copy(
            src_ref=pieces_of(total.at[0], piece), dst_ref=pieces_of(back, piece), send_sem=back_send.at[piece], recv_sem=back_recv.at[piece], device_id=beside, device_id_type=MESH
        )

    def stay(source, piece):
        return pltpu.make_async_copy(pieces_of(source, piece), slot(own_chunk, core, piece), local_sem.at[piece])

    def take(value, start):
        high, low = split(value.reshape(-1, width))
        at = slice(start, start + high.shape[0])
        rows[at, :width] = low
        rows[at, width:] = high

    def publish(source, piece):
        @pl.when(col < n_col - 1)
        def _():
            move(pieces_of(source, piece), own_chunk, UP, piece, above).start()

        @pl.when(col > 0)
        def _():
            move(pieces_of(source, piece), own_chunk, DOWN, piece, below).start()

        lend(source, piece).start()
        move(pieces_of(source, piece), own_chunk, ACROSS, piece, across).start()
        move(pieces_of(source, piece), own_chunk, CORE, piece, partner).start()
        stay(source, piece).start()
        take(source[piece * part : (piece + 1) * part], size + piece * part * virtuals)

    def relay(distance, first, last):
        def of(position, target, device, more):
            near = 2 * position + half
            away = near + 1 - 2 * half

            def one(piece, carry):
                landed(near, core, piece)

                @pl.when(more)
                def _():
                    move(slot(near, core, piece), near, target, piece, device).start()

                @pl.when(piece > 0)
                def _():
                    move(slot(near, core, piece), near, ACROSS, piece, across).start()

                @pl.when(piece == 0)
                def _():
                    landed(away, core, piece)

                    @pl.when(more)
                    def _():
                        move(slot(away, core, piece), away, target, piece, device).start()

                    move(slot(away, core, piece), away, CORE, piece, partner).start()

                move(slot(near, core, piece), near, CORE, piece, partner).start()
                return carry

            lax.fori_loop(first, last, one, 0)

        @pl.when(col + distance < n_col)
        def _():
            of(col + distance, DOWN, below, col > 0)

        @pl.when(col >= distance)
        def _():
            of(col - distance, UP, above, col < n_col - 1)

    def turn():
        chunk = own_chunk + 1 - 2 * half
        landed(chunk, core, 0)

        @pl.when(col < n_col - 1)
        def _():
            move(slot(chunk, core, 0), chunk, UP, 0, above).start()

        @pl.when(col > 0)
        def _():
            move(slot(chunk, core, 0), chunk, DOWN, 0, below).start()

        move(slot(chunk, core, 0), chunk, CORE, 0, partner).start()

    def cross(chunk):
        def one(piece, carry):
            landed(chunk, core, piece)
            move(slot(chunk, core, piece), chunk, CORE, piece, partner).start()
            return carry

        lax.fori_loop(1, PIECES, one, 0)

    def settle():
        def one(position, carry):
            def each(piece, carry):
                near = 2 * position + half
                away = near + 1 - 2 * half

                def sent(chunk, target, device):
                    move(slot(chunk, core, piece), chunk, target, piece, device).wait_send()

                sent(near, CORE, partner)
                sent(away, CORE, partner)

                @pl.when((piece > 0) | (position == col))
                def _():
                    sent(near, ACROSS, across)

                @pl.when((position >= col) & (col > 0))
                def _():
                    sent(near, DOWN, below)

                    @pl.when(piece == 0)
                    def _():
                        sent(away, DOWN, below)

                @pl.when((position <= col) & (col < n_col - 1))
                def _():
                    sent(near, UP, above)

                    @pl.when(piece == 0)
                    def _():
                        sent(away, UP, above)

                return carry

            return lax.fori_loop(0, PIECES, each, carry)

        lax.fori_loop(0, n_col, one, 0)
        for piece in range(PIECES):
            lend(factor, piece).wait_send()

    barrier = pltpu.get_barrier_semaphore()

    def greet_row(other, carry):
        pl.semaphore_signal(barrier, inc=1, device_id=(lax.rem(row + other, n_row), col), device_id_type=MESH)
        return carry

    def greet_col(other, carry):
        pl.semaphore_signal(barrier, inc=1, device_id=(row, lax.rem(col + other, n_col)), device_id_type=MESH)
        return carry

    lax.fori_loop(1, n_row, greet_row, 0)
    lax.fori_loop(1, n_col, greet_col, 0)
    pl.semaphore_wait(barrier, n_row + n_col - 2)

    for piece in range(PIECES):
        publish(chol_ref, piece)

    scale = jnp.float32(occupied * virtuals * n_row * n_col)
    vertical = lax.broadcasted_iota(jnp.int32, (virtuals, LANES), 0)
    lateral = lax.broadcasted_iota(jnp.int32, (1, LANES), 1)

    for which in range(2):
        first = ((row + (1 - which) * (2 - 4 * side)) * n_col + col) * virtuals
        level = jnp.zeros((virtuals, LANES), jnp.float32)
        for index in range(virtuals):
            level = jnp.where(vertical == index, vir_ref[first + index], level)

        def lower(index, carry):
            bottoms[which, index] = scale * (level - occ_ref[index])
            return carry

        lax.fori_loop(0, occupied, lower, 0)

    def raised(chunk, carry):
        position, other = lax.div(chunk, 2), lax.rem(chunk, 2)
        level = jnp.zeros((1, LANES), jnp.float32)
        for index in range(2 * virtuals):
            source = (4 * other + 2 * side + index // virtuals) * n_col + position
            level = jnp.where(lax.rem(lateral, 2 * virtuals) == index, vir_ref[source * virtuals + index % virtuals], level)
        for block in range(blocks):
            deep = jnp.zeros((1, LANES), jnp.float32)
            for index in range(group):
                deep = jnp.where(lax.div(lateral, 2 * virtuals) == index, occ_ref[block * group + index], deep)
            tops[chunk, block : block + 1, :] = scale * (level - deep)
        return carry

    lax.fori_loop(0, chunks, raised, 0)

    def convert(step, chunk, place):
        def one(index, carry):
            high, low = split(land[chunk, index])
            at = pl.ds(pl.multiple_of(index * 2 * virtuals, 2 * virtuals), 2 * virtuals)
            fresh[place, at, :width] = high
            fresh[place, at, width:] = low

            @pl.when(step == 0)
            def _():
                kept[chunk, at, :width] = high
                kept[chunk, at, width:] = low

            return carry

        lax.fori_loop(0, occupied, one, 0, unroll=8)

    lane = lax.broadcasted_iota(jnp.int32, (virtuals, LANES), 1) // (2 * virtuals)

    def product(which, place, part, start, count):
        at = pl.ds(pl.multiple_of(start, LANES), count)
        whose = pl.ds(pl.multiple_of(which * size, size), size)
        value = lax.dot_general(rows[whose, :], fresh[place, at, :], NT, preferred_element_type=jnp.float32)
        value += lax.dot_general(rows[whose, width:], fresh[place, at, :width], NT, preferred_element_type=jnp.float32)
        direct[part * size : (part + 1) * size, at] = value

    def amplitude(which, chunk, part, first, second):
        at = pl.ds(pl.multiple_of(part * size + first * tall, tall), tall)
        to = slice(second * LANES, (second + 1) * LANES)
        plain = direct[at, to]
        turned = direct[part * size + second * tall : part * size + (second + 1) * tall, pl.ds(pl.multiple_of(first * LANES, LANES), LANES)]
        skew = [turned[(-m) % group * virtuals : ((-m) % group + 1) * virtuals] for m in range(group)]
        skew = [pltpu.roll(value, (-m) % group * 2 * virtuals, 1) if m else value for m, value in enumerate(skew)]
        stride = 1
        while stride < group:
            upper = (lane & stride) != 0
            skew = [jnp.where(upper, skew[(m - stride) % group], skew[m]) for m in range(group)]
            stride *= 2
        top = tops[chunk, second : second + 1, :]
        values = []
        for m in range(group):
            exchange = pltpu.roll(skew[m], LANES - m * 2 * virtuals, 1) if m else skew[m]
            bottom = bottoms[which, first * group + m]
            values.append((exchange - 2.0 * plain[m * virtuals : (m + 1) * virtuals]) / (bottom + top))
        high, low = split(jnp.concatenate(values, axis=0))
        high_tile[at, to] = high
        low_tile[at, to] = low

    def collect(which, chunk, start, count):
        at = pl.ds(pl.multiple_of(start, tall), count)
        both = jnp.dot(high_tile[at, :], kept[chunk], preferred_element_type=jnp.float32)
        value = both[:, :width] + both[:, width:]
        value += jnp.dot(low_tile[at, :], kept[chunk, :, :width], preferred_element_type=jnp.float32)
        return value.reshape(count // virtuals, virtuals, width)

    def contract(one, two, last):
        (which, chunk, place), (other, second_chunk, second_place) = one, two
        product(which, place, 0, 0, span)
        cuts = span // (2 * LANES)

        def begin(index, carry):
            for block in range(blocks * blocks // cuts):
                amplitude(which, chunk, 0, index * (blocks // cuts) + block // blocks, block % blocks)
            product(other, second_place, 1, index * 2 * LANES, 2 * LANES)
            return carry

        lax.fori_loop(0, cuts, begin, 0)

        def finish(index, carry):
            for block in range(blocks * blocks // 2):
                amplitude(other, second_chunk, 1, index * (blocks // 2) + block // blocks, block % blocks)
            at = pl.ds(index * (occupied // 2), occupied // 2)
            total[which, at] += collect(which, chunk, index * (size // 2), size // 2)

            @pl.when(last)
            def _():
                for piece in range(PIECES // 2):
                    give(index * (PIECES // 2) + piece).start()

            return carry

        lax.fori_loop(0, 2, finish, 0)
        total[other] += collect(other, second_chunk, size, size)

    def iterate(step, carry):
        total[...] = jnp.zeros_like(total)
        turn()
        relay(1, 0, PIECES)
        for piece in range(PIECES):
            stay(factor, piece).wait()

        def chunk_of(order, odd):
            return 2 * nearest(col, n_col, order) + half + odd * (1 - 2 * half)

        def there(chunk):
            def one(piece, carry):
                landed(chunk, 1 - core, piece)
                return carry

            lax.fori_loop(0, PIECES, one, 0)

        def one(index, carry):
            order = lax.div(index, 2)
            odd = lax.rem(index, 2)
            early = jnp.where(index < 2, 1, 0)
            chunk = chunk_of(order * (1 - early), odd * (1 - early))

            @pl.when(index == 0)
            def _():
                there(own_chunk)
                convert(step, own_chunk, 0)
                beyond = own_chunk + 1 - 2 * half
                cross(beyond)
                there(beyond)
                convert(step, beyond, 1)

            @pl.when(index == 1)
            def _():
                for piece in range(PIECES):
                    lend(factor, piece).wait_recv()
                take(held[...], 0)

            @pl.when(index >= 2)
            def _():
                @pl.when((odd == 0) & (order < n_col - 1))
                def _():
                    relay(order + 1, 0, PIECES // 2)

                @pl.when((odd == 1) & (order < n_col - 1))
                def _():
                    relay(order + 1, PIECES // 2, PIECES)

                @pl.when(odd == 1)
                def _():
                    cross(chunk)

                there(chunk)
                convert(step, chunk, 0)

            which = jnp.where(index == 0, 1, 0)
            other = jnp.where(index == 1, 0, 1)
            second = chunk_of(order * (1 - early), early + odd * (1 - early))
            contract((which, chunk, 0), (other, second, early), index == chunks - 1)
            return carry

        lax.fori_loop(0, chunks, one, 0)
        settle()

        @pl.when(step == 0)
        def _():
            def thank(device):
                pl.semaphore_signal(credit, inc=1, device_id=device, device_id_type=MESH)

            thank(partner)
            thank(beside)
            thank(across)

            @pl.when(col < n_col - 1)
            def _():
                thank(above)

            @pl.when(col > 0)
            def _():
                thank(below)

            pl.semaphore_wait(credit, 3 + jnp.minimum(col, 1) + jnp.minimum(n_col - 1 - col, 1))

        energy = jnp.zeros((virtuals, width), jnp.float32)
        for piece in range(PIECES):
            give(piece).wait_recv()
            at = slice(piece * part, (piece + 1) * part)
            value = total[1, at] + back[at]
            energy += jnp.sum(chol_ref[at] * value, axis=0)

            @pl.when(step == 0)
            def _():
                factor[at] = chol_ref[at] + value
                publish(factor, piece)

            @pl.when(step == ITERS - 1)
            def _():
                out_ref[at] = value

        folded = energy[:, :LANES]
        for index in range(1, width // LANES):
            folded += energy[:, index * LANES : (index + 1) * LANES]
        mine[step] = folded
        for piece in range(PIECES):
            give(piece).wait_send()
        return carry

    lax.fori_loop(0, ITERS, iterate, 0)

    def to_ring(other):
        return pltpu.make_async_remote_copy(
            src_ref=mine, dst_ref=around.at[row], send_sem=ring_send.at[other], recv_sem=ring_recv.at[row], device_id=(lax.rem(row + other, n_row), col), device_id_type=MESH
        )

    def from_ring(other):
        source = lax.rem(row + other, n_row)
        return pltpu.make_async_remote_copy(
            src_ref=mine, dst_ref=around.at[source], send_sem=ring_send.at[other], recv_sem=ring_recv.at[source], device_id=(source, col), device_id_type=MESH
        )

    for other in range(1, n_row):
        to_ring(other).start()
    around[row] = mine[...]
    for other in range(1, n_row):
        from_ring(other).wait_recv()
    for other in range(1, n_row):
        to_ring(other).wait_send()
    mine[...] = sum(around[index] for index in range(n_row))

    def to_line(other):
        return pltpu.make_async_remote_copy(
            src_ref=mine, dst_ref=along.at[col], send_sem=line_send.at[other], recv_sem=line_recv.at[col], device_id=(row, lax.rem(col + other, n_col)), device_id_type=MESH
        )

    def from_line(other):
        source = lax.rem(col + other, n_col)
        return pltpu.make_async_remote_copy(
            src_ref=mine, dst_ref=along.at[source], send_sem=line_send.at[other], recv_sem=line_recv.at[source], device_id=(row, source), device_id_type=MESH
        )

    for other in range(1, n_col):
        to_line(other).start()
    along[col] = mine[...]
    for other in range(1, n_col):
        from_line(other).wait_recv()
    for other in range(1, n_col):
        to_line(other).wait_send()
    energy_ref[...] = sum(along[index] for index in range(n_col))


def fused(chol, eps_occ, eps_vir):
    n_col = lax.axis_size("col")
    n_row = lax.axis_size("row")
    shard, width = chol.shape
    occupied = eps_occ.shape[0]
    virtuals = shard // occupied
    scale = jnp.float32(eps_vir.shape[0] * occupied)
    size, span = shard, 2 * shard
    chol_t = jnp.transpose(chol.reshape(virtuals, occupied, width), (1, 0, 2))
    shape = (occupied, virtuals, width)
    dma = pltpu.SemaphoreType.DMA
    work, energies = pl.pallas_call(
        functools.partial(fused_kernel, n_col),
        out_shape=(jax.ShapeDtypeStruct(shape, jnp.float32), jax.ShapeDtypeStruct((ITERS, virtuals, LANES), jnp.float32)),
        in_specs=[pl.BlockSpec(memory_space=pltpu.VMEM), pl.BlockSpec(memory_space=pltpu.SMEM), pl.BlockSpec(memory_space=pltpu.SMEM)],
        out_specs=(pl.BlockSpec(memory_space=pltpu.VMEM), pl.BlockSpec(memory_space=pltpu.VMEM)),
        scratch_shapes=[
            pltpu.VMEM((2 * n_col, occupied, 2 * virtuals, width), jnp.float32),
            pltpu.VMEM(shape, jnp.float32),
            pltpu.VMEM(shape, jnp.float32),
            pltpu.VMEM(shape, jnp.float32),
            pltpu.VMEM((2 * size, 2 * width), jnp.bfloat16),
            pltpu.VMEM((2, span, 2 * width), jnp.bfloat16),
            pltpu.VMEM((2 * n_col, span, 2 * width), jnp.bfloat16),
            pltpu.VMEM((2 * size, span), jnp.float32),
            pltpu.VMEM((2 * size, span), jnp.bfloat16),
            pltpu.VMEM((2 * size, span), jnp.bfloat16),
            pltpu.VMEM((2,) + shape, jnp.float32),
            pltpu.VMEM((2, occupied, virtuals, LANES), jnp.float32),
            pltpu.VMEM((2 * n_col, 2 * occupied * virtuals // LANES, LANES), jnp.float32),
            pltpu.VMEM((ITERS, virtuals, LANES), jnp.float32),
            pltpu.VMEM((n_row, ITERS, virtuals, LANES), jnp.float32),
            pltpu.VMEM((n_col, ITERS, virtuals, LANES), jnp.float32),
            dma((PIECES,)),
            dma((2 * n_col, 4, PIECES)),
            dma((2 * n_col, 2, PIECES)),
            dma((PIECES,)),
            dma((PIECES,)),
            dma((PIECES,)),
            dma((PIECES,)),
            dma((n_row,)),
            dma((n_row,)),
            dma((n_col,)),
            dma((n_col,)),
            pltpu.SemaphoreType.REGULAR,
        ],
        compiler_params=pltpu.CompilerParams(collective_id=0, has_side_effects=True, vmem_limit_bytes=66 * 1000 * 1000),
    )(chol_t, eps_occ, eps_vir)
    return jnp.transpose(work, (1, 0, 2)).reshape(shard, width), jnp.sum(energies, axis=(1, 2)) / scale


def shards(chol, eps_occ, eps_vir):
    if lax.axis_size("row") == 8 and chol.shape[0] == 8 * eps_occ.shape[0] and eps_occ.shape[0] % 48 == 0:
        return fused(chol, eps_occ, eps_vir)
    n_row = lax.axis_size("row")
    n_col = lax.axis_size("col")
    row_index = lax.axis_index("row")
    col_index = lax.axis_index("col")
    shard, width = chol.shape
    occupied = eps_occ.shape[0]
    virtual = eps_vir.shape[0]
    shard_virtuals = shard // occupied
    block_virtuals = n_col * shard_virtuals
    total = virtual * occupied
    scale = jnp.float32(total)
    row_vir = lax.dynamic_slice_in_dim(eps_vir, row_index * block_virtuals, block_virtuals, 0)
    col_vir = lax.dynamic_slice_in_dim(
        eps_vir.reshape(n_row, block_virtuals), col_index * shard_virtuals, shard_virtuals, 1
    ).reshape(n_row * shard_virtuals)
    rpair = scale * (row_vir[None, :] - eps_occ[:, None])
    rpair = jnp.broadcast_to(rpair[:, :, None], (occupied, block_virtuals, LANES))
    cpair = (scale * (col_vir[None, :] - eps_occ[:, None])).reshape(-1, LANES)
    chol_t = jnp.transpose(chol.reshape(shard_virtuals, occupied, width), (1, 0, 2))
    chol_cols = gather(chol_t, "row")
    factor = chol_t
    sums = []
    for step in range(ITERS):
        if shard_virtuals % 8:
            rows = gather(factor, "col")
            turn = jnp.zeros((1,), jnp.int32)
        else:
            rows = passed(factor, "col")
            turn = jnp.full((1,), n_col - col_index, jnp.int32)
        cols = chol_cols if step == 0 else gather(factor, "row")
        partial_value = update(turn, rows, cols, chol_cols, rpair, cpair)
        if shard_virtuals % 8:
            partial_value = jnp.transpose(
                partial_value.reshape(occupied, n_col, shard_virtuals, width), (1, 0, 2, 3)
            )
        work = lax.psum_scatter(partial_value, "col", scatter_dimension=0, tiled=False)
        factor = chol_t + work
        sums.append(jnp.sum(chol_t * work))
    energies = lax.psum(jnp.stack(sums), ("row", "col"))
    return jnp.transpose(work, (1, 0, 2)).reshape(shard, width), energies / scale


def solution(mesh):
    placed = (P(("row", "col"), None), P(), P())
    return jax.shard_map(
        shards,
        mesh=mesh,
        in_specs=placed,
        out_specs=(P(("row", "col"), None), P()),
        check_vma=False,
    )
```

```python
import functools

import jax
import jax.numpy as jnp
from jax import lax
from jax.experimental import pallas as pl
from jax.experimental.pallas import tpu as pltpu
from jax.sharding import PartitionSpec as P

ITERS = 2
LANES = 128
NT = (((1,), (1,)), ((), ()))


def split(x):
    high = x.astype(jnp.bfloat16)
    low = (x - high.astype(jnp.float32)).astype(jnp.bfloat16)
    return high, low


def flat(ref, index, turn=None):
    parts = range(ref.shape[0])
    pieces = [ref[part if turn is None else (part + turn) % len(parts), index] for part in parts]
    return pieces[0] if len(pieces) == 1 else jnp.concatenate(pieces, axis=0)


def kernel(steps, turn_ref, rows_ref, cols_ref, chol_ref, rpair_ref, cpair_ref, out_ref, rows, cols, chol, direct, high_tile, low_tile):
    step = pl.program_id(0)
    parts, occupied, shard_virtuals, width = rows_ref.shape
    height = parts * shard_virtuals
    block = occupied // steps
    breadth = cols_ref.shape[0] * cols_ref.shape[2]
    span = block * breadth
    group = LANES // breadth

    @pl.when(step == 0)
    def _():
        def one(index, carry):
            high, low = split(flat(rows_ref, index, turn_ref[0]))
            at = pl.ds(pl.multiple_of(index * height, height), height)
            rows[at, :width] = high
            rows[at, width:] = low
            return carry

        lax.fori_loop(0, occupied, one, 0)

    @pl.when(step < steps)
    def _():
        for index in range(block):
            high, low = split(flat(cols_ref, index))
            cols[index * breadth : (index + 1) * breadth, :width] = low
            cols[index * breadth : (index + 1) * breadth, width:] = high
            high, low = split(flat(chol_ref, index))
            at = pl.ds(pl.multiple_of(step * span + index * breadth, breadth), breadth)
            chol[at, :width] = high
            chol[at, width:] = low

        def one(index, carry):
            at = pl.ds(pl.multiple_of(index * block * height, block * height), block * height)
            value = lax.dot_general(rows[at, :], cols[...], NT, preferred_element_type=jnp.float32)
            value += lax.dot_general(rows[at, :width], cols[:, width:], NT, preferred_element_type=jnp.float32)
            direct[at, pl.ds(pl.multiple_of(step * span, span), span)] = value
            return carry

        lax.fori_loop(0, steps, one, 0)

    @pl.when(step >= steps)
    def _():
        first = (step - steps) * block
        lane = lax.broadcasted_iota(jnp.int32, (height, LANES), 1) // breadth

        def one(index, carry):
            lead = first + index * group
            columns = pl.ds(pl.multiple_of(lead * breadth, LANES), LANES)
            bottoms = [rpair_ref[lead + own] for own in range(group)]
            for other in range(occupied // group):
                swapped = [direct[pl.ds((other * group + m) * height, height), columns] for m in range(group)]
                to = slice(other * LANES, (other + 1) * LANES)
                tops = cpair_ref[other : other + 1, :]
                for own in range(group):
                    exchange = swapped[0] if own == 0 else pltpu.roll(swapped[0], (LANES - own * breadth) % LANES, 1)
                    for m in range(1, group):
                        shift = ((m - own) * breadth) % LANES
                        moved = pltpu.roll(swapped[m], shift, 1) if shift else swapped[m]
                        exchange = jnp.where(lane == m, moved, exchange)
                    at = pl.ds(pl.multiple_of((lead + own) * height, height), height)
                    value = (exchange - 2.0 * direct[at, to]) / (bottoms[own] + tops)
                    high, low = split(value)
                    put = pl.ds(pl.multiple_of((index * group + own) * height, height), height)
                    high_tile[put, to] = high
                    low_tile[put, to] = low
            return carry

        lax.fori_loop(0, block // group, one, 0)
        both = jnp.dot(high_tile[...], chol[...], preferred_element_type=jnp.float32)
        value = both[:, :width] + both[:, width:]
        value += jnp.dot(low_tile[...], chol[:, :width], preferred_element_type=jnp.float32)
        value = value.reshape(block, parts, shard_virtuals, width)
        for part in range(parts):
            out_ref[part] = value[:, part]


def update(turn, rows, cols, chol, rpair, cpair):
    parts, occupied, shard_virtuals, width = rows.shape
    height = parts * shard_virtuals
    breadth = cols.shape[0] * cols.shape[2]
    steps = 6
    block = occupied // steps
    pair_columns = occupied * breadth
    column_block = (cols.shape[0], block, cols.shape[2], width)

    def of_columns(step):
        return (0, jnp.minimum(step, steps - 1), 0, 0)

    return pl.pallas_call(
        functools.partial(kernel, steps),
        grid=(2 * steps,),
        out_shape=jax.ShapeDtypeStruct(rows.shape, jnp.float32),
        in_specs=[
            pl.BlockSpec(memory_space=pltpu.SMEM),
            pl.BlockSpec(rows.shape, lambda step: (0, 0, 0, 0)),
            pl.BlockSpec(column_block, of_columns),
            pl.BlockSpec(column_block, of_columns),
            pl.BlockSpec(rpair.shape, lambda step: (0, 0, 0)),
            pl.BlockSpec(cpair.shape, lambda step: (0, 0)),
        ],
        out_specs=pl.BlockSpec((parts, block, shard_virtuals, width), lambda step: (0, jnp.maximum(step - steps, 0), 0, 0)),
        scratch_shapes=[
            pltpu.VMEM((occupied * height, 2 * width), jnp.bfloat16),
            pltpu.VMEM((block * breadth, 2 * width), jnp.bfloat16),
            pltpu.VMEM((pair_columns, 2 * width), jnp.bfloat16),
            pltpu.VMEM((occupied * height, pair_columns), jnp.float32),
            pltpu.VMEM((block * height, pair_columns), jnp.bfloat16),
            pltpu.VMEM((block * height, pair_columns), jnp.bfloat16),
        ],
        compiler_params=pltpu.CompilerParams(
            dimension_semantics=("arbitrary",), vmem_limit_bytes=66 * 1000 * 1000
        ),
        cost_estimate=pl.CostEstimate(
            flops=12 * occupied * height * pair_columns * width, bytes_accessed=4 * width * (2 * occupied * height + 2 * pair_columns), transcendentals=0
        ),
    )(turn, rows, cols, chol, rpair, cpair)


def gather(x, axis):
    parts = lax.all_gather(x, axis, axis=0)
    if x.shape[1] % 8:
        parts = jnp.transpose(parts, (1, 0, 2, 3)).reshape(1, x.shape[0], -1, x.shape[2])
    return parts


def passed(x, axis):
    n = lax.axis_size(axis)
    blocks = [x]
    for k in range(1, n):
        blocks.append(lax.ppermute(x, axis, [(j, (j - k) % n) for j in range(n)]))
    return jnp.stack(blocks)


PIECES = 6
CORE, ACROSS, UP, DOWN = 0, 1, 2, 3
MESH = pl.DeviceIdType.MESH


def place():
    row = lax.axis_index("row")
    core = lax.rem(row, 2)
    side = lax.rem(lax.div(row, 2), 2)
    half = lax.div(row, 4)
    return row, half, side, core, lax.axis_index("col")


def nearest(col, n_col, order):
    near = jnp.minimum(col, n_col - 1 - col)
    far = order - near
    away = jnp.where(col < n_col - 1 - col, far, -far)
    turn = lax.div(order + 1, 2) * (2 * lax.rem(order, 2) - 1)
    return col + jnp.where(order <= 2 * near, turn, away)


def fused_kernel(
    n_col, chol_ref, occ_ref, vir_ref, out_ref, energy_ref, land, held, back, factor, rows, fresh, kept, direct, high_tile, low_tile, total, bottoms, tops,
    mine, around, along, local_sem, send_sem, recv_sem, held_send, held_recv, back_send, back_recv, ring_send, ring_recv, line_send, line_recv, credit,
):
    row, half, side, core, col = place()
    n_row = 8
    occupied, width = chol_ref.shape[0], chol_ref.shape[2]
    virtuals = chol_ref.shape[1]
    size = occupied * virtuals
    span = occupied * 2 * virtuals
    part = occupied // PIECES
    chunks = 2 * n_col
    group = LANES // (2 * virtuals)
    blocks = occupied // group
    tall = group * virtuals
    partner = (row + 1 - 2 * core, col)
    beside = (row + 2 - 4 * side, col)
    across = (row + 4 - 8 * half, col)
    above = (row, col + 1)
    below = (row, col - 1)
    own_chunk = 2 * col + half

    def slot(chunk, owner, piece):
        return land.at[chunk, pl.ds(piece * part, part), pl.ds(pl.multiple_of(owner * virtuals, virtuals), virtuals), :]

    def move(source, chunk, target, piece, device):
        return pltpu.make_async_remote_copy(
            src_ref=source,
            dst_ref=slot(chunk, core, piece),
            send_sem=send_sem.at[chunk, target, piece],
            recv_sem=recv_sem.at[chunk, core, piece],
            device_id=device,
            device_id_type=MESH,
        )

    def landed(chunk, owner, piece):
        pltpu.make_async_remote_copy(
            src_ref=slot(chunk, owner, piece),
            dst_ref=slot(chunk, owner, piece),
            send_sem=send_sem.at[chunk, CORE, piece],
            recv_sem=recv_sem.at[chunk, owner, piece],
            device_id=partner,
            device_id_type=MESH,
        ).wait_recv()

    def pieces_of(ref, piece):
        return ref.at[pl.ds(piece * part, part), :, :]

    def lend(source, step, piece):
        return pltpu.make_async_remote_copy(
            src_ref=pieces_of(source, piece), dst_ref=pieces_of(held.at[step], piece), send_sem=held_send.at[piece], recv_sem=held_recv.at[piece], device_id=beside, device_id_type=MESH
        )

    def give(piece):
        return pltpu.make_async_remote_copy(
            src_ref=pieces_of(total.at[0], piece), dst_ref=pieces_of(back, piece), send_sem=back_send.at[piece], recv_sem=back_recv.at[piece], device_id=beside, device_id_type=MESH
        )

    def stay(source, piece):
        return pltpu.make_async_copy(pieces_of(source, piece), slot(own_chunk, core, piece), local_sem.at[piece])

    def take(value, start):
        high, low = split(value.reshape(-1, width))
        at = slice(start, start + high.shape[0])
        rows[at, :width] = low
        rows[at, width:] = high

    def publish(source, step, piece):
        @pl.when(col < n_col - 1)
        def _():
            move(pieces_of(source, piece), own_chunk, UP, piece, above).start()

        @pl.when(col > 0)
        def _():
            move(pieces_of(source, piece), own_chunk, DOWN, piece, below).start()

        lend(source, step, piece).start()
        move(pieces_of(source, piece), own_chunk, ACROSS, piece, across).start()
        move(pieces_of(source, piece), own_chunk, CORE, piece, partner).start()
        stay(source, piece).start()

    def relay(distance, first, last):
        def of(position, target, device, more):
            near = 2 * position + half
            away = near + 1 - 2 * half

            def one(piece, carry):
                landed(near, core, piece)

                @pl.when(more)
                def _():
                    move(slot(near, core, piece), near, target, piece, device).start()

                @pl.when(piece > 0)
                def _():
                    move(slot(near, core, piece), near, ACROSS, piece, across).start()

                @pl.when(piece == 0)
                def _():
                    landed(away, core, piece)

                    @pl.when(more)
                    def _():
                        move(slot(away, core, piece), away, target, piece, device).start()

                    move(slot(away, core, piece), away, CORE, piece, partner).start()

                move(slot(near, core, piece), near, CORE, piece, partner).start()
                return carry

            lax.fori_loop(first, last, one, 0)

        @pl.when(col + distance < n_col)
        def _():
            of(col + distance, DOWN, below, col > 0)

        @pl.when(col >= distance)
        def _():
            of(col - distance, UP, above, col < n_col - 1)

    def turn():
        chunk = own_chunk + 1 - 2 * half
        landed(chunk, core, 0)

        @pl.when(col < n_col - 1)
        def _():
            move(slot(chunk, core, 0), chunk, UP, 0, above).start()

        @pl.when(col > 0)
        def _():
            move(slot(chunk, core, 0), chunk, DOWN, 0, below).start()

        move(slot(chunk, core, 0), chunk, CORE, 0, partner).start()

    def cross(chunk):
        def one(piece, carry):
            landed(chunk, core, piece)
            move(slot(chunk, core, piece), chunk, CORE, piece, partner).start()
            return carry

        lax.fori_loop(1, PIECES, one, 0)

    def settle():
        def one(position, carry):
            def each(piece, carry):
                near = 2 * position + half
                away = near + 1 - 2 * half

                def sent(chunk, target, device):
                    move(slot(chunk, core, piece), chunk, target, piece, device).wait_send()

                sent(near, CORE, partner)
                sent(away, CORE, partner)

                @pl.when((piece > 0) | (position == col))
                def _():
                    sent(near, ACROSS, across)

                @pl.when((position >= col) & (col > 0))
                def _():
                    sent(near, DOWN, below)

                    @pl.when(piece == 0)
                    def _():
                        sent(away, DOWN, below)

                @pl.when((position <= col) & (col < n_col - 1))
                def _():
                    sent(near, UP, above)

                    @pl.when(piece == 0)
                    def _():
                        sent(away, UP, above)

                return carry

            return lax.fori_loop(0, PIECES, each, carry)

        lax.fori_loop(0, n_col, one, 0)
        for piece in range(PIECES):
            lend(factor, 0, piece).wait_send()

    barrier = pltpu.get_barrier_semaphore()

    def greet_row(other, carry):
        pl.semaphore_signal(barrier, inc=1, device_id=(lax.rem(row + other, n_row), col), device_id_type=MESH)
        return carry

    def greet_col(other, carry):
        pl.semaphore_signal(barrier, inc=1, device_id=(row, lax.rem(col + other, n_col)), device_id_type=MESH)
        return carry

    lax.fori_loop(1, n_row, greet_row, 0)
    lax.fori_loop(1, n_col, greet_col, 0)
    pl.semaphore_wait(barrier, n_row + n_col - 2)

    for piece in range(PIECES):
        publish(chol_ref, 0, piece)
    take(chol_ref[...], size)

    scale = jnp.float32(occupied * virtuals * n_row * n_col)
    vertical = lax.broadcasted_iota(jnp.int32, (virtuals, LANES), 0)
    lateral = lax.broadcasted_iota(jnp.int32, (1, LANES), 1)

    for which in range(2):
        first = ((row + (1 - which) * (2 - 4 * side)) * n_col + col) * virtuals
        level = jnp.zeros((virtuals, LANES), jnp.float32)
        for index in range(virtuals):
            level = jnp.where(vertical == index, vir_ref[first + index], level)

        def lower(index, carry):
            bottoms[which, index] = scale * (level - occ_ref[index])
            return carry

        lax.fori_loop(0, occupied, lower, 0)

    def raised(chunk, carry):
        position, other = lax.div(chunk, 2), lax.rem(chunk, 2)
        level = jnp.zeros((1, LANES), jnp.float32)
        for index in range(2 * virtuals):
            source = (4 * other + 2 * side + index // virtuals) * n_col + position
            level = jnp.where(lax.rem(lateral, 2 * virtuals) == index, vir_ref[source * virtuals + index % virtuals], level)
        for block in range(blocks):
            deep = jnp.zeros((1, LANES), jnp.float32)
            for index in range(group):
                deep = jnp.where(lax.div(lateral, 2 * virtuals) == index, occ_ref[block * group + index], deep)
            tops[chunk, block : block + 1, :] = scale * (level - deep)
        return carry

    lax.fori_loop(0, chunks, raised, 0)

    def convert(step, chunk, place):
        def one(index, carry):
            high, low = split(land[chunk, index])
            at = pl.ds(pl.multiple_of(index * 2 * virtuals, 2 * virtuals), 2 * virtuals)
            fresh[place, at, :width] = high
            fresh[place, at, width:] = low

            @pl.when(step == 0)
            def _():
                kept[chunk, at, :width] = high
                kept[chunk, at, width:] = low

            return carry

        lax.fori_loop(0, occupied, one, 0, unroll=8)

    lane = lax.broadcasted_iota(jnp.int32, (virtuals, LANES), 1) // (2 * virtuals)

    def product(which, place, part, start, count):
        at = pl.ds(pl.multiple_of(start, LANES), count)
        whose = pl.ds(pl.multiple_of(which * size, size), size)
        value = lax.dot_general(rows[whose, :], fresh[place, at, :], NT, preferred_element_type=jnp.float32)
        value += lax.dot_general(rows[whose, width:], fresh[place, at, :width], NT, preferred_element_type=jnp.float32)
        direct[part * size : (part + 1) * size, at] = value

    def amplitude(which, chunk, part, first, second):
        at = pl.ds(pl.multiple_of(part * size + first * tall, tall), tall)
        to = slice(second * LANES, (second + 1) * LANES)
        plain = direct[at, to]
        turned = direct[part * size + second * tall : part * size + (second + 1) * tall, pl.ds(pl.multiple_of(first * LANES, LANES), LANES)]
        skew = [turned[(-m) % group * virtuals : ((-m) % group + 1) * virtuals] for m in range(group)]
        skew = [pltpu.roll(value, (-m) % group * 2 * virtuals, 1) if m else value for m, value in enumerate(skew)]
        stride = 1
        while stride < group:
            upper = (lane & stride) != 0
            skew = [jnp.where(upper, skew[(m - stride) % group], skew[m]) for m in range(group)]
            stride *= 2
        top = tops[chunk, second : second + 1, :]
        values = []
        for m in range(group):
            exchange = pltpu.roll(skew[m], LANES - m * 2 * virtuals, 1) if m else skew[m]
            bottom = bottoms[which, first * group + m]
            values.append((exchange - 2.0 * plain[m * virtuals : (m + 1) * virtuals]) / (bottom + top))
        high, low = split(jnp.concatenate(values, axis=0))
        high_tile[at, to] = high
        low_tile[at, to] = low

    def collect(which, chunk, start, count):
        at = pl.ds(pl.multiple_of(start, tall), count)
        both = jnp.dot(high_tile[at, :], kept[chunk], preferred_element_type=jnp.float32)
        value = both[:, :width] + both[:, width:]
        value += jnp.dot(low_tile[at, :], kept[chunk, :, :width], preferred_element_type=jnp.float32)
        return value.reshape(count // virtuals, virtuals, width)

    def contract(one, two, last, between):
        (which, chunk, place), (other, second_chunk, second_place) = one, two
        product(which, place, 0, 0, span)
        cuts = span // (2 * LANES)

        def begin(index, carry):
            for block in range(blocks * blocks // cuts):
                amplitude(which, chunk, 0, index * (blocks // cuts) + block // blocks, block % blocks)
            product(other, second_place, 1, index * 2 * LANES, 2 * LANES)
            return carry

        lax.fori_loop(0, cuts, begin, 0)
        between()

        def finish(index, carry):
            for block in range(blocks * blocks // 2):
                amplitude(other, second_chunk, 1, index * (blocks // 2) + block // blocks, block % blocks)
            at = pl.ds(index * (occupied // 2), occupied // 2)
            total[which, at] += collect(which, chunk, index * (size // 2), size // 2)

            @pl.when(last)
            def _():
                for piece in range(PIECES // 2):
                    give(index * (PIECES // 2) + piece).start()

            return carry

        lax.fori_loop(0, 2, finish, 0)
        total[other] += collect(other, second_chunk, size, size)

    def to_ring(other):
        return pltpu.make_async_remote_copy(
            src_ref=mine, dst_ref=around.at[row], send_sem=ring_send.at[other], recv_sem=ring_recv.at[row], device_id=(lax.rem(row + other, n_row), col), device_id_type=MESH
        )

    def from_ring(other):
        source = lax.rem(row + other, n_row)
        return pltpu.make_async_remote_copy(
            src_ref=mine, dst_ref=around.at[source], send_sem=ring_send.at[other], recv_sem=ring_recv.at[source], device_id=(source, col), device_id_type=MESH
        )

    def to_line(other):
        return pltpu.make_async_remote_copy(
            src_ref=along.at[col], dst_ref=along.at[col], send_sem=line_send.at[other], recv_sem=line_recv.at[col], device_id=(row, lax.rem(col + other, n_col)), device_id_type=MESH
        )

    def from_line(other):
        source = lax.rem(col + other, n_col)
        return pltpu.make_async_remote_copy(
            src_ref=along.at[source], dst_ref=along.at[source], send_sem=line_send.at[other], recv_sem=line_recv.at[source], device_id=(row, source), device_id_type=MESH
        )

    def iterate(step, carry):
        total[...] = jnp.zeros_like(total)
        turn()
        relay(1, 0, PIECES)
        for piece in range(PIECES):
            stay(factor, piece).wait()

        def chunk_of(order, odd):
            return 2 * nearest(col, n_col, order) + half + odd * (1 - 2 * half)

        def there(chunk):
            def one(piece, carry):
                landed(chunk, 1 - core, piece)
                return carry

            lax.fori_loop(0, PIECES, one, 0)

        def one(index, carry):
            order = lax.div(index, 2)
            odd = lax.rem(index, 2)
            early = jnp.where(index < 2, 1, 0)
            chunk = chunk_of(order * (1 - early), odd * (1 - early))

            def pass_on(turn):
                event = 2 * index - 1 + turn

                @pl.when((event >= 0) & (event < (n_col - 2) * PIECES))
                def _():
                    piece = lax.rem(event, PIECES)
                    relay(2 + lax.div(event, PIECES), piece, piece + 1)

            pass_on(0)

            @pl.when(index == 0)
            def _():
                there(own_chunk)
                convert(step, own_chunk, 0)
                beyond = own_chunk + 1 - 2 * half
                cross(beyond)
                there(beyond)
                convert(step, beyond, 1)

            @pl.when(index == 1)
            def _():
                for piece in range(PIECES):
                    lend(factor, step, piece).wait_recv()
                take(held[step], 0)

            @pl.when(index >= 2)
            def _():
                @pl.when(odd == 1)
                def _():
                    cross(chunk)

                there(chunk)
                convert(step, chunk, 0)

            which = jnp.where(index == 0, 1, 0)
            other = jnp.where(index == 1, 0, 1)
            second = chunk_of(order * (1 - early), early + odd * (1 - early))
            contract((which, chunk, 0), (other, second, early), index == chunks - 1, lambda: pass_on(1))
            return carry

        lax.fori_loop(0, chunks, one, 0)
        settle()

        @pl.when(step == 0)
        def _():
            def thank(device):
                pl.semaphore_signal(credit, inc=1, device_id=device, device_id_type=MESH)

            thank(partner)
            thank(beside)
            thank(across)

            @pl.when(col < n_col - 1)
            def _():
                thank(above)

            @pl.when(col > 0)
            def _():
                thank(below)

            pl.semaphore_wait(credit, 3 + jnp.minimum(col, 1) + jnp.minimum(n_col - 1 - col, 1))

        def weigh(index, energy):
            return energy + chol_ref[index] * total[1, index] + held[0, index] * total[0, index]

        energy = lax.fori_loop(0, occupied, weigh, jnp.zeros((virtuals, width), jnp.float32), unroll=4)
        folded = energy[:, :LANES]
        for index in range(1, width // LANES):
            folded += energy[:, index * LANES : (index + 1) * LANES]
        mine[step] = folded

        @pl.when(step == ITERS - 1)
        def _():
            around[row] = mine[...]
            for other in range(1, n_row):
                to_ring(other).start()

        for piece in range(PIECES):
            if piece == PIECES // 2:

                @pl.when(step == ITERS - 1)
                def _():
                    for other in range(1, n_row):
                        from_ring(other).wait_recv()
                    along[col] = sum(around[index] for index in range(n_row))
                    for other in range(1, n_col):
                        to_line(other).start()

            give(piece).wait_recv()
            at = slice(piece * part, (piece + 1) * part)
            value = total[1, at] + back[at]

            @pl.when(step == 0)
            def _():
                fresh_rows = chol_ref[at] + value
                factor[at] = fresh_rows
                publish(factor, 1, piece)
                take(fresh_rows, size + piece * part * virtuals)

            @pl.when(step == ITERS - 1)
            def _():
                out_ref[:, at, :] = jnp.transpose(value, (1, 0, 2))

        for piece in range(PIECES):
            give(piece).wait_send()
        return carry

    lax.fori_loop(0, ITERS, iterate, 0)
    for other in range(1, n_col):
        from_line(other).wait_recv()
    energy_ref[...] = sum(along[index] for index in range(n_col))
    for other in range(1, n_row):
        to_ring(other).wait_send()
    for other in range(1, n_col):
        to_line(other).wait_send()


def fused(chol, eps_occ, eps_vir):
    n_col = lax.axis_size("col")
    n_row = lax.axis_size("row")
    shard, width = chol.shape
    occupied = eps_occ.shape[0]
    virtuals = shard // occupied
    scale = jnp.float32(eps_vir.shape[0] * occupied)
    size, span = shard, 2 * shard
    chol_t = jnp.transpose(chol.reshape(virtuals, occupied, width), (1, 0, 2))
    shape = (occupied, virtuals, width)
    dma = pltpu.SemaphoreType.DMA
    work, energies = pl.pallas_call(
        functools.partial(fused_kernel, n_col),
        out_shape=(jax.ShapeDtypeStruct((virtuals, occupied, width), jnp.float32), jax.ShapeDtypeStruct((ITERS, virtuals, LANES), jnp.float32)),
        in_specs=[pl.BlockSpec(memory_space=pltpu.VMEM), pl.BlockSpec(memory_space=pltpu.SMEM), pl.BlockSpec(memory_space=pltpu.SMEM)],
        out_specs=(pl.BlockSpec(memory_space=pltpu.VMEM), pl.BlockSpec(memory_space=pltpu.VMEM)),
        scratch_shapes=[
            pltpu.VMEM((2 * n_col, occupied, 2 * virtuals, width), jnp.float32),
            pltpu.VMEM((ITERS,) + shape, jnp.float32),
            pltpu.VMEM(shape, jnp.float32),
            pltpu.VMEM(shape, jnp.float32),
            pltpu.VMEM((2 * size, 2 * width), jnp.bfloat16),
            pltpu.VMEM((2, span, 2 * width), jnp.bfloat16),
            pltpu.VMEM((2 * n_col, span, 2 * width), jnp.bfloat16),
            pltpu.VMEM((2 * size, span), jnp.float32),
            pltpu.VMEM((2 * size, span), jnp.bfloat16),
            pltpu.VMEM((2 * size, span), jnp.bfloat16),
            pltpu.VMEM((2,) + shape, jnp.float32),
            pltpu.VMEM((2, occupied, virtuals, LANES), jnp.float32),
            pltpu.VMEM((2 * n_col, 2 * occupied * virtuals // LANES, LANES), jnp.float32),
            pltpu.VMEM((ITERS, virtuals, LANES), jnp.float32),
            pltpu.VMEM((n_row, ITERS, virtuals, LANES), jnp.float32),
            pltpu.VMEM((n_col, ITERS, virtuals, LANES), jnp.float32),
            dma((PIECES,)),
            dma((2 * n_col, 4, PIECES)),
            dma((2 * n_col, 2, PIECES)),
            dma((PIECES,)),
            dma((PIECES,)),
            dma((PIECES,)),
            dma((PIECES,)),
            dma((n_row,)),
            dma((n_row,)),
            dma((n_col,)),
            dma((n_col,)),
            pltpu.SemaphoreType.REGULAR,
        ],
        compiler_params=pltpu.CompilerParams(collective_id=0, has_side_effects=True, vmem_limit_bytes=66 * 1000 * 1000),
    )(chol_t, eps_occ, eps_vir)
    return work.reshape(shard, width), jnp.sum(energies, axis=(1, 2)) / scale


def shards(chol, eps_occ, eps_vir):
    if lax.axis_size("row") == 8 and chol.shape[0] == 8 * eps_occ.shape[0] and eps_occ.shape[0] % 48 == 0:
        return fused(chol, eps_occ, eps_vir)
    n_row = lax.axis_size("row")
    n_col = lax.axis_size("col")
    row_index = lax.axis_index("row")
    col_index = lax.axis_index("col")
    shard, width = chol.shape
    occupied = eps_occ.shape[0]
    virtual = eps_vir.shape[0]
    shard_virtuals = shard // occupied
    block_virtuals = n_col * shard_virtuals
    total = virtual * occupied
    scale = jnp.float32(total)
    row_vir = lax.dynamic_slice_in_dim(eps_vir, row_index * block_virtuals, block_virtuals, 0)
    col_vir = lax.dynamic_slice_in_dim(
        eps_vir.reshape(n_row, block_virtuals), col_index * shard_virtuals, shard_virtuals, 1
    ).reshape(n_row * shard_virtuals)
    rpair = scale * (row_vir[None, :] - eps_occ[:, None])
    rpair = jnp.broadcast_to(rpair[:, :, None], (occupied, block_virtuals, LANES))
    cpair = (scale * (col_vir[None, :] - eps_occ[:, None])).reshape(-1, LANES)
    chol_t = jnp.transpose(chol.reshape(shard_virtuals, occupied, width), (1, 0, 2))
    chol_cols = gather(chol_t, "row")
    factor = chol_t
    sums = []
    for step in range(ITERS):
        if shard_virtuals % 8:
            rows = gather(factor, "col")
            turn = jnp.zeros((1,), jnp.int32)
        else:
            rows = passed(factor, "col")
            turn = jnp.full((1,), n_col - col_index, jnp.int32)
        cols = chol_cols if step == 0 else gather(factor, "row")
        partial_value = update(turn, rows, cols, chol_cols, rpair, cpair)
        if shard_virtuals % 8:
            partial_value = jnp.transpose(
                partial_value.reshape(occupied, n_col, shard_virtuals, width), (1, 0, 2, 3)
            )
        work = lax.psum_scatter(partial_value, "col", scatter_dimension=0, tiled=False)
        factor = chol_t + work
        sums.append(jnp.sum(chol_t * work))
    energies = lax.psum(jnp.stack(sums), ("row", "col"))
    return jnp.transpose(work, (1, 0, 2)).reshape(shard, width), energies / scale


def solution(mesh):
    placed = (P(("row", "col"), None), P(), P())
    return jax.shard_map(
        shards,
        mesh=mesh,
        in_specs=placed,
        out_specs=(P(("row", "col"), None), P()),
        check_vma=False,
    )
```

```python
import functools

import jax
import jax.numpy as jnp
from jax import lax
from jax.experimental import pallas as pl
from jax.experimental.pallas import tpu as pltpu
from jax.sharding import PartitionSpec as P

ITERS = 2
LANES = 128
NT = (((1,), (1,)), ((), ()))


def split(x):
    high = x.astype(jnp.bfloat16)
    low = (x - high.astype(jnp.float32)).astype(jnp.bfloat16)
    return high, low


def flat(ref, index, turn=None):
    parts = range(ref.shape[0])
    pieces = [ref[part if turn is None else (part + turn) % len(parts), index] for part in parts]
    return pieces[0] if len(pieces) == 1 else jnp.concatenate(pieces, axis=0)


def kernel(steps, turn_ref, rows_ref, cols_ref, chol_ref, rpair_ref, cpair_ref, out_ref, rows, cols, chol, direct, high_tile, low_tile):
    step = pl.program_id(0)
    parts, occupied, shard_virtuals, width = rows_ref.shape
    height = parts * shard_virtuals
    block = occupied // steps
    breadth = cols_ref.shape[0] * cols_ref.shape[2]
    span = block * breadth
    group = LANES // breadth

    @pl.when(step == 0)
    def _():
        def one(index, carry):
            high, low = split(flat(rows_ref, index, turn_ref[0]))
            at = pl.ds(pl.multiple_of(index * height, height), height)
            rows[at, :width] = high
            rows[at, width:] = low
            return carry

        lax.fori_loop(0, occupied, one, 0)

    @pl.when(step < steps)
    def _():
        for index in range(block):
            high, low = split(flat(cols_ref, index))
            cols[index * breadth : (index + 1) * breadth, :width] = low
            cols[index * breadth : (index + 1) * breadth, width:] = high
            high, low = split(flat(chol_ref, index))
            at = pl.ds(pl.multiple_of(step * span + index * breadth, breadth), breadth)
            chol[at, :width] = high
            chol[at, width:] = low

        def one(index, carry):
            at = pl.ds(pl.multiple_of(index * block * height, block * height), block * height)
            value = lax.dot_general(rows[at, :], cols[...], NT, preferred_element_type=jnp.float32)
            value += lax.dot_general(rows[at, :width], cols[:, width:], NT, preferred_element_type=jnp.float32)
            direct[at, pl.ds(pl.multiple_of(step * span, span), span)] = value
            return carry

        lax.fori_loop(0, steps, one, 0)

    @pl.when(step >= steps)
    def _():
        first = (step - steps) * block
        lane = lax.broadcasted_iota(jnp.int32, (height, LANES), 1) // breadth

        def one(index, carry):
            lead = first + index * group
            columns = pl.ds(pl.multiple_of(lead * breadth, LANES), LANES)
            bottoms = [rpair_ref[lead + own] for own in range(group)]
            for other in range(occupied // group):
                swapped = [direct[pl.ds((other * group + m) * height, height), columns] for m in range(group)]
                to = slice(other * LANES, (other + 1) * LANES)
                tops = cpair_ref[other : other + 1, :]
                for own in range(group):
                    exchange = swapped[0] if own == 0 else pltpu.roll(swapped[0], (LANES - own * breadth) % LANES, 1)
                    for m in range(1, group):
                        shift = ((m - own) * breadth) % LANES
                        moved = pltpu.roll(swapped[m], shift, 1) if shift else swapped[m]
                        exchange = jnp.where(lane == m, moved, exchange)
                    at = pl.ds(pl.multiple_of((lead + own) * height, height), height)
                    value = (exchange - 2.0 * direct[at, to]) / (bottoms[own] + tops)
                    high, low = split(value)
                    put = pl.ds(pl.multiple_of((index * group + own) * height, height), height)
                    high_tile[put, to] = high
                    low_tile[put, to] = low
            return carry

        lax.fori_loop(0, block // group, one, 0)
        both = jnp.dot(high_tile[...], chol[...], preferred_element_type=jnp.float32)
        value = both[:, :width] + both[:, width:]
        value += jnp.dot(low_tile[...], chol[:, :width], preferred_element_type=jnp.float32)
        value = value.reshape(block, parts, shard_virtuals, width)
        for part in range(parts):
            out_ref[part] = value[:, part]


def update(turn, rows, cols, chol, rpair, cpair):
    parts, occupied, shard_virtuals, width = rows.shape
    height = parts * shard_virtuals
    breadth = cols.shape[0] * cols.shape[2]
    steps = 6
    block = occupied // steps
    pair_columns = occupied * breadth
    column_block = (cols.shape[0], block, cols.shape[2], width)

    def of_columns(step):
        return (0, jnp.minimum(step, steps - 1), 0, 0)

    return pl.pallas_call(
        functools.partial(kernel, steps),
        grid=(2 * steps,),
        out_shape=jax.ShapeDtypeStruct(rows.shape, jnp.float32),
        in_specs=[
            pl.BlockSpec(memory_space=pltpu.SMEM),
            pl.BlockSpec(rows.shape, lambda step: (0, 0, 0, 0)),
            pl.BlockSpec(column_block, of_columns),
            pl.BlockSpec(column_block, of_columns),
            pl.BlockSpec(rpair.shape, lambda step: (0, 0, 0)),
            pl.BlockSpec(cpair.shape, lambda step: (0, 0)),
        ],
        out_specs=pl.BlockSpec((parts, block, shard_virtuals, width), lambda step: (0, jnp.maximum(step - steps, 0), 0, 0)),
        scratch_shapes=[
            pltpu.VMEM((occupied * height, 2 * width), jnp.bfloat16),
            pltpu.VMEM((block * breadth, 2 * width), jnp.bfloat16),
            pltpu.VMEM((pair_columns, 2 * width), jnp.bfloat16),
            pltpu.VMEM((occupied * height, pair_columns), jnp.float32),
            pltpu.VMEM((block * height, pair_columns), jnp.bfloat16),
            pltpu.VMEM((block * height, pair_columns), jnp.bfloat16),
        ],
        compiler_params=pltpu.CompilerParams(
            dimension_semantics=("arbitrary",), vmem_limit_bytes=66 * 1000 * 1000
        ),
        cost_estimate=pl.CostEstimate(
            flops=12 * occupied * height * pair_columns * width, bytes_accessed=4 * width * (2 * occupied * height + 2 * pair_columns), transcendentals=0
        ),
    )(turn, rows, cols, chol, rpair, cpair)


def gather(x, axis):
    parts = lax.all_gather(x, axis, axis=0)
    if x.shape[1] % 8:
        parts = jnp.transpose(parts, (1, 0, 2, 3)).reshape(1, x.shape[0], -1, x.shape[2])
    return parts


def passed(x, axis):
    n = lax.axis_size(axis)
    blocks = [x]
    for k in range(1, n):
        blocks.append(lax.ppermute(x, axis, [(j, (j - k) % n) for j in range(n)]))
    return jnp.stack(blocks)


PIECES = 6
CORE, ACROSS, UP, DOWN = 0, 1, 2, 3
MESH = pl.DeviceIdType.MESH


def place():
    row = lax.axis_index("row")
    core = lax.rem(row, 2)
    side = lax.rem(lax.div(row, 2), 2)
    half = lax.div(row, 4)
    return row, half, side, core, lax.axis_index("col")


def nearest(col, n_col, order):
    near = jnp.minimum(col, n_col - 1 - col)
    far = order - near
    away = jnp.where(col < n_col - 1 - col, far, -far)
    turn = lax.div(order + 1, 2) * (2 * lax.rem(order, 2) - 1)
    return col + jnp.where(order <= 2 * near, turn, away)


def fused_kernel(
    n_col, chol_ref, occ_ref, vir_ref, out_ref, energy_ref, land, held, back, factor, rows, fresh, kept, direct, other_direct, high_tile, other_high, low_tile, other_low, total, bottoms, tops,
    mine, around, along, facing, local_sem, send_sem, recv_sem, held_send, held_recv, back_send, back_recv, side_send, side_recv, line_send, line_recv, facing_sem, credit,
):
    row, half, side, core, col = place()
    n_row = 8
    occupied, width = chol_ref.shape[0], chol_ref.shape[2]
    virtuals = chol_ref.shape[1]
    size = occupied * virtuals
    span = occupied * 2 * virtuals
    part = occupied // PIECES
    chunks = 2 * n_col
    group = LANES // (2 * virtuals)
    blocks = occupied // group
    tall = group * virtuals
    partner = (row + 1 - 2 * core, col)
    beside = (row + 2 - 4 * side, col)
    across = (row + 4 - 8 * half, col)
    above = (row, col + 1)
    below = (row, col - 1)
    own_chunk = 2 * col + half

    def slot(chunk, owner, piece):
        return land.at[chunk, pl.ds(piece * part, part), pl.ds(pl.multiple_of(owner * virtuals, virtuals), virtuals), :]

    def move(source, chunk, target, piece, device):
        return pltpu.make_async_remote_copy(
            src_ref=source,
            dst_ref=slot(chunk, core, piece),
            send_sem=send_sem.at[chunk, target, piece],
            recv_sem=recv_sem.at[chunk, core, piece],
            device_id=device,
            device_id_type=MESH,
        )

    def landed(chunk, owner, piece):
        pltpu.make_async_remote_copy(
            src_ref=slot(chunk, owner, piece),
            dst_ref=slot(chunk, owner, piece),
            send_sem=send_sem.at[chunk, CORE, piece],
            recv_sem=recv_sem.at[chunk, owner, piece],
            device_id=partner,
            device_id_type=MESH,
        ).wait_recv()

    def pieces_of(ref, piece):
        return ref.at[pl.ds(piece * part, part), :, :]

    def lend(source, step, piece):
        return pltpu.make_async_remote_copy(
            src_ref=pieces_of(source, piece), dst_ref=pieces_of(held.at[step], piece), send_sem=held_send.at[piece], recv_sem=held_recv.at[piece], device_id=beside, device_id_type=MESH
        )

    def give(piece):
        return pltpu.make_async_remote_copy(
            src_ref=pieces_of(total.at[0], piece), dst_ref=pieces_of(back, piece), send_sem=back_send.at[piece], recv_sem=back_recv.at[piece], device_id=beside, device_id_type=MESH
        )

    def stay(source, piece):
        return pltpu.make_async_copy(pieces_of(source, piece), slot(own_chunk, core, piece), local_sem.at[piece])

    def take(value, start):
        high, low = split(value.reshape(-1, width))
        at = slice(start, start + high.shape[0])
        rows[at, :width] = low
        rows[at, width:] = high

    def publish(source, step, piece):
        @pl.when(col < n_col - 1)
        def _():
            move(pieces_of(source, piece), own_chunk, UP, piece, above).start()

        @pl.when(col > 0)
        def _():
            move(pieces_of(source, piece), own_chunk, DOWN, piece, below).start()

        lend(source, step, piece).start()
        move(pieces_of(source, piece), own_chunk, ACROSS, piece, across).start()
        move(pieces_of(source, piece), own_chunk, CORE, piece, partner).start()
        stay(source, piece).start()

    def relay(distance, first, last):
        def of(position, target, device, more):
            near = 2 * position + half
            away = near + 1 - 2 * half

            def one(piece, carry):
                landed(near, core, piece)

                @pl.when(more)
                def _():
                    move(slot(near, core, piece), near, target, piece, device).start()

                @pl.when(piece > 0)
                def _():
                    move(slot(near, core, piece), near, ACROSS, piece, across).start()

                @pl.when(piece == 0)
                def _():
                    landed(away, core, piece)

                    @pl.when(more)
                    def _():
                        move(slot(away, core, piece), away, target, piece, device).start()

                    move(slot(away, core, piece), away, CORE, piece, partner).start()

                move(slot(near, core, piece), near, CORE, piece, partner).start()
                return carry

            lax.fori_loop(first, last, one, 0)

        @pl.when(col + distance < n_col)
        def _():
            of(col + distance, DOWN, below, col > 0)

        @pl.when(col >= distance)
        def _():
            of(col - distance, UP, above, col < n_col - 1)

    def turn():
        chunk = own_chunk + 1 - 2 * half
        landed(chunk, core, 0)

        @pl.when(col < n_col - 1)
        def _():
            move(slot(chunk, core, 0), chunk, UP, 0, above).start()

        @pl.when(col > 0)
        def _():
            move(slot(chunk, core, 0), chunk, DOWN, 0, below).start()

        move(slot(chunk, core, 0), chunk, CORE, 0, partner).start()

    def cross(chunk, first, last):
        def one(piece, carry):
            landed(chunk, core, piece)
            move(slot(chunk, core, piece), chunk, CORE, piece, partner).start()
            return carry

        lax.fori_loop(first, last, one, 0)

    def settle():
        def one(position, carry):
            def each(piece, carry):
                near = 2 * position + half
                away = near + 1 - 2 * half

                def sent(chunk, target, device):
                    move(slot(chunk, core, piece), chunk, target, piece, device).wait_send()

                sent(near, CORE, partner)
                sent(away, CORE, partner)

                @pl.when((piece > 0) | (position == col))
                def _():
                    sent(near, ACROSS, across)

                @pl.when((position >= col) & (col > 0))
                def _():
                    sent(near, DOWN, below)

                    @pl.when(piece == 0)
                    def _():
                        sent(away, DOWN, below)

                @pl.when((position <= col) & (col < n_col - 1))
                def _():
                    sent(near, UP, above)

                    @pl.when(piece == 0)
                    def _():
                        sent(away, UP, above)

                return carry

            return lax.fori_loop(0, PIECES, each, carry)

        lax.fori_loop(0, n_col, one, 0)
        for piece in range(PIECES):
            lend(factor, 0, piece).wait_send()

    barrier = pltpu.get_barrier_semaphore()

    def same_side(other):
        return lax.rem(half + lax.div(other, 2), 2) * 4 + side * 2 + lax.rem(core + other, 2)

    def greet(device):
        pl.semaphore_signal(barrier, inc=1, device_id=device, device_id_type=MESH)

    greet(beside)
    for other in range(1, n_row // 2):
        greet((same_side(other), col))
    for other in range(1, n_col):
        greet((row, lax.rem(col + other, n_col)))
    pl.semaphore_wait(barrier, n_row // 2 + n_col - 1)

    for piece in range(PIECES):
        publish(chol_ref, 0, piece)
    take(chol_ref[...], size)

    scale = jnp.float32(occupied * virtuals * n_row * n_col)
    vertical = lax.broadcasted_iota(jnp.int32, (virtuals, LANES), 0)
    lateral = lax.broadcasted_iota(jnp.int32, (1, LANES), 1)

    for which in range(2):
        first = ((row + (1 - which) * (2 - 4 * side)) * n_col + col) * virtuals
        level = jnp.zeros((virtuals, LANES), jnp.float32)
        for index in range(virtuals):
            level = jnp.where(vertical == index, vir_ref[first + index], level)

        def lower(index, carry):
            bottoms[which, index] = scale * (level - occ_ref[index])
            return carry

        lax.fori_loop(0, occupied, lower, 0)

    def raised(chunk, carry):
        position, other = lax.div(chunk, 2), lax.rem(chunk, 2)
        level = jnp.zeros((1, LANES), jnp.float32)
        for index in range(2 * virtuals):
            source = (4 * other + 2 * side + index // virtuals) * n_col + position
            level = jnp.where(lax.rem(lateral, 2 * virtuals) == index, vir_ref[source * virtuals + index % virtuals], level)
        for block in range(blocks):
            deep = jnp.zeros((1, LANES), jnp.float32)
            for index in range(group):
                deep = jnp.where(lax.div(lateral, 2 * virtuals) == index, occ_ref[block * group + index], deep)
            tops[chunk, block : block + 1, :] = scale * (level - deep)
        return carry

    lax.fori_loop(0, chunks, raised, 0)

    def convert(step, chunk, place):
        def one(index, carry):
            high, low = split(land[chunk, index])
            at = pl.ds(pl.multiple_of(index * 2 * virtuals, 2 * virtuals), 2 * virtuals)
            fresh[place, at, :width] = high
            fresh[place, at, width:] = low

            @pl.when(step == 0)
            def _():
                kept[chunk, at, :width] = high
                kept[chunk, at, width:] = low

            return carry

        lax.fori_loop(0, occupied, one, 0, unroll=8)

    lane = lax.broadcasted_iota(jnp.int32, (virtuals, LANES), 1) // (2 * virtuals)

    products = (direct, other_direct)
    highs, lows = (high_tile, other_high), (low_tile, other_low)

    def product(which, place, part, start, count):
        at = pl.ds(pl.multiple_of(start, LANES), count)
        whose = pl.ds(pl.multiple_of(which * size, size), size)
        value = lax.dot_general(rows[whose, :], fresh[place, at, :], NT, preferred_element_type=jnp.float32)
        value += lax.dot_general(rows[whose, width:], fresh[place, at, :width], NT, preferred_element_type=jnp.float32)
        products[part][:, at] = value

    def amplitude(which, chunk, part, first, second):
        at = pl.ds(pl.multiple_of(first * tall, tall), tall)
        to = slice(second * LANES, (second + 1) * LANES)
        plain = products[part][at, to]
        turned = products[part][second * tall : (second + 1) * tall, pl.ds(pl.multiple_of(first * LANES, LANES), LANES)]
        skew = [turned[(-m) % group * virtuals : ((-m) % group + 1) * virtuals] for m in range(group)]
        skew = [pltpu.roll(value, (-m) % group * 2 * virtuals, 1) if m else value for m, value in enumerate(skew)]
        stride = 1
        while stride < group:
            upper = (lane & stride) != 0
            skew = [jnp.where(upper, skew[(m - stride) % group], skew[m]) for m in range(group)]
            stride *= 2
        top = tops[chunk, second : second + 1, :]
        values = []
        for m in range(group):
            exchange = pltpu.roll(skew[m], LANES - m * 2 * virtuals, 1) if m else skew[m]
            bottom = bottoms[which, first * group + m]
            values.append((exchange - 2.0 * plain[m * virtuals : (m + 1) * virtuals]) / (bottom + top))
        high, low = split(jnp.concatenate(values, axis=0))
        highs[part][at, to] = high
        lows[part][at, to] = low

    def collect(chunk, part, start, count):
        at = pl.ds(pl.multiple_of(start, tall), count)
        both = jnp.dot(highs[part][at, :], kept[chunk], preferred_element_type=jnp.float32)
        value = both[:, :width] + both[:, width:]
        value += jnp.dot(lows[part][at, :], kept[chunk, :, :width], preferred_element_type=jnp.float32)
        return value.reshape(count // virtuals, virtuals, width)

    cuts = span // (2 * LANES)

    def alone(which, chunk, place):
        product(which, place, 0, 0, span)

        def rate(index, carry):
            for block in range(2 * blocks):
                amplitude(which, chunk, 0, index * 2 + block // blocks, block % blocks)
            return carry

        lax.fori_loop(0, blocks // 2, rate, 0)
        total[which] += collect(chunk, 0, 0, size)

    def contract(one, two, last, between):
        (which, chunk, place), (other, second_chunk, second_place) = one, two
        product(which, place, 0, 0, span)

        def begin(index, carry):
            for block in range(blocks * blocks // cuts):
                amplitude(which, chunk, 0, index * (blocks // cuts) + block // blocks, block % blocks)
            product(other, second_place, 1, index * 2 * LANES, 2 * LANES)
            return carry

        lax.fori_loop(0, cuts, begin, 0)
        between()

        def finish(index, carry):
            for block in range(blocks * blocks // 2):
                amplitude(other, second_chunk, 1, index * (blocks // 2) + block // blocks, block % blocks)
            at = pl.ds(index * (occupied // 2), occupied // 2)
            total[which, at] += collect(chunk, 0, index * (size // 2), size // 2)

            @pl.when(last)
            def _():
                for piece in range(PIECES // 2):
                    give(index * (PIECES // 2) + piece).start()

            return carry

        lax.fori_loop(0, 2, finish, 0)
        total[other] += collect(second_chunk, 1, 0, size)

    def to_line(other):
        return pltpu.make_async_remote_copy(
            src_ref=mine, dst_ref=along.at[col], send_sem=line_send.at[other], recv_sem=line_recv.at[col], device_id=(row, lax.rem(col + other, n_col)), device_id_type=MESH
        )

    def from_line(other):
        source = lax.rem(col + other, n_col)
        return pltpu.make_async_remote_copy(
            src_ref=mine, dst_ref=along.at[source], send_sem=line_send.at[other], recv_sem=line_recv.at[source], device_id=(row, source), device_id_type=MESH
        )

    me = 2 * half + core

    def to_side(other):
        return pltpu.make_async_remote_copy(
            src_ref=around.at[me], dst_ref=around.at[me], send_sem=side_send.at[other], recv_sem=side_recv.at[me], device_id=(same_side(other), col), device_id_type=MESH
        )

    def from_side(other):
        source = 2 * lax.rem(half + lax.div(other, 2), 2) + lax.rem(core + other, 2)
        return pltpu.make_async_remote_copy(
            src_ref=around.at[source], dst_ref=around.at[source], send_sem=side_send.at[other], recv_sem=side_recv.at[source], device_id=(same_side(other), col), device_id_type=MESH
        )

    def to_beside():
        return pltpu.make_async_remote_copy(
            src_ref=facing.at[0], dst_ref=facing.at[1], send_sem=facing_sem.at[0], recv_sem=facing_sem.at[1], device_id=beside, device_id_type=MESH
        )

    def iterate(step, carry):
        total[...] = jnp.zeros_like(total)
        turn()
        for piece in range(PIECES):
            stay(factor, piece).wait()

        def chunk_of(index):
            return 2 * nearest(col, n_col, lax.div(index, 2)) + half + lax.rem(index, 2) * (1 - 2 * half)

        def there(chunk):
            def one(piece, carry):
                landed(chunk, 1 - core, piece)
                return carry

            lax.fori_loop(0, PIECES, one, 0)

        def one(index, carry):
            chunk = chunk_of(jnp.where(index >= 4, index - 1, jnp.where((index == 1) | (index == 2), 1, 0)))

            def pass_on(event):
                @pl.when((event >= 0) & (event < (n_col - 2) * PIECES))
                def _():
                    piece = lax.rem(event, PIECES)
                    relay(2 + lax.div(event, PIECES), piece, piece + 1)

            first = jnp.where(index < 4, 2 * index - 3, 2 * index - 4)
            pass_on(first)

            @pl.when(index == chunks - 1)
            def _():
                pass_on(first + 1)

            @pl.when(index == 0)
            def _():
                there(own_chunk)
                convert(step, own_chunk, 0)

            @pl.when(index == 1)
            def _():
                relay(1, 0, PIECES)
                cross(chunk, 1, PIECES)
                there(chunk)
                convert(step, chunk, 1)
                there(chunk_of(2))
                convert(step, chunk_of(2), 2)

            @pl.when(index == 2)
            def _():
                for piece in range(PIECES):
                    lend(factor, step, piece).wait_recv()
                take(held[step], 0)

            @pl.when(index == 3)
            def _():
                cross(chunk_of(3), 1, PIECES // 2)

            @pl.when(index >= 4)
            def _():
                @pl.when(index == 4)
                def _():
                    cross(chunk, PIECES // 2, PIECES)

                @pl.when((index > 4) & (lax.rem(index, 2) == 0))
                def _():
                    cross(chunk, PIECES - 1, PIECES)

                there(chunk)
                convert(step, chunk, 1)

            @pl.when(lax.rem(index, 3) == 0)
            def _():
                @pl.when(index < 4)
                def _():
                    alone(jnp.where(index == 0, 1, 0), own_chunk, 0)

            @pl.when((index == 1) | (index == 2) | (index >= 4))
            def _():
                def between():
                    @pl.when(index != chunks - 1)
                    def _():
                        pass_on(first + 1)

                    @pl.when((index > 4) & (lax.rem(index, 2) == 1))
                    def _():
                        cross(chunk_of(index), 1, PIECES - 1)

                which = jnp.where(index == 1, 1, 0)
                other = jnp.where(index == 2, 0, 1)
                second = chunk_of(jnp.where(index < 4, 2, index - 1))
                contract((which, chunk, 1), (other, second, jnp.where(index < 4, 2, 1)), index == chunks, between)

            return carry

        lax.fori_loop(0, chunks + 1, one, 0)
        settle()

        @pl.when(step == 0)
        def _():
            def thank(device):
                pl.semaphore_signal(credit, inc=1, device_id=device, device_id_type=MESH)

            thank(partner)
            thank(beside)
            thank(across)

            @pl.when(col < n_col - 1)
            def _():
                thank(above)

            @pl.when(col > 0)
            def _():
                thank(below)

            pl.semaphore_wait(credit, 3 + jnp.minimum(col, 1) + jnp.minimum(n_col - 1 - col, 1))

        def weigh(index, energy):
            return energy + chol_ref[index] * total[1, index] + held[0, index] * total[0, index]

        energy = lax.fori_loop(0, occupied, weigh, jnp.zeros((virtuals, width), jnp.float32), unroll=4)
        folded = energy[:, :LANES]
        for index in range(1, width // LANES):
            folded += energy[:, index * LANES : (index + 1) * LANES]
        mine[step] = folded

        @pl.when(step == ITERS - 1)
        def _():
            along[col] = mine[...]
            for other in range(1, n_col):
                to_line(other).start()

        for piece in range(PIECES):
            if piece == PIECES // 3:

                @pl.when(step == ITERS - 1)
                def _():
                    for other in range(1, n_col):
                        from_line(other).wait_recv()
                    around[me] = sum(along[index] for index in range(n_col))
                    for other in range(1, n_row // 2):
                        to_side(other).start()

            if piece == 2 * PIECES // 3:

                @pl.when(step == ITERS - 1)
                def _():
                    for other in range(1, n_row // 2):
                        from_side(other).wait_recv()
                    facing[0] = sum(around[index] for index in range(n_row // 2))
                    to_beside().start()

            give(piece).wait_recv()
            at = slice(piece * part, (piece + 1) * part)
            value = total[1, at] + back[at]

            @pl.when(step == 0)
            def _():
                fresh_rows = chol_ref[at] + value
                factor[at] = fresh_rows
                publish(factor, 1, piece)
                take(fresh_rows, size + piece * part * virtuals)

            @pl.when(step == ITERS - 1)
            def _():
                out_ref[:, at, :] = jnp.transpose(value, (1, 0, 2))

        for piece in range(PIECES):
            give(piece).wait_send()
        return carry

    lax.fori_loop(0, ITERS, iterate, 0)
    to_beside().wait_recv()
    energy_ref[...] = facing[0] + facing[1]
    to_beside().wait_send()
    for other in range(1, n_col):
        to_line(other).wait_send()
    for other in range(1, n_row // 2):
        to_side(other).wait_send()


def fused(chol, eps_occ, eps_vir):
    n_col = lax.axis_size("col")
    n_row = lax.axis_size("row")
    shard, width = chol.shape
    occupied = eps_occ.shape[0]
    virtuals = shard // occupied
    scale = jnp.float32(eps_vir.shape[0] * occupied)
    size, span = shard, 2 * shard
    chol_t = jnp.transpose(chol.reshape(virtuals, occupied, width), (1, 0, 2))
    shape = (occupied, virtuals, width)
    dma = pltpu.SemaphoreType.DMA
    work, energies = pl.pallas_call(
        functools.partial(fused_kernel, n_col),
        out_shape=(jax.ShapeDtypeStruct((virtuals, occupied, width), jnp.float32), jax.ShapeDtypeStruct((ITERS, virtuals, LANES), jnp.float32)),
        in_specs=[pl.BlockSpec(memory_space=pltpu.VMEM), pl.BlockSpec(memory_space=pltpu.SMEM), pl.BlockSpec(memory_space=pltpu.SMEM)],
        out_specs=(pl.BlockSpec(memory_space=pltpu.VMEM), pl.BlockSpec(memory_space=pltpu.VMEM)),
        scratch_shapes=[
            pltpu.VMEM((2 * n_col, occupied, 2 * virtuals, width), jnp.float32),
            pltpu.VMEM((ITERS,) + shape, jnp.float32),
            pltpu.VMEM(shape, jnp.float32),
            pltpu.VMEM(shape, jnp.float32),
            pltpu.VMEM((2 * size, 2 * width), jnp.bfloat16),
            pltpu.VMEM((3, span, 2 * width), jnp.bfloat16),
            pltpu.VMEM((2 * n_col, span, 2 * width), jnp.bfloat16),
            pltpu.VMEM((size, span), jnp.float32),
            pltpu.VMEM((size, span), jnp.float32),
            pltpu.VMEM((size, span), jnp.bfloat16),
            pltpu.VMEM((size, span), jnp.bfloat16),
            pltpu.VMEM((size, span), jnp.bfloat16),
            pltpu.VMEM((size, span), jnp.bfloat16),
            pltpu.VMEM((2,) + shape, jnp.float32),
            pltpu.VMEM((2, occupied, virtuals, LANES), jnp.float32),
            pltpu.VMEM((2 * n_col, 2 * occupied * virtuals // LANES, LANES), jnp.float32),
            pltpu.VMEM((ITERS, virtuals, LANES), jnp.float32),
            pltpu.VMEM((n_row // 2, ITERS, virtuals, LANES), jnp.float32),
            pltpu.VMEM((n_col, ITERS, virtuals, LANES), jnp.float32),
            pltpu.VMEM((2, ITERS, virtuals, LANES), jnp.float32),
            dma((PIECES,)),
            dma((2 * n_col, 4, PIECES)),
            dma((2 * n_col, 2, PIECES)),
            dma((PIECES,)),
            dma((PIECES,)),
            dma((PIECES,)),
            dma((PIECES,)),
            dma((n_row // 2,)),
            dma((n_row // 2,)),
            dma((n_col,)),
            dma((n_col,)),
            dma((2,)),
            pltpu.SemaphoreType.REGULAR,
        ],
        compiler_params=pltpu.CompilerParams(collective_id=0, has_side_effects=True, vmem_limit_bytes=66 * 1000 * 1000),
    )(chol_t, eps_occ, eps_vir)
    return work.reshape(shard, width), jnp.sum(energies, axis=(1, 2)) / scale


def shards(chol, eps_occ, eps_vir):
    if lax.axis_size("row") == 8 and chol.shape[0] == 8 * eps_occ.shape[0] and eps_occ.shape[0] % 48 == 0:
        return fused(chol, eps_occ, eps_vir)
    n_row = lax.axis_size("row")
    n_col = lax.axis_size("col")
    row_index = lax.axis_index("row")
    col_index = lax.axis_index("col")
    shard, width = chol.shape
    occupied = eps_occ.shape[0]
    virtual = eps_vir.shape[0]
    shard_virtuals = shard // occupied
    block_virtuals = n_col * shard_virtuals
    total = virtual * occupied
    scale = jnp.float32(total)
    row_vir = lax.dynamic_slice_in_dim(eps_vir, row_index * block_virtuals, block_virtuals, 0)
    col_vir = lax.dynamic_slice_in_dim(
        eps_vir.reshape(n_row, block_virtuals), col_index * shard_virtuals, shard_virtuals, 1
    ).reshape(n_row * shard_virtuals)
    rpair = scale * (row_vir[None, :] - eps_occ[:, None])
    rpair = jnp.broadcast_to(rpair[:, :, None], (occupied, block_virtuals, LANES))
    cpair = (scale * (col_vir[None, :] - eps_occ[:, None])).reshape(-1, LANES)
    chol_t = jnp.transpose(chol.reshape(shard_virtuals, occupied, width), (1, 0, 2))
    chol_cols = gather(chol_t, "row")
    factor = chol_t
    sums = []
    for step in range(ITERS):
        if shard_virtuals % 8:
            rows = gather(factor, "col")
            turn = jnp.zeros((1,), jnp.int32)
        else:
            rows = passed(factor, "col")
            turn = jnp.full((1,), n_col - col_index, jnp.int32)
        cols = chol_cols if step == 0 else gather(factor, "row")
        partial_value = update(turn, rows, cols, chol_cols, rpair, cpair)
        if shard_virtuals % 8:
            partial_value = jnp.transpose(
                partial_value.reshape(occupied, n_col, shard_virtuals, width), (1, 0, 2, 3)
            )
        work = lax.psum_scatter(partial_value, "col", scatter_dimension=0, tiled=False)
        factor = chol_t + work
        sums.append(jnp.sum(chol_t * work))
    energies = lax.psum(jnp.stack(sums), ("row", "col"))
    return jnp.transpose(work, (1, 0, 2)).reshape(shard, width), energies / scale


def solution(mesh):
    placed = (P(("row", "col"), None), P(), P())
    return jax.shard_map(
        shards,
        mesh=mesh,
        in_specs=placed,
        out_specs=(P(("row", "col"), None), P()),
        check_vma=False,
    )
```

```python
import functools

import jax
import jax.numpy as jnp
from jax import lax
from jax.experimental import pallas as pl
from jax.experimental.pallas import tpu as pltpu
from jax.sharding import PartitionSpec as P

ITERS = 2
LANES = 128
NT = (((1,), (1,)), ((), ()))


def split(x):
    high = x.astype(jnp.bfloat16)
    low = (x - high.astype(jnp.float32)).astype(jnp.bfloat16)
    return high, low


def flat(ref, index, turn=None):
    parts = range(ref.shape[0])
    pieces = [ref[part if turn is None else (part + turn) % len(parts), index] for part in parts]
    return pieces[0] if len(pieces) == 1 else jnp.concatenate(pieces, axis=0)


def kernel(steps, turn_ref, rows_ref, cols_ref, chol_ref, rpair_ref, cpair_ref, out_ref, rows, cols, chol, direct, high_tile, low_tile):
    step = pl.program_id(0)
    parts, occupied, shard_virtuals, width = rows_ref.shape
    height = parts * shard_virtuals
    block = occupied // steps
    breadth = cols_ref.shape[0] * cols_ref.shape[2]
    span = block * breadth
    group = LANES // breadth

    @pl.when(step == 0)
    def _():
        def one(index, carry):
            high, low = split(flat(rows_ref, index, turn_ref[0]))
            at = pl.ds(pl.multiple_of(index * height, height), height)
            rows[at, :width] = high
            rows[at, width:] = low
            return carry

        lax.fori_loop(0, occupied, one, 0)

    @pl.when(step < steps)
    def _():
        for index in range(block):
            high, low = split(flat(cols_ref, index))
            cols[index * breadth : (index + 1) * breadth, :width] = low
            cols[index * breadth : (index + 1) * breadth, width:] = high
            high, low = split(flat(chol_ref, index))
            at = pl.ds(pl.multiple_of(step * span + index * breadth, breadth), breadth)
            chol[at, :width] = high
            chol[at, width:] = low

        def one(index, carry):
            at = pl.ds(pl.multiple_of(index * block * height, block * height), block * height)
            value = lax.dot_general(rows[at, :], cols[...], NT, preferred_element_type=jnp.float32)
            value += lax.dot_general(rows[at, :width], cols[:, width:], NT, preferred_element_type=jnp.float32)
            direct[at, pl.ds(pl.multiple_of(step * span, span), span)] = value
            return carry

        lax.fori_loop(0, steps, one, 0)

    @pl.when(step >= steps)
    def _():
        first = (step - steps) * block
        lane = lax.broadcasted_iota(jnp.int32, (height, LANES), 1) // breadth

        def one(index, carry):
            lead = first + index * group
            columns = pl.ds(pl.multiple_of(lead * breadth, LANES), LANES)
            bottoms = [rpair_ref[lead + own] for own in range(group)]
            for other in range(occupied // group):
                swapped = [direct[pl.ds((other * group + m) * height, height), columns] for m in range(group)]
                to = slice(other * LANES, (other + 1) * LANES)
                tops = cpair_ref[other : other + 1, :]
                for own in range(group):
                    exchange = swapped[0] if own == 0 else pltpu.roll(swapped[0], (LANES - own * breadth) % LANES, 1)
                    for m in range(1, group):
                        shift = ((m - own) * breadth) % LANES
                        moved = pltpu.roll(swapped[m], shift, 1) if shift else swapped[m]
                        exchange = jnp.where(lane == m, moved, exchange)
                    at = pl.ds(pl.multiple_of((lead + own) * height, height), height)
                    value = (exchange - 2.0 * direct[at, to]) / (bottoms[own] + tops)
                    high, low = split(value)
                    put = pl.ds(pl.multiple_of((index * group + own) * height, height), height)
                    high_tile[put, to] = high
                    low_tile[put, to] = low
            return carry

        lax.fori_loop(0, block // group, one, 0)
        both = jnp.dot(high_tile[...], chol[...], preferred_element_type=jnp.float32)
        value = both[:, :width] + both[:, width:]
        value += jnp.dot(low_tile[...], chol[:, :width], preferred_element_type=jnp.float32)
        value = value.reshape(block, parts, shard_virtuals, width)
        for part in range(parts):
            out_ref[part] = value[:, part]


def update(turn, rows, cols, chol, rpair, cpair):
    parts, occupied, shard_virtuals, width = rows.shape
    height = parts * shard_virtuals
    breadth = cols.shape[0] * cols.shape[2]
    steps = 6
    block = occupied // steps
    pair_columns = occupied * breadth
    column_block = (cols.shape[0], block, cols.shape[2], width)

    def of_columns(step):
        return (0, jnp.minimum(step, steps - 1), 0, 0)

    return pl.pallas_call(
        functools.partial(kernel, steps),
        grid=(2 * steps,),
        out_shape=jax.ShapeDtypeStruct(rows.shape, jnp.float32),
        in_specs=[
            pl.BlockSpec(memory_space=pltpu.SMEM),
            pl.BlockSpec(rows.shape, lambda step: (0, 0, 0, 0)),
            pl.BlockSpec(column_block, of_columns),
            pl.BlockSpec(column_block, of_columns),
            pl.BlockSpec(rpair.shape, lambda step: (0, 0, 0)),
            pl.BlockSpec(cpair.shape, lambda step: (0, 0)),
        ],
        out_specs=pl.BlockSpec((parts, block, shard_virtuals, width), lambda step: (0, jnp.maximum(step - steps, 0), 0, 0)),
        scratch_shapes=[
            pltpu.VMEM((occupied * height, 2 * width), jnp.bfloat16),
            pltpu.VMEM((block * breadth, 2 * width), jnp.bfloat16),
            pltpu.VMEM((pair_columns, 2 * width), jnp.bfloat16),
            pltpu.VMEM((occupied * height, pair_columns), jnp.float32),
            pltpu.VMEM((block * height, pair_columns), jnp.bfloat16),
            pltpu.VMEM((block * height, pair_columns), jnp.bfloat16),
        ],
        compiler_params=pltpu.CompilerParams(
            dimension_semantics=("arbitrary",), vmem_limit_bytes=66 * 1000 * 1000
        ),
        cost_estimate=pl.CostEstimate(
            flops=12 * occupied * height * pair_columns * width, bytes_accessed=4 * width * (2 * occupied * height + 2 * pair_columns), transcendentals=0
        ),
    )(turn, rows, cols, chol, rpair, cpair)


def gather(x, axis):
    parts = lax.all_gather(x, axis, axis=0)
    if x.shape[1] % 8:
        parts = jnp.transpose(parts, (1, 0, 2, 3)).reshape(1, x.shape[0], -1, x.shape[2])
    return parts


def passed(x, axis):
    n = lax.axis_size(axis)
    blocks = [x]
    for k in range(1, n):
        blocks.append(lax.ppermute(x, axis, [(j, (j - k) % n) for j in range(n)]))
    return jnp.stack(blocks)


PIECES = 6
LAST = PIECES - 1
CORE, ACROSS, UP, DOWN = 0, 1, 2, 3
MESH = pl.DeviceIdType.MESH


def place():
    row = lax.axis_index("row")
    core = lax.rem(row, 2)
    side = lax.rem(lax.div(row, 2), 2)
    half = lax.div(row, 4)
    return row, half, side, core, lax.axis_index("col")


def nearest(col, n_col, order):
    near = jnp.minimum(col, n_col - 1 - col)
    far = order - near
    away = jnp.where(col < n_col - 1 - col, far, -far)
    turn = lax.div(order + 1, 2) * (2 * lax.rem(order, 2) - 1)
    return col + jnp.where(order <= 2 * near, turn, away)


def fused_kernel(
    n_col, given_ref, occ_ref, vir_ref, out_ref, energy_ref, given, chol_ref, land, held, back, factor, rows, fresh, kept, direct, other_direct, high_tile, other_high, low_tile, other_low, total, bottoms, tops,
    mine, around, along, facing, local_sem, send_sem, recv_sem, held_send, held_recv, back_send, back_recv, side_send, side_recv, line_send, line_recv, facing_sem, given_sem, credit,
):
    row, half, side, core, col = place()
    n_row = 8
    bring = pltpu.make_async_copy(given_ref, given, given_sem)
    bring.start()
    occupied, width = chol_ref.shape[0], chol_ref.shape[2]
    virtuals = chol_ref.shape[1]
    size = occupied * virtuals
    span = occupied * 2 * virtuals
    part = occupied // PIECES
    chunks = 2 * n_col
    group = LANES // (2 * virtuals)
    blocks = occupied // group
    tall = group * virtuals
    partner = (row + 1 - 2 * core, col)
    beside = (row + 2 - 4 * side, col)
    across = (row + 4 - 8 * half, col)
    above = (row, col + 1)
    below = (row, col - 1)
    own_chunk = 2 * col + half

    def slot(chunk, owner, piece):
        return land.at[chunk, pl.ds(piece * part, part), pl.ds(pl.multiple_of(owner * virtuals, virtuals), virtuals), :]

    def move(source, chunk, target, piece, device):
        return pltpu.make_async_remote_copy(
            src_ref=source,
            dst_ref=slot(chunk, core, piece),
            send_sem=send_sem.at[chunk, target, piece],
            recv_sem=recv_sem.at[chunk, core, piece],
            device_id=device,
            device_id_type=MESH,
        )

    def landed(chunk, owner, piece):
        pltpu.make_async_remote_copy(
            src_ref=slot(chunk, owner, piece),
            dst_ref=slot(chunk, owner, piece),
            send_sem=send_sem.at[chunk, CORE, piece],
            recv_sem=recv_sem.at[chunk, owner, piece],
            device_id=partner,
            device_id_type=MESH,
        ).wait_recv()

    def pieces_of(ref, piece):
        return ref.at[pl.ds(piece * part, part), :, :]

    def lend(source, step, piece):
        return pltpu.make_async_remote_copy(
            src_ref=pieces_of(source, piece), dst_ref=pieces_of(held.at[step], piece), send_sem=held_send.at[piece], recv_sem=held_recv.at[piece], device_id=beside, device_id_type=MESH
        )

    def give(piece):
        return pltpu.make_async_remote_copy(
            src_ref=pieces_of(total.at[0], piece), dst_ref=pieces_of(back, piece), send_sem=back_send.at[piece], recv_sem=back_recv.at[piece], device_id=beside, device_id_type=MESH
        )

    def stay(source, piece):
        return pltpu.make_async_copy(pieces_of(source, piece), slot(own_chunk, core, piece), local_sem.at[piece])

    def take(value, start):
        high, low = split(value.reshape(-1, width))
        at = slice(start, start + high.shape[0])
        rows[at, :width] = low
        rows[at, width:] = high

    def publish(source, step, piece):
        @pl.when(col < n_col - 1)
        def _():
            move(pieces_of(source, piece), own_chunk, UP, piece, above).start()

        @pl.when(col > 0)
        def _():
            move(pieces_of(source, piece), own_chunk, DOWN, piece, below).start()

        lend(source, step, piece).start()
        move(pieces_of(source, piece), own_chunk, ACROSS, piece, across).start()
        move(pieces_of(source, piece), own_chunk, CORE, piece, partner).start()
        stay(source, piece).start()

    def relay(distance, first, last):
        def of(position, target, device, more):
            near = 2 * position + half
            away = near + 1 - 2 * half

            def one(order, carry):
                piece = lax.rem(order + 1, PIECES)
                landed(near, core, piece)

                @pl.when(more)
                def _():
                    move(slot(near, core, piece), near, target, piece, device).start()

                @pl.when(piece > 0)
                def _():
                    move(slot(near, core, piece), near, ACROSS, piece, across).start()

                @pl.when(piece == 0)
                def _():
                    landed(away, core, piece)

                    @pl.when(more)
                    def _():
                        move(slot(away, core, piece), away, target, piece, device).start()

                    move(slot(away, core, piece), away, CORE, piece, partner).start()

                move(slot(near, core, piece), near, CORE, piece, partner).start()
                return carry

            lax.fori_loop(first, last, one, 0)

        @pl.when(col + distance < n_col)
        def _():
            of(col + distance, DOWN, below, col > 0)

        @pl.when(col >= distance)
        def _():
            of(col - distance, UP, above, col < n_col - 1)

    def turn():
        chunk = own_chunk + 1 - 2 * half
        landed(chunk, core, 0)

        @pl.when(col < n_col - 1)
        def _():
            move(slot(chunk, core, 0), chunk, UP, 0, above).start()

        @pl.when(col > 0)
        def _():
            move(slot(chunk, core, 0), chunk, DOWN, 0, below).start()

        move(slot(chunk, core, 0), chunk, CORE, 0, partner).start()

    def cross(chunk, first, last):
        def one(order, carry):
            piece = order + 1
            landed(chunk, core, piece)
            move(slot(chunk, core, piece), chunk, CORE, piece, partner).start()
            return carry

        lax.fori_loop(first, last, one, 0)

    def settle(step):
        def one(position, carry):
            def each(piece, carry):
                near = 2 * position + half
                away = near + 1 - 2 * half

                def sent(chunk, target, device):
                    move(slot(chunk, core, piece), chunk, target, piece, device).wait_send()

                sent(near, CORE, partner)
                sent(away, CORE, partner)

                @pl.when((piece > 0) | (position == col))
                def _():
                    sent(near, ACROSS, across)

                @pl.when((position >= col) & (col > 0))
                def _():
                    sent(near, DOWN, below)

                    @pl.when(piece == 0)
                    def _():
                        sent(away, DOWN, below)

                @pl.when((position <= col) & (col < n_col - 1))
                def _():
                    sent(near, UP, above)

                    @pl.when(piece == 0)
                    def _():
                        sent(away, UP, above)

                return carry

            return lax.fori_loop(0, PIECES, each, carry)

        lax.fori_loop(0, n_col, one, 0)
        for piece in range(PIECES):
            lend(factor, 0, piece).wait_send()

        @pl.when(step == 0)
        def _():
            def thank(device):
                pl.semaphore_signal(credit, inc=1, device_id=device, device_id_type=MESH)

            thank(partner)
            thank(beside)
            thank(across)

            @pl.when(col < n_col - 1)
            def _():
                thank(above)

            @pl.when(col > 0)
            def _():
                thank(below)

    barrier = pltpu.get_barrier_semaphore()

    def same_side(other):
        return lax.rem(half + lax.div(other, 2), 2) * 4 + side * 2 + lax.rem(core + other, 2)

    def greet(device):
        pl.semaphore_signal(barrier, inc=1, device_id=device, device_id_type=MESH)

    greet(beside)
    for other in range(1, n_row // 2):
        greet((same_side(other), col))
    for other in range(1, n_col):
        greet((row, lax.rem(col + other, n_col)))
    bring.wait()
    for piece in range(PIECES):
        at = slice(piece * part, (piece + 1) * part)
        chol_ref[at] = jnp.transpose(given[:, at, :], (1, 0, 2))
    pl.semaphore_wait(barrier, n_row // 2 + n_col - 1)

    for piece in range(PIECES):
        publish(chol_ref, 0, piece)
    take(chol_ref[...], size)

    scale = jnp.float32(occupied * virtuals * n_row * n_col)
    vertical = lax.broadcasted_iota(jnp.int32, (virtuals, LANES), 0)
    lateral = lax.broadcasted_iota(jnp.int32, (1, LANES), 1)

    for which in range(2):
        first = ((row + (1 - which) * (2 - 4 * side)) * n_col + col) * virtuals
        level = jnp.zeros((virtuals, LANES), jnp.float32)
        for index in range(virtuals):
            level = jnp.where(vertical == index, vir_ref[first + index], level)

        def lower(index, carry):
            bottoms[which, index] = scale * (level - occ_ref[index])
            return carry

        lax.fori_loop(0, occupied, lower, 0)

    def raised(chunk, carry):
        position, other = lax.div(chunk, 2), lax.rem(chunk, 2)
        level = jnp.zeros((1, LANES), jnp.float32)
        for index in range(2 * virtuals):
            source = (4 * other + 2 * side + index // virtuals) * n_col + position
            level = jnp.where(lax.rem(lateral, 2 * virtuals) == index, vir_ref[source * virtuals + index % virtuals], level)
        for block in range(blocks):
            deep = jnp.zeros((1, LANES), jnp.float32)
            for index in range(group):
                deep = jnp.where(lax.div(lateral, 2 * virtuals) == index, occ_ref[block * group + index], deep)
            tops[chunk, block : block + 1, :] = scale * (level - deep)
        return carry

    lax.fori_loop(0, chunks, raised, 0)

    def convert(step, chunk, place):
        def one(index, carry):
            high, low = split(land[chunk, index])
            at = pl.ds(pl.multiple_of(index * 2 * virtuals, 2 * virtuals), 2 * virtuals)
            fresh[place, at, :width] = high
            fresh[place, at, width:] = low

            @pl.when(step == 0)
            def _():
                kept[chunk, at, :width] = high
                kept[chunk, at, width:] = low

            return carry

        lax.fori_loop(0, occupied, one, 0, unroll=8)

    lane = lax.broadcasted_iota(jnp.int32, (virtuals, LANES), 1) // (2 * virtuals)

    products = (direct, other_direct)
    highs, lows = (high_tile, other_high), (low_tile, other_low)

    def product(which, place, part, start, count):
        at = pl.ds(pl.multiple_of(start, LANES), count)
        whose = pl.ds(pl.multiple_of(which * size, size), size)
        value = lax.dot_general(rows[whose, :], fresh[place, at, :], NT, preferred_element_type=jnp.float32)
        value += lax.dot_general(rows[whose, width:], fresh[place, at, :width], NT, preferred_element_type=jnp.float32)
        products[part][:, at] = value

    def amplitude(which, chunk, part, first, second):
        at = pl.ds(pl.multiple_of(first * tall, tall), tall)
        to = slice(second * LANES, (second + 1) * LANES)
        plain = products[part][at, to]
        turned = products[part][second * tall : (second + 1) * tall, pl.ds(pl.multiple_of(first * LANES, LANES), LANES)]
        skew = [turned[(-m) % group * virtuals : ((-m) % group + 1) * virtuals] for m in range(group)]
        skew = [pltpu.roll(value, (-m) % group * 2 * virtuals, 1) if m else value for m, value in enumerate(skew)]
        stride = 1
        while stride < group:
            upper = (lane & stride) != 0
            skew = [jnp.where(upper, skew[(m - stride) % group], skew[m]) for m in range(group)]
            stride *= 2
        top = tops[chunk, second : second + 1, :]
        values = []
        for m in range(group):
            exchange = pltpu.roll(skew[m], LANES - m * 2 * virtuals, 1) if m else skew[m]
            bottom = bottoms[which, first * group + m]
            values.append((exchange - 2.0 * plain[m * virtuals : (m + 1) * virtuals]) / (bottom + top))
        high, low = split(jnp.concatenate(values, axis=0))
        highs[part][at, to] = high
        lows[part][at, to] = low

    def collect(chunk, part, start, count):
        at = pl.ds(pl.multiple_of(start, tall), count)
        both = jnp.dot(highs[part][at, :], kept[chunk], preferred_element_type=jnp.float32)
        value = both[:, :width] + both[:, width:]
        value += jnp.dot(lows[part][at, :], kept[chunk, :, :width], preferred_element_type=jnp.float32)
        return value.reshape(count // virtuals, virtuals, width)

    cuts = span // (2 * LANES)

    def alone(which, chunk, place):
        product(which, place, 0, 0, span)

        def rate(index, carry):
            for block in range(2 * blocks):
                amplitude(which, chunk, 0, index * 2 + block // blocks, block % blocks)
            return carry

        lax.fori_loop(0, blocks // 2, rate, 0)
        total[which] += collect(chunk, 0, 0, size)

    def contract(one, two, between):
        (which, chunk, place), (other, second_chunk, second_place) = one, two
        product(which, place, 0, 0, span)

        def begin(index, carry):
            for block in range(blocks * blocks // cuts):
                amplitude(which, chunk, 0, index * (blocks // cuts) + block // blocks, block % blocks)
            product(other, second_place, 1, index * 2 * LANES, 2 * LANES)
            return carry

        lax.fori_loop(0, cuts, begin, 0)
        between()

        def finish(index, carry):
            for block in range(blocks * blocks // 2):
                amplitude(other, second_chunk, 1, index * (blocks // 2) + block // blocks, block % blocks)
            at = pl.ds(index * (occupied // 2), occupied // 2)
            total[which, at] += collect(chunk, 0, index * (size // 2), size // 2)

            return carry

        lax.fori_loop(0, 2, finish, 0)
        total[other] += collect(second_chunk, 1, 0, size)

    def to_line(other):
        return pltpu.make_async_remote_copy(
            src_ref=mine, dst_ref=along.at[col], send_sem=line_send.at[other], recv_sem=line_recv.at[col], device_id=(row, lax.rem(col + other, n_col)), device_id_type=MESH
        )

    def from_line(other):
        source = lax.rem(col + other, n_col)
        return pltpu.make_async_remote_copy(
            src_ref=mine, dst_ref=along.at[source], send_sem=line_send.at[other], recv_sem=line_recv.at[source], device_id=(row, source), device_id_type=MESH
        )

    me = 2 * half + core

    def to_side(other):
        return pltpu.make_async_remote_copy(
            src_ref=around.at[me], dst_ref=around.at[me], send_sem=side_send.at[other], recv_sem=side_recv.at[me], device_id=(same_side(other), col), device_id_type=MESH
        )

    def from_side(other):
        source = 2 * lax.rem(half + lax.div(other, 2), 2) + lax.rem(core + other, 2)
        return pltpu.make_async_remote_copy(
            src_ref=around.at[source], dst_ref=around.at[source], send_sem=side_send.at[other], recv_sem=side_recv.at[source], device_id=(same_side(other), col), device_id_type=MESH
        )

    def to_beside():
        return pltpu.make_async_remote_copy(
            src_ref=facing.at[0], dst_ref=facing.at[1], send_sem=facing_sem.at[0], recv_sem=facing_sem.at[1], device_id=beside, device_id_type=MESH
        )

    def iterate(step, carry):
        total[...] = jnp.zeros_like(total)
        for piece in range(PIECES):
            stay(factor, piece).wait()

        def chunk_of(index):
            return 2 * nearest(col, n_col, lax.div(index, 2)) + half + lax.rem(index, 2) * (1 - 2 * half)

        def there(chunk):
            def one(piece, carry):
                landed(chunk, 1 - core, piece)
                return carry

            lax.fori_loop(0, PIECES, one, 0)

        def one(index, carry):
            chunk = chunk_of(jnp.where(index >= 4, jnp.minimum(index, chunks - 1) - 1, jnp.where((index == 1) | (index == 2), 1, 0)))

            def pass_on(event):
                @pl.when((event >= 0) & (event < (n_col - 2) * PIECES))
                def _():
                    piece = lax.rem(event, PIECES)
                    relay(2 + lax.div(event, PIECES), piece, piece + 1)

            first = jnp.where(index < 4, 2 * index - 3, 2 * index - 4)
            pass_on(first)

            @pl.when(index == chunks - 1)
            def _():
                pass_on(first + 1)

            @pl.when(index == 0)
            def _():
                there(own_chunk)
                convert(step, own_chunk, 0)

            @pl.when(index == 1)
            def _():
                turn()
                relay(1, 0, PIECES)
                cross(chunk, 0, LAST)
                there(chunk)
                convert(step, chunk, 1)
                there(chunk_of(2))
                convert(step, chunk_of(2), 2)

            @pl.when(index == 2)
            def _():
                for piece in range(PIECES):
                    lend(factor, step, piece).wait_recv()
                take(held[step], 0)

            @pl.when(index == 3)
            def _():
                cross(chunk_of(3), 0, PIECES // 2)

            @pl.when(index == 4)
            def _():
                cross(chunk, PIECES // 2, LAST)

            @pl.when(index == 6)
            def _():
                cross(chunk, LAST - 1, LAST)

            @pl.when((index >= 4) & (index < chunks))
            def _():
                there(chunk)
                convert(step, chunk, 1)

            @pl.when(index == chunks - 1)
            def _():
                cross(chunk_of(index), LAST - 2, LAST)
                there(chunk_of(index))
                convert(step, chunk_of(index), 2)

            @pl.when(index == chunks)
            def _():
                for piece in range(PIECES):
                    give(piece).start()
                settle(step)

            @pl.when(lax.rem(index, 3) == 0)
            def _():
                @pl.when(index < 4)
                def _():
                    alone(jnp.where(index == 0, 1, 0), own_chunk, 0)

            @pl.when((index == 1) | (index == 2) | (index >= 4))
            def _():
                def between():
                    @pl.when(index != chunks - 1)
                    def _():
                        pass_on(first + 1)

                    @pl.when(index == 5)
                    def _():
                        cross(chunk_of(5), 0, LAST - 1)

                    @pl.when(index == 6)
                    def _():
                        cross(chunk_of(7), 0, LAST - 2)

                late = index >= chunks - 1
                which = jnp.where((index == 1) | (index == chunks), 1, 0)
                other = jnp.where((index == 2) | (index == chunks - 1), 0, 1)
                second = jnp.where(index < 4, 2, jnp.where(late, chunks - 1, index - 1))
                contract((which, chunk, 1), (other, chunk_of(second), jnp.where((index < 4) | late, 2, 1)), between)

            return carry

        lax.fori_loop(0, chunks + 1, one, 0)
        @pl.when(step == 0)
        def _():
            pl.semaphore_wait(credit, 3 + jnp.minimum(col, 1) + jnp.minimum(n_col - 1 - col, 1))

        def weigh(index, energy):
            return energy + chol_ref[index] * total[1, index] + held[0, index] * total[0, index]

        def tally():
            energy = lax.fori_loop(0, occupied, weigh, jnp.zeros((virtuals, width), jnp.float32), unroll=4)
            folded = energy[:, :LANES]
            for index in range(1, width // LANES):
                folded += energy[:, index * LANES : (index + 1) * LANES]
            mine[step] = folded

        @pl.when(step == ITERS - 1)
        def _():
            tally()
            along[col] = mine[...]
            for other in range(1, n_col):
                to_line(other).start()

        for piece in range(PIECES):
            if piece == PIECES // 3:

                @pl.when(step == ITERS - 1)
                def _():
                    for other in range(1, n_col):
                        from_line(other).wait_recv()
                    around[me] = sum(along[index] for index in range(n_col))
                    for other in range(1, n_row // 2):
                        to_side(other).start()

            if piece == 2 * PIECES // 3:

                @pl.when(step == ITERS - 1)
                def _():
                    for other in range(1, n_row // 2):
                        from_side(other).wait_recv()
                    facing[0] = sum(around[index] for index in range(n_row // 2))
                    to_beside().start()

            give(piece).wait_recv()
            at = slice(piece * part, (piece + 1) * part)
            value = total[1, at] + back[at]

            @pl.when(step == 0)
            def _():
                fresh_rows = chol_ref[at] + value
                factor[at] = fresh_rows
                publish(factor, 1, piece)
                take(fresh_rows, size + piece * part * virtuals)

            @pl.when(step == ITERS - 1)
            def _():
                out_ref[:, at, :] = jnp.transpose(value, (1, 0, 2))

        for piece in range(PIECES):
            give(piece).wait_send()

        @pl.when(step == 0)
        def _():
            tally()

        return carry

    lax.fori_loop(0, ITERS, iterate, 0)
    to_beside().wait_recv()
    both = facing[0] + facing[1]
    for step in range(ITERS):
        energy_ref[step] = jnp.sum(both[step]) / scale
    to_beside().wait_send()
    for other in range(1, n_col):
        to_line(other).wait_send()
    for other in range(1, n_row // 2):
        to_side(other).wait_send()


def fused(chol, eps_occ, eps_vir):
    n_col = lax.axis_size("col")
    n_row = lax.axis_size("row")
    shard, width = chol.shape
    occupied = eps_occ.shape[0]
    virtuals = shard // occupied
    size, span = shard, 2 * shard
    shape = (occupied, virtuals, width)
    dma = pltpu.SemaphoreType.DMA
    work, energies = pl.pallas_call(
        functools.partial(fused_kernel, n_col),
        out_shape=(jax.ShapeDtypeStruct((virtuals, occupied, width), jnp.float32), jax.ShapeDtypeStruct((ITERS,), jnp.float32)),
        in_specs=[pl.BlockSpec(memory_space=pl.ANY), pl.BlockSpec(memory_space=pltpu.SMEM), pl.BlockSpec(memory_space=pltpu.SMEM)],
        out_specs=(pl.BlockSpec(memory_space=pltpu.VMEM), pl.BlockSpec(memory_space=pltpu.SMEM)),
        scratch_shapes=[
            pltpu.VMEM((virtuals, occupied, width), jnp.float32),
            pltpu.VMEM(shape, jnp.float32),
            pltpu.VMEM((2 * n_col, occupied, 2 * virtuals, width), jnp.float32),
            pltpu.VMEM((ITERS,) + shape, jnp.float32),
            pltpu.VMEM(shape, jnp.float32),
            pltpu.VMEM(shape, jnp.float32),
            pltpu.VMEM((2 * size, 2 * width), jnp.bfloat16),
            pltpu.VMEM((3, span, 2 * width), jnp.bfloat16),
            pltpu.VMEM((2 * n_col, span, 2 * width), jnp.bfloat16),
            pltpu.VMEM((size, span), jnp.float32),
            pltpu.VMEM((size, span), jnp.float32),
            pltpu.VMEM((size, span), jnp.bfloat16),
            pltpu.VMEM((size, span), jnp.bfloat16),
            pltpu.VMEM((size, span), jnp.bfloat16),
            pltpu.VMEM((size, span), jnp.bfloat16),
            pltpu.VMEM((2,) + shape, jnp.float32),
            pltpu.VMEM((2, occupied, virtuals, LANES), jnp.float32),
            pltpu.VMEM((2 * n_col, 2 * occupied * virtuals // LANES, LANES), jnp.float32),
            pltpu.VMEM((ITERS, virtuals, LANES), jnp.float32),
            pltpu.VMEM((n_row // 2, ITERS, virtuals, LANES), jnp.float32),
            pltpu.VMEM((n_col, ITERS, virtuals, LANES), jnp.float32),
            pltpu.VMEM((2, ITERS, virtuals, LANES), jnp.float32),
            dma((PIECES,)),
            dma((2 * n_col, 4, PIECES)),
            dma((2 * n_col, 2, PIECES)),
            dma((PIECES,)),
            dma((PIECES,)),
            dma((PIECES,)),
            dma((PIECES,)),
            dma((n_row // 2,)),
            dma((n_row // 2,)),
            dma((n_col,)),
            dma((n_col,)),
            dma((2,)),
            dma(()),
            pltpu.SemaphoreType.REGULAR,
        ],
        compiler_params=pltpu.CompilerParams(collective_id=0, has_side_effects=True, vmem_limit_bytes=66 * 1000 * 1000),
    )(chol.reshape(virtuals, occupied, width), eps_occ, eps_vir)
    return work.reshape(shard, width), energies


def shards(chol, eps_occ, eps_vir):
    if lax.axis_size("row") == 8 and chol.shape[0] == 8 * eps_occ.shape[0] and eps_occ.shape[0] % 48 == 0:
        return fused(chol, eps_occ, eps_vir)
    n_row = lax.axis_size("row")
    n_col = lax.axis_size("col")
    row_index = lax.axis_index("row")
    col_index = lax.axis_index("col")
    shard, width = chol.shape
    occupied = eps_occ.shape[0]
    virtual = eps_vir.shape[0]
    shard_virtuals = shard // occupied
    block_virtuals = n_col * shard_virtuals
    total = virtual * occupied
    scale = jnp.float32(total)
    row_vir = lax.dynamic_slice_in_dim(eps_vir, row_index * block_virtuals, block_virtuals, 0)
    col_vir = lax.dynamic_slice_in_dim(
        eps_vir.reshape(n_row, block_virtuals), col_index * shard_virtuals, shard_virtuals, 1
    ).reshape(n_row * shard_virtuals)
    rpair = scale * (row_vir[None, :] - eps_occ[:, None])
    rpair = jnp.broadcast_to(rpair[:, :, None], (occupied, block_virtuals, LANES))
    cpair = (scale * (col_vir[None, :] - eps_occ[:, None])).reshape(-1, LANES)
    chol_t = jnp.transpose(chol.reshape(shard_virtuals, occupied, width), (1, 0, 2))
    chol_cols = gather(chol_t, "row")
    factor = chol_t
    sums = []
    for step in range(ITERS):
        if shard_virtuals % 8:
            rows = gather(factor, "col")
            turn = jnp.zeros((1,), jnp.int32)
        else:
            rows = passed(factor, "col")
            turn = jnp.full((1,), n_col - col_index, jnp.int32)
        cols = chol_cols if step == 0 else gather(factor, "row")
        partial_value = update(turn, rows, cols, chol_cols, rpair, cpair)
        if shard_virtuals % 8:
            partial_value = jnp.transpose(
                partial_value.reshape(occupied, n_col, shard_virtuals, width), (1, 0, 2, 3)
            )
        work = lax.psum_scatter(partial_value, "col", scatter_dimension=0, tiled=False)
        factor = chol_t + work
        sums.append(jnp.sum(chol_t * work))
    energies = lax.psum(jnp.stack(sums), ("row", "col"))
    return jnp.transpose(work, (1, 0, 2)).reshape(shard, width), energies / scale


def solution(mesh):
    placed = (P(("row", "col"), None), P(), P())
    return jax.shard_map(
        shards,
        mesh=mesh,
        in_specs=placed,
        out_specs=(P(("row", "col"), None), P()),
        check_vma=False,
    )
```

```python
import functools

import jax
import jax.numpy as jnp
from jax import lax
from jax.experimental import pallas as pl
from jax.experimental.pallas import tpu as pltpu
from jax.sharding import PartitionSpec as P

ITERS = 2
LANES = 128
NT = (((1,), (1,)), ((), ()))


def split(x):
    high = x.astype(jnp.bfloat16)
    low = (x - high.astype(jnp.float32)).astype(jnp.bfloat16)
    return high, low


def flat(ref, index, turn=None):
    parts = range(ref.shape[0])
    pieces = [ref[part if turn is None else (part + turn) % len(parts), index] for part in parts]
    return pieces[0] if len(pieces) == 1 else jnp.concatenate(pieces, axis=0)


def kernel(steps, turn_ref, rows_ref, cols_ref, chol_ref, rpair_ref, cpair_ref, out_ref, rows, cols, chol, direct, high_tile, low_tile):
    step = pl.program_id(0)
    parts, occupied, shard_virtuals, width = rows_ref.shape
    height = parts * shard_virtuals
    block = occupied // steps
    breadth = cols_ref.shape[0] * cols_ref.shape[2]
    span = block * breadth
    group = LANES // breadth

    @pl.when(step == 0)
    def _():
        def one(index, carry):
            high, low = split(flat(rows_ref, index, turn_ref[0]))
            at = pl.ds(pl.multiple_of(index * height, height), height)
            rows[at, :width] = high
            rows[at, width:] = low
            return carry

        lax.fori_loop(0, occupied, one, 0)

    @pl.when(step < steps)
    def _():
        for index in range(block):
            high, low = split(flat(cols_ref, index))
            cols[index * breadth : (index + 1) * breadth, :width] = low
            cols[index * breadth : (index + 1) * breadth, width:] = high
            high, low = split(flat(chol_ref, index))
            at = pl.ds(pl.multiple_of(step * span + index * breadth, breadth), breadth)
            chol[at, :width] = high
            chol[at, width:] = low

        def one(index, carry):
            at = pl.ds(pl.multiple_of(index * block * height, block * height), block * height)
            value = lax.dot_general(rows[at, :], cols[...], NT, preferred_element_type=jnp.float32)
            value += lax.dot_general(rows[at, :width], cols[:, width:], NT, preferred_element_type=jnp.float32)
            direct[at, pl.ds(pl.multiple_of(step * span, span), span)] = value
            return carry

        lax.fori_loop(0, steps, one, 0)

    @pl.when(step >= steps)
    def _():
        first = (step - steps) * block
        lane = lax.broadcasted_iota(jnp.int32, (height, LANES), 1) // breadth

        def one(index, carry):
            lead = first + index * group
            columns = pl.ds(pl.multiple_of(lead * breadth, LANES), LANES)
            bottoms = [rpair_ref[lead + own] for own in range(group)]
            for other in range(occupied // group):
                swapped = [direct[pl.ds((other * group + m) * height, height), columns] for m in range(group)]
                to = slice(other * LANES, (other + 1) * LANES)
                tops = cpair_ref[other : other + 1, :]
                for own in range(group):
                    exchange = swapped[0] if own == 0 else pltpu.roll(swapped[0], (LANES - own * breadth) % LANES, 1)
                    for m in range(1, group):
                        shift = ((m - own) * breadth) % LANES
                        moved = pltpu.roll(swapped[m], shift, 1) if shift else swapped[m]
                        exchange = jnp.where(lane == m, moved, exchange)
                    at = pl.ds(pl.multiple_of((lead + own) * height, height), height)
                    value = (exchange - 2.0 * direct[at, to]) / (bottoms[own] + tops)
                    high, low = split(value)
                    put = pl.ds(pl.multiple_of((index * group + own) * height, height), height)
                    high_tile[put, to] = high
                    low_tile[put, to] = low
            return carry

        lax.fori_loop(0, block // group, one, 0)
        both = jnp.dot(high_tile[...], chol[...], preferred_element_type=jnp.float32)
        value = both[:, :width] + both[:, width:]
        value += jnp.dot(low_tile[...], chol[:, :width], preferred_element_type=jnp.float32)
        value = value.reshape(block, parts, shard_virtuals, width)
        for part in range(parts):
            out_ref[part] = value[:, part]


def update(turn, rows, cols, chol, rpair, cpair):
    parts, occupied, shard_virtuals, width = rows.shape
    height = parts * shard_virtuals
    breadth = cols.shape[0] * cols.shape[2]
    steps = 6
    block = occupied // steps
    pair_columns = occupied * breadth
    column_block = (cols.shape[0], block, cols.shape[2], width)

    def of_columns(step):
        return (0, jnp.minimum(step, steps - 1), 0, 0)

    return pl.pallas_call(
        functools.partial(kernel, steps),
        grid=(2 * steps,),
        out_shape=jax.ShapeDtypeStruct(rows.shape, jnp.float32),
        in_specs=[
            pl.BlockSpec(memory_space=pltpu.SMEM),
            pl.BlockSpec(rows.shape, lambda step: (0, 0, 0, 0)),
            pl.BlockSpec(column_block, of_columns),
            pl.BlockSpec(column_block, of_columns),
            pl.BlockSpec(rpair.shape, lambda step: (0, 0, 0)),
            pl.BlockSpec(cpair.shape, lambda step: (0, 0)),
        ],
        out_specs=pl.BlockSpec((parts, block, shard_virtuals, width), lambda step: (0, jnp.maximum(step - steps, 0), 0, 0)),
        scratch_shapes=[
            pltpu.VMEM((occupied * height, 2 * width), jnp.bfloat16),
            pltpu.VMEM((block * breadth, 2 * width), jnp.bfloat16),
            pltpu.VMEM((pair_columns, 2 * width), jnp.bfloat16),
            pltpu.VMEM((occupied * height, pair_columns), jnp.float32),
            pltpu.VMEM((block * height, pair_columns), jnp.bfloat16),
            pltpu.VMEM((block * height, pair_columns), jnp.bfloat16),
        ],
        compiler_params=pltpu.CompilerParams(
            dimension_semantics=("arbitrary",), vmem_limit_bytes=66 * 1000 * 1000
        ),
        cost_estimate=pl.CostEstimate(
            flops=12 * occupied * height * pair_columns * width, bytes_accessed=4 * width * (2 * occupied * height + 2 * pair_columns), transcendentals=0
        ),
    )(turn, rows, cols, chol, rpair, cpair)


def gather(x, axis):
    parts = lax.all_gather(x, axis, axis=0)
    if x.shape[1] % 8:
        parts = jnp.transpose(parts, (1, 0, 2, 3)).reshape(1, x.shape[0], -1, x.shape[2])
    return parts


def passed(x, axis):
    n = lax.axis_size(axis)
    blocks = [x]
    for k in range(1, n):
        blocks.append(lax.ppermute(x, axis, [(j, (j - k) % n) for j in range(n)]))
    return jnp.stack(blocks)


PIECES = 6
LAST = PIECES - 1
CORE, ACROSS, UP, DOWN = 0, 1, 2, 3
MESH = pl.DeviceIdType.MESH


def place():
    row = lax.axis_index("row")
    core = lax.rem(row, 2)
    side = lax.rem(lax.div(row, 2), 2)
    half = lax.div(row, 4)
    return row, half, side, core, lax.axis_index("col")


def nearest(col, n_col, order):
    near = jnp.minimum(col, n_col - 1 - col)
    far = order - near
    away = jnp.where(col < n_col - 1 - col, far, -far)
    turn = lax.div(order + 1, 2) * (2 * lax.rem(order, 2) - 1)
    return col + jnp.where(order <= 2 * near, turn, away)


def fused_kernel(
    n_col, given_ref, occ_ref, vir_ref, out_ref, energy_ref, given, chol_ref, land, held, back, factor, rows, fresh, kept, direct, other_direct, high_tile, other_high, low_tile, other_low, total, bottoms, tops,
    mine, around, along, facing, local_sem, send_sem, recv_sem, held_send, held_recv, back_send, back_recv, side_send, side_recv, line_send, line_recv, facing_sem, given_sem, pair_recv, credit,
):
    row, half, side, core, col = place()
    n_row = 8
    bring = pltpu.make_async_copy(given_ref, given, given_sem)
    bring.start()
    occupied, width = chol_ref.shape[0], chol_ref.shape[2]
    virtuals = chol_ref.shape[1]
    size = occupied * virtuals
    span = occupied * 2 * virtuals
    part = occupied // PIECES
    chunks = 2 * n_col
    group = LANES // (2 * virtuals)
    blocks = occupied // group
    tall = group * virtuals
    partner = (row + 1 - 2 * core, col)
    beside = (row + 2 - 4 * side, col)
    across = (row + 4 - 8 * half, col)
    above = (row, col + 1)
    below = (row, col - 1)
    own_chunk = 2 * col + half

    def slot(chunk, owner, piece):
        return land.at[chunk, owner, pl.ds(piece * part, part), :, :]

    def move(source, chunk, target, piece, device):
        return pltpu.make_async_remote_copy(
            src_ref=source,
            dst_ref=slot(chunk, core, piece),
            send_sem=send_sem.at[chunk, target],
            recv_sem=pair_recv.at[chunk] if target == CORE else recv_sem.at[chunk, piece],
            device_id=device,
            device_id_type=MESH,
        )

    def landed(chunk, piece):
        pltpu.make_async_remote_copy(
            src_ref=slot(chunk, core, piece),
            dst_ref=slot(chunk, core, piece),
            send_sem=send_sem.at[chunk, CORE],
            recv_sem=recv_sem.at[chunk, piece],
            device_id=partner,
            device_id_type=MESH,
        ).wait_recv()

    def paired(chunk):
        pltpu.make_async_remote_copy(
            src_ref=land.at[chunk, 1 - core],
            dst_ref=land.at[chunk, 1 - core],
            send_sem=send_sem.at[chunk, CORE],
            recv_sem=pair_recv.at[chunk],
            device_id=partner,
            device_id_type=MESH,
        ).wait_recv()

    def sent(ref, chunk, target, device):
        pltpu.make_async_remote_copy(
            src_ref=ref, dst_ref=ref, send_sem=send_sem.at[chunk, target], recv_sem=pair_recv.at[chunk], device_id=device, device_id_type=MESH
        ).wait_send()

    def pieces_of(ref, piece):
        return ref.at[pl.ds(piece * part, part), :, :]

    def lend(source, step, piece):
        return pltpu.make_async_remote_copy(
            src_ref=pieces_of(source, piece), dst_ref=pieces_of(held.at[step], piece), send_sem=held_send, recv_sem=held_recv, device_id=beside, device_id_type=MESH
        )

    def lent(step):
        return pltpu.make_async_remote_copy(
            src_ref=factor, dst_ref=held.at[step], send_sem=held_send, recv_sem=held_recv, device_id=beside, device_id_type=MESH
        )

    def gave():
        return pltpu.make_async_remote_copy(
            src_ref=total.at[0], dst_ref=back, send_sem=back_send, recv_sem=back_recv.at[0], device_id=beside, device_id_type=MESH
        )

    def give(piece):
        return pltpu.make_async_remote_copy(
            src_ref=pieces_of(total.at[0], piece), dst_ref=pieces_of(back, piece), send_sem=back_send, recv_sem=back_recv.at[piece], device_id=beside, device_id_type=MESH
        )

    def stay(source, piece):
        return pltpu.make_async_copy(pieces_of(source, piece), slot(own_chunk, core, piece), local_sem)

    def take(value, start):
        high, low = split(value.reshape(-1, width))
        at = slice(start, start + high.shape[0])
        rows[at, :width] = low
        rows[at, width:] = high

    def publish(source, step, piece):
        @pl.when(col < n_col - 1)
        def _():
            move(pieces_of(source, piece), own_chunk, UP, piece, above).start()

        @pl.when(col > 0)
        def _():
            move(pieces_of(source, piece), own_chunk, DOWN, piece, below).start()

        lend(source, step, piece).start()
        move(pieces_of(source, piece), own_chunk, ACROSS, piece, across).start()
        move(pieces_of(source, piece), own_chunk, CORE, piece, partner).start()
        stay(source, piece).start()

    def relay(distance, first, last):
        def of(position, target, device, more):
            near = 2 * position + half
            away = near + 1 - 2 * half

            def one(order, carry):
                piece = lax.rem(order + 1, PIECES)
                landed(near, piece)

                @pl.when(more)
                def _():
                    move(slot(near, core, piece), near, target, piece, device).start()

                @pl.when(piece > 0)
                def _():
                    move(slot(near, core, piece), near, ACROSS, piece, across).start()

                @pl.when(piece == 0)
                def _():
                    landed(away, piece)

                    @pl.when(more)
                    def _():
                        move(slot(away, core, piece), away, target, piece, device).start()

                    move(slot(away, core, piece), away, CORE, piece, partner).start()

                move(slot(near, core, piece), near, CORE, piece, partner).start()
                return carry

            lax.fori_loop(first, last, one, 0)

        @pl.when(col + distance < n_col)
        def _():
            of(col + distance, DOWN, below, col > 0)

        @pl.when(col >= distance)
        def _():
            of(col - distance, UP, above, col < n_col - 1)

    def turn():
        chunk = own_chunk + 1 - 2 * half
        landed(chunk, 0)

        @pl.when(col < n_col - 1)
        def _():
            move(slot(chunk, core, 0), chunk, UP, 0, above).start()

        @pl.when(col > 0)
        def _():
            move(slot(chunk, core, 0), chunk, DOWN, 0, below).start()

        move(slot(chunk, core, 0), chunk, CORE, 0, partner).start()

    def cross(chunk, first, last):
        def one(order, carry):
            piece = order + 1
            landed(chunk, piece)
            move(slot(chunk, core, piece), chunk, CORE, piece, partner).start()
            return carry

        lax.fori_loop(first, last, one, 0)

    def settle(step):
        def one(position, carry):
            near = 2 * position + half
            away = near + 1 - 2 * half
            sent(land.at[near, core], near, CORE, partner)
            sent(land.at[away, core], away, CORE, partner)

            @pl.when(position == col)
            def _():
                sent(land.at[near, core], near, ACROSS, across)

            @pl.when(position != col)
            def _():
                sent(land.at[near, core, pl.ds(part, occupied - part), :, :], near, ACROSS, across)

            @pl.when((position >= col) & (col > 0))
            def _():
                sent(land.at[near, core], near, DOWN, below)
                sent(slot(away, core, 0), away, DOWN, below)

            @pl.when((position <= col) & (col < n_col - 1))
            def _():
                sent(land.at[near, core], near, UP, above)
                sent(slot(away, core, 0), away, UP, above)

            return carry

        lax.fori_loop(0, n_col, one, 0)
        lent(0).wait_send()

        @pl.when(step == 0)
        def _():
            def thank(device):
                pl.semaphore_signal(credit, inc=1, device_id=device, device_id_type=MESH)

            thank(partner)
            thank(beside)
            thank(across)

            @pl.when(col < n_col - 1)
            def _():
                thank(above)

            @pl.when(col > 0)
            def _():
                thank(below)

    barrier = pltpu.get_barrier_semaphore()

    def same_side(other):
        return lax.rem(half + lax.div(other, 2), 2) * 4 + side * 2 + lax.rem(core + other, 2)

    def greet(device):
        pl.semaphore_signal(barrier, inc=1, device_id=device, device_id_type=MESH)

    greet(beside)
    for other in range(1, n_row // 2):
        greet((same_side(other), col))
    for other in range(1, n_col):
        greet((row, lax.rem(col + other, n_col)))
    bring.wait()
    for piece in range(PIECES):
        at = slice(piece * part, (piece + 1) * part)
        chol_ref[at] = jnp.transpose(given[:, at, :], (1, 0, 2))
    pl.semaphore_wait(barrier, n_row // 2 + n_col - 1)

    for piece in range(PIECES):
        publish(chol_ref, 0, piece)
    take(chol_ref[...], size)

    scale = jnp.float32(occupied * virtuals * n_row * n_col)
    vertical = lax.broadcasted_iota(jnp.int32, (virtuals, LANES), 0)
    lateral = lax.broadcasted_iota(jnp.int32, (1, LANES), 1)

    for which in range(2):
        first = ((row + (1 - which) * (2 - 4 * side)) * n_col + col) * virtuals
        level = jnp.zeros((virtuals, LANES), jnp.float32)
        for index in range(virtuals):
            level = jnp.where(vertical == index, vir_ref[first + index], level)

        def lower(index, carry):
            bottoms[which, index] = scale * (level - occ_ref[index])
            return carry

        lax.fori_loop(0, occupied, lower, 0)

    def raised(chunk, carry):
        position, other = lax.div(chunk, 2), lax.rem(chunk, 2)
        level = jnp.zeros((1, LANES), jnp.float32)
        for index in range(2 * virtuals):
            source = (4 * other + 2 * side + index // virtuals) * n_col + position
            level = jnp.where(lax.rem(lateral, 2 * virtuals) == index, vir_ref[source * virtuals + index % virtuals], level)
        for block in range(blocks):
            deep = jnp.zeros((1, LANES), jnp.float32)
            for index in range(group):
                deep = jnp.where(lax.div(lateral, 2 * virtuals) == index, occ_ref[block * group + index], deep)
            tops[chunk, block : block + 1, :] = scale * (level - deep)
        return carry

    lax.fori_loop(0, chunks, raised, 0)

    def convert(step, chunk, place):
        def one(index, carry):
            high, low = split(jnp.concatenate([land[chunk, 0, index], land[chunk, 1, index]], axis=0))
            at = pl.ds(pl.multiple_of(index * 2 * virtuals, 2 * virtuals), 2 * virtuals)
            fresh[place, at, :width] = high
            fresh[place, at, width:] = low

            @pl.when(step == 0)
            def _():
                kept[chunk, at, :width] = high
                kept[chunk, at, width:] = low

            return carry

        lax.fori_loop(0, occupied, one, 0, unroll=8)

    lane = lax.broadcasted_iota(jnp.int32, (virtuals, LANES), 1) // (2 * virtuals)

    products = (direct, other_direct)
    highs, lows = (high_tile, other_high), (low_tile, other_low)

    def product(which, place, part, start, count):
        at = pl.ds(pl.multiple_of(start, LANES), count)
        whose = pl.ds(pl.multiple_of(which * size, size), size)
        value = lax.dot_general(rows[whose, :], fresh[place, at, :], NT, preferred_element_type=jnp.float32)
        value += lax.dot_general(rows[whose, width:], fresh[place, at, :width], NT, preferred_element_type=jnp.float32)
        products[part][:, at] = value

    def amplitude(which, chunk, part, first, second):
        at = pl.ds(pl.multiple_of(first * tall, tall), tall)
        to = slice(second * LANES, (second + 1) * LANES)
        plain = products[part][at, to]
        turned = products[part][second * tall : (second + 1) * tall, pl.ds(pl.multiple_of(first * LANES, LANES), LANES)]
        skew = [turned[(-m) % group * virtuals : ((-m) % group + 1) * virtuals] for m in range(group)]
        skew = [pltpu.roll(value, (-m) % group * 2 * virtuals, 1) if m else value for m, value in enumerate(skew)]
        stride = 1
        while stride < group:
            upper = (lane & stride) != 0
            skew = [jnp.where(upper, skew[(m - stride) % group], skew[m]) for m in range(group)]
            stride *= 2
        top = tops[chunk, second : second + 1, :]
        values = []
        for m in range(group):
            exchange = pltpu.roll(skew[m], LANES - m * 2 * virtuals, 1) if m else skew[m]
            bottom = bottoms[which, first * group + m]
            values.append((exchange - 2.0 * plain[m * virtuals : (m + 1) * virtuals]) / (bottom + top))
        high, low = split(jnp.concatenate(values, axis=0))
        highs[part][at, to] = high
        lows[part][at, to] = low

    def collect(chunk, part, start, count):
        at = pl.ds(pl.multiple_of(start, tall), count)
        both = jnp.dot(highs[part][at, :], kept[chunk], preferred_element_type=jnp.float32)
        value = both[:, :width] + both[:, width:]
        value += jnp.dot(lows[part][at, :], kept[chunk, :, :width], preferred_element_type=jnp.float32)
        return value.reshape(count // virtuals, virtuals, width)

    cuts = span // (2 * LANES)

    def alone(which, chunk, place):
        product(which, place, 0, 0, span)

        def rate(index, carry):
            for block in range(2 * blocks):
                amplitude(which, chunk, 0, index * 2 + block // blocks, block % blocks)
            return carry

        lax.fori_loop(0, blocks // 2, rate, 0)
        total[which] += collect(chunk, 0, 0, size)

    def contract(one, two, between):
        (which, chunk, place), (other, second_chunk, second_place) = one, two
        product(which, place, 0, 0, span)

        def begin(index, carry):
            for block in range(blocks * blocks // cuts):
                amplitude(which, chunk, 0, index * (blocks // cuts) + block // blocks, block % blocks)
            product(other, second_place, 1, index * 2 * LANES, 2 * LANES)
            return carry

        lax.fori_loop(0, cuts, begin, 0)
        between()

        def finish(index, carry):
            for block in range(blocks * blocks // 2):
                amplitude(other, second_chunk, 1, index * (blocks // 2) + block // blocks, block % blocks)
            at = pl.ds(index * (occupied // 2), occupied // 2)
            total[which, at] += collect(chunk, 0, index * (size // 2), size // 2)

            return carry

        lax.fori_loop(0, 2, finish, 0)
        total[other] += collect(second_chunk, 1, 0, size)

    def to_line(other):
        return pltpu.make_async_remote_copy(
            src_ref=mine, dst_ref=along.at[col], send_sem=line_send.at[other], recv_sem=line_recv.at[col], device_id=(row, lax.rem(col + other, n_col)), device_id_type=MESH
        )

    def from_line(other):
        source = lax.rem(col + other, n_col)
        return pltpu.make_async_remote_copy(
            src_ref=mine, dst_ref=along.at[source], send_sem=line_send.at[other], recv_sem=line_recv.at[source], device_id=(row, source), device_id_type=MESH
        )

    me = 2 * half + core

    def to_side(other):
        return pltpu.make_async_remote_copy(
            src_ref=around.at[me], dst_ref=around.at[me], send_sem=side_send.at[other], recv_sem=side_recv.at[me], device_id=(same_side(other), col), device_id_type=MESH
        )

    def from_side(other):
        source = 2 * lax.rem(half + lax.div(other, 2), 2) + lax.rem(core + other, 2)
        return pltpu.make_async_remote_copy(
            src_ref=around.at[source], dst_ref=around.at[source], send_sem=side_send.at[other], recv_sem=side_recv.at[source], device_id=(same_side(other), col), device_id_type=MESH
        )

    def to_beside():
        return pltpu.make_async_remote_copy(
            src_ref=facing.at[0], dst_ref=facing.at[1], send_sem=facing_sem.at[0], recv_sem=facing_sem.at[1], device_id=beside, device_id_type=MESH
        )

    def iterate(step, carry):
        total[...] = jnp.zeros_like(total)
        pltpu.make_async_copy(factor, land.at[own_chunk, core], local_sem).wait()

        def chunk_of(index):
            return 2 * nearest(col, n_col, lax.div(index, 2)) + half + lax.rem(index, 2) * (1 - 2 * half)

        def one(index, carry):
            chunk = chunk_of(jnp.where(index >= 4, jnp.minimum(index, chunks - 1) - 1, jnp.where((index == 1) | (index == 2), 1, 0)))

            def pass_on(event):
                @pl.when((event >= 0) & (event < (n_col - 2) * PIECES))
                def _():
                    piece = lax.rem(event, PIECES)
                    relay(2 + lax.div(event, PIECES), piece, piece + 1)

            first = jnp.where(index < 4, 2 * index - 3, 2 * index - 4)
            pass_on(first)

            @pl.when(index == chunks - 1)
            def _():
                pass_on(first + 1)

            @pl.when(index == 0)
            def _():
                paired(own_chunk)
                convert(step, own_chunk, 0)

            @pl.when(index == 1)
            def _():
                turn()
                relay(1, 0, PIECES)
                cross(chunk, 0, LAST)
                paired(chunk)
                convert(step, chunk, 1)
                paired(chunk_of(2))
                convert(step, chunk_of(2), 2)

            @pl.when(index == 2)
            def _():
                lent(step).wait_recv()
                take(held[step], 0)

            @pl.when(index == 3)
            def _():
                cross(chunk_of(3), 0, PIECES // 2)

            @pl.when(index == 4)
            def _():
                cross(chunk, PIECES // 2, LAST)

            @pl.when(index == 6)
            def _():
                cross(chunk, LAST - 1, LAST)

            @pl.when((index >= 4) & (index < chunks))
            def _():
                paired(chunk)
                convert(step, chunk, 1)

            @pl.when(index == chunks - 1)
            def _():
                cross(chunk_of(index), LAST - 2, LAST)
                paired(chunk_of(index))
                convert(step, chunk_of(index), 2)

            @pl.when(index == chunks)
            def _():
                for piece in range(PIECES):
                    give(piece).start()
                settle(step)

            @pl.when(lax.rem(index, 3) == 0)
            def _():
                @pl.when(index < 4)
                def _():
                    alone(jnp.where(index == 0, 1, 0), own_chunk, 0)

            @pl.when((index == 1) | (index == 2) | (index >= 4))
            def _():
                def between():
                    @pl.when(index != chunks - 1)
                    def _():
                        pass_on(first + 1)

                    @pl.when(index == 5)
                    def _():
                        cross(chunk_of(5), 0, LAST - 1)

                    @pl.when(index == 6)
                    def _():
                        cross(chunk_of(7), 0, LAST - 2)

                late = index >= chunks - 1
                which = jnp.where((index == 1) | (index == chunks), 1, 0)
                other = jnp.where((index == 2) | (index == chunks - 1), 0, 1)
                second = jnp.where(index < 4, 2, jnp.where(late, chunks - 1, index - 1))
                contract((which, chunk, 1), (other, chunk_of(second), jnp.where((index < 4) | late, 2, 1)), between)

            return carry

        lax.fori_loop(0, chunks + 1, one, 0)
        @pl.when(step == 0)
        def _():
            pl.semaphore_wait(credit, 3 + jnp.minimum(col, 1) + jnp.minimum(n_col - 1 - col, 1))

        def weigh(index, energy):
            return energy + chol_ref[index] * total[1, index] + held[0, index] * total[0, index]

        def tally():
            energy = lax.fori_loop(0, occupied, weigh, jnp.zeros((virtuals, width), jnp.float32), unroll=4)
            folded = energy[:, :LANES]
            for index in range(1, width // LANES):
                folded += energy[:, index * LANES : (index + 1) * LANES]
            mine[step] = folded

        @pl.when(step == ITERS - 1)
        def _():
            tally()
            along[col] = mine[...]
            for other in range(1, n_col):
                to_line(other).start()

        for piece in range(PIECES):
            if piece == PIECES // 3:

                @pl.when(step == ITERS - 1)
                def _():
                    for other in range(1, n_col):
                        from_line(other).wait_recv()
                    around[me] = sum(along[index] for index in range(n_col))
                    for other in range(1, n_row // 2):
                        to_side(other).start()

            if piece == 2 * PIECES // 3:

                @pl.when(step == ITERS - 1)
                def _():
                    for other in range(1, n_row // 2):
                        from_side(other).wait_recv()
                    facing[0] = sum(around[index] for index in range(n_row // 2))
                    to_beside().start()

            give(piece).wait_recv()
            at = slice(piece * part, (piece + 1) * part)
            value = total[1, at] + back[at]

            @pl.when(step == 0)
            def _():
                fresh_rows = chol_ref[at] + value
                factor[at] = fresh_rows
                publish(factor, 1, piece)
                take(fresh_rows, size + piece * part * virtuals)

            @pl.when(step == ITERS - 1)
            def _():
                out_ref[:, at, :] = jnp.transpose(value, (1, 0, 2))

        gave().wait_send()

        @pl.when(step == 0)
        def _():
            tally()

        return carry

    lax.fori_loop(0, ITERS, iterate, 0)
    to_beside().wait_recv()
    both = facing[0] + facing[1]
    for step in range(ITERS):
        energy_ref[step] = jnp.sum(both[step]) / scale
    to_beside().wait_send()
    for other in range(1, n_col):
        to_line(other).wait_send()
    for other in range(1, n_row // 2):
        to_side(other).wait_send()


def fused(chol, eps_occ, eps_vir):
    n_col = lax.axis_size("col")
    n_row = lax.axis_size("row")
    shard, width = chol.shape
    occupied = eps_occ.shape[0]
    virtuals = shard // occupied
    size, span = shard, 2 * shard
    shape = (occupied, virtuals, width)
    dma = pltpu.SemaphoreType.DMA
    work, energies = pl.pallas_call(
        functools.partial(fused_kernel, n_col),
        out_shape=(pltpu.VMEM((virtuals, occupied, width), jnp.float32), jax.ShapeDtypeStruct((ITERS,), jnp.float32)),
        in_specs=[pl.BlockSpec(memory_space=pl.ANY), pl.BlockSpec(memory_space=pltpu.SMEM), pl.BlockSpec(memory_space=pltpu.SMEM)],
        out_specs=(pl.BlockSpec(memory_space=pltpu.VMEM), pl.BlockSpec(memory_space=pltpu.SMEM)),
        scratch_shapes=[
            pltpu.VMEM((virtuals, occupied, width), jnp.float32),
            pltpu.VMEM(shape, jnp.float32),
            pltpu.VMEM((2 * n_col, 2, occupied, virtuals, width), jnp.float32),
            pltpu.VMEM((ITERS,) + shape, jnp.float32),
            pltpu.VMEM(shape, jnp.float32),
            pltpu.VMEM(shape, jnp.float32),
            pltpu.VMEM((2 * size, 2 * width), jnp.bfloat16),
            pltpu.VMEM((3, span, 2 * width), jnp.bfloat16),
            pltpu.VMEM((2 * n_col, span, 2 * width), jnp.bfloat16),
            pltpu.VMEM((size, span), jnp.float32),
            pltpu.VMEM((size, span), jnp.float32),
            pltpu.VMEM((size, span), jnp.bfloat16),
            pltpu.VMEM((size, span), jnp.bfloat16),
            pltpu.VMEM((size, span), jnp.bfloat16),
            pltpu.VMEM((size, span), jnp.bfloat16),
            pltpu.VMEM((2,) + shape, jnp.float32),
            pltpu.VMEM((2, occupied, virtuals, LANES), jnp.float32),
            pltpu.VMEM((2 * n_col, 2 * occupied * virtuals // LANES, LANES), jnp.float32),
            pltpu.VMEM((ITERS, virtuals, LANES), jnp.float32),
            pltpu.VMEM((n_row // 2, ITERS, virtuals, LANES), jnp.float32),
            pltpu.VMEM((n_col, ITERS, virtuals, LANES), jnp.float32),
            pltpu.VMEM((2, ITERS, virtuals, LANES), jnp.float32),
            dma(()),
            dma((2 * n_col, 4)),
            dma((2 * n_col, PIECES)),
            dma(()),
            dma(()),
            dma(()),
            dma((PIECES,)),
            dma((n_row // 2,)),
            dma((n_row // 2,)),
            dma((n_col,)),
            dma((n_col,)),
            dma((2,)),
            dma(()),
            dma((2 * n_col,)),
            pltpu.SemaphoreType.REGULAR,
        ],
        compiler_params=pltpu.CompilerParams(collective_id=0, has_side_effects=True, vmem_limit_bytes=60 * 1000 * 1000),
    )(chol.reshape(virtuals, occupied, width), eps_occ, eps_vir)
    return work.reshape(shard, width), energies


def shards(chol, eps_occ, eps_vir):
    if lax.axis_size("row") == 8 and chol.shape[0] == 8 * eps_occ.shape[0] and eps_occ.shape[0] % 48 == 0:
        return fused(chol, eps_occ, eps_vir)
    n_row = lax.axis_size("row")
    n_col = lax.axis_size("col")
    row_index = lax.axis_index("row")
    col_index = lax.axis_index("col")
    shard, width = chol.shape
    occupied = eps_occ.shape[0]
    virtual = eps_vir.shape[0]
    shard_virtuals = shard // occupied
    block_virtuals = n_col * shard_virtuals
    total = virtual * occupied
    scale = jnp.float32(total)
    row_vir = lax.dynamic_slice_in_dim(eps_vir, row_index * block_virtuals, block_virtuals, 0)
    col_vir = lax.dynamic_slice_in_dim(
        eps_vir.reshape(n_row, block_virtuals), col_index * shard_virtuals, shard_virtuals, 1
    ).reshape(n_row * shard_virtuals)
    rpair = scale * (row_vir[None, :] - eps_occ[:, None])
    rpair = jnp.broadcast_to(rpair[:, :, None], (occupied, block_virtuals, LANES))
    cpair = (scale * (col_vir[None, :] - eps_occ[:, None])).reshape(-1, LANES)
    chol_t = jnp.transpose(chol.reshape(shard_virtuals, occupied, width), (1, 0, 2))
    chol_cols = gather(chol_t, "row")
    factor = chol_t
    sums = []
    for step in range(ITERS):
        if shard_virtuals % 8:
            rows = gather(factor, "col")
            turn = jnp.zeros((1,), jnp.int32)
        else:
            rows = passed(factor, "col")
            turn = jnp.full((1,), n_col - col_index, jnp.int32)
        cols = chol_cols if step == 0 else gather(factor, "row")
        partial_value = update(turn, rows, cols, chol_cols, rpair, cpair)
        if shard_virtuals % 8:
            partial_value = jnp.transpose(
                partial_value.reshape(occupied, n_col, shard_virtuals, width), (1, 0, 2, 3)
            )
        work = lax.psum_scatter(partial_value, "col", scatter_dimension=0, tiled=False)
        factor = chol_t + work
        sums.append(jnp.sum(chol_t * work))
    energies = lax.psum(jnp.stack(sums), ("row", "col"))
    return jnp.transpose(work, (1, 0, 2)).reshape(shard, width), energies / scale


def solution(mesh):
    placed = (P(("row", "col"), None), P(), P())
    return jax.shard_map(
        shards,
        mesh=mesh,
        in_specs=placed,
        out_specs=(P(("row", "col"), None), P()),
        check_vma=False,
    )
```

```python
import functools

import jax
import jax.numpy as jnp
from jax import lax
from jax.experimental import pallas as pl
from jax.experimental.pallas import tpu as pltpu
from jax.sharding import PartitionSpec as P

ITERS = 2
LANES = 128
NT = (((1,), (1,)), ((), ()))


def split(x):
    high = x.astype(jnp.bfloat16)
    low = (x - high.astype(jnp.float32)).astype(jnp.bfloat16)
    return high, low


def flat(ref, index, turn=None):
    parts = range(ref.shape[0])
    pieces = [ref[part if turn is None else (part + turn) % len(parts), index] for part in parts]
    return pieces[0] if len(pieces) == 1 else jnp.concatenate(pieces, axis=0)


def kernel(steps, turn_ref, rows_ref, cols_ref, chol_ref, rpair_ref, cpair_ref, out_ref, rows, cols, chol, direct, high_tile, low_tile):
    step = pl.program_id(0)
    parts, occupied, shard_virtuals, width = rows_ref.shape
    height = parts * shard_virtuals
    block = occupied // steps
    breadth = cols_ref.shape[0] * cols_ref.shape[2]
    span = block * breadth
    group = LANES // breadth

    @pl.when(step == 0)
    def _():
        def one(index, carry):
            high, low = split(flat(rows_ref, index, turn_ref[0]))
            at = pl.ds(pl.multiple_of(index * height, height), height)
            rows[at, :width] = high
            rows[at, width:] = low
            return carry

        lax.fori_loop(0, occupied, one, 0)

    @pl.when(step < steps)
    def _():
        for index in range(block):
            high, low = split(flat(cols_ref, index))
            cols[index * breadth : (index + 1) * breadth, :width] = low
            cols[index * breadth : (index + 1) * breadth, width:] = high
            high, low = split(flat(chol_ref, index))
            at = pl.ds(pl.multiple_of(step * span + index * breadth, breadth), breadth)
            chol[at, :width] = high
            chol[at, width:] = low

        def one(index, carry):
            at = pl.ds(pl.multiple_of(index * block * height, block * height), block * height)
            value = lax.dot_general(rows[at, :], cols[...], NT, preferred_element_type=jnp.float32)
            value += lax.dot_general(rows[at, :width], cols[:, width:], NT, preferred_element_type=jnp.float32)
            direct[at, pl.ds(pl.multiple_of(step * span, span), span)] = value
            return carry

        lax.fori_loop(0, steps, one, 0)

    @pl.when(step >= steps)
    def _():
        first = (step - steps) * block
        lane = lax.broadcasted_iota(jnp.int32, (height, LANES), 1) // breadth

        def one(index, carry):
            lead = first + index * group
            columns = pl.ds(pl.multiple_of(lead * breadth, LANES), LANES)
            bottoms = [rpair_ref[lead + own] for own in range(group)]
            for other in range(occupied // group):
                swapped = [direct[pl.ds((other * group + m) * height, height), columns] for m in range(group)]
                to = slice(other * LANES, (other + 1) * LANES)
                tops = cpair_ref[other : other + 1, :]
                for own in range(group):
                    exchange = swapped[0] if own == 0 else pltpu.roll(swapped[0], (LANES - own * breadth) % LANES, 1)
                    for m in range(1, group):
                        shift = ((m - own) * breadth) % LANES
                        moved = pltpu.roll(swapped[m], shift, 1) if shift else swapped[m]
                        exchange = jnp.where(lane == m, moved, exchange)
                    at = pl.ds(pl.multiple_of((lead + own) * height, height), height)
                    value = (exchange - 2.0 * direct[at, to]) / (bottoms[own] + tops)
                    high, low = split(value)
                    put = pl.ds(pl.multiple_of((index * group + own) * height, height), height)
                    high_tile[put, to] = high
                    low_tile[put, to] = low
            return carry

        lax.fori_loop(0, block // group, one, 0)
        both = jnp.dot(high_tile[...], chol[...], preferred_element_type=jnp.float32)
        value = both[:, :width] + both[:, width:]
        value += jnp.dot(low_tile[...], chol[:, :width], preferred_element_type=jnp.float32)
        value = value.reshape(block, parts, shard_virtuals, width)
        for part in range(parts):
            out_ref[part] = value[:, part]


def update(turn, rows, cols, chol, rpair, cpair):
    parts, occupied, shard_virtuals, width = rows.shape
    height = parts * shard_virtuals
    breadth = cols.shape[0] * cols.shape[2]
    steps = 6
    block = occupied // steps
    pair_columns = occupied * breadth
    column_block = (cols.shape[0], block, cols.shape[2], width)

    def of_columns(step):
        return (0, jnp.minimum(step, steps - 1), 0, 0)

    return pl.pallas_call(
        functools.partial(kernel, steps),
        grid=(2 * steps,),
        out_shape=jax.ShapeDtypeStruct(rows.shape, jnp.float32),
        in_specs=[
            pl.BlockSpec(memory_space=pltpu.SMEM),
            pl.BlockSpec(rows.shape, lambda step: (0, 0, 0, 0)),
            pl.BlockSpec(column_block, of_columns),
            pl.BlockSpec(column_block, of_columns),
            pl.BlockSpec(rpair.shape, lambda step: (0, 0, 0)),
            pl.BlockSpec(cpair.shape, lambda step: (0, 0)),
        ],
        out_specs=pl.BlockSpec((parts, block, shard_virtuals, width), lambda step: (0, jnp.maximum(step - steps, 0), 0, 0)),
        scratch_shapes=[
            pltpu.VMEM((occupied * height, 2 * width), jnp.bfloat16),
            pltpu.VMEM((block * breadth, 2 * width), jnp.bfloat16),
            pltpu.VMEM((pair_columns, 2 * width), jnp.bfloat16),
            pltpu.VMEM((occupied * height, pair_columns), jnp.float32),
            pltpu.VMEM((block * height, pair_columns), jnp.bfloat16),
            pltpu.VMEM((block * height, pair_columns), jnp.bfloat16),
        ],
        compiler_params=pltpu.CompilerParams(
            dimension_semantics=("arbitrary",), vmem_limit_bytes=66 * 1000 * 1000
        ),
        cost_estimate=pl.CostEstimate(
            flops=12 * occupied * height * pair_columns * width, bytes_accessed=4 * width * (2 * occupied * height + 2 * pair_columns), transcendentals=0
        ),
    )(turn, rows, cols, chol, rpair, cpair)


def gather(x, axis):
    parts = lax.all_gather(x, axis, axis=0)
    if x.shape[1] % 8:
        parts = jnp.transpose(parts, (1, 0, 2, 3)).reshape(1, x.shape[0], -1, x.shape[2])
    return parts


def passed(x, axis):
    n = lax.axis_size(axis)
    blocks = [x]
    for k in range(1, n):
        blocks.append(lax.ppermute(x, axis, [(j, (j - k) % n) for j in range(n)]))
    return jnp.stack(blocks)


PIECES = 6
LAST = PIECES - 1
CORE, ACROSS, UP, DOWN = 0, 1, 2, 3
MESH = pl.DeviceIdType.MESH


def place():
    row = lax.axis_index("row")
    core = lax.rem(row, 2)
    side = lax.rem(lax.div(row, 2), 2)
    half = lax.div(row, 4)
    return row, half, side, core, lax.axis_index("col")


def nearest(col, n_col, order):
    near = jnp.minimum(col, n_col - 1 - col)
    far = order - near
    away = jnp.where(col < n_col - 1 - col, far, -far)
    turn = lax.div(order + 1, 2) * (2 * lax.rem(order, 2) - 1)
    return col + jnp.where(order <= 2 * near, turn, away)


def fused_kernel(
    n_col, given_ref, occ_ref, vir_ref, out_ref, energy_ref, given, chol_ref, land, held, back, factor, rows, fresh, kept, direct, other_direct, high_tile, other_high, low_tile, other_low, total, bottoms, tops,
    mine, around, along, facing, local_sem, send_sem, recv_sem, held_send, held_recv, back_send, back_recv, side_send, side_recv, line_send, line_recv, facing_sem, given_sem, pair_recv, credit,
):
    row, half, side, core, col = place()
    n_row = 8
    bring = pltpu.make_async_copy(given_ref, given, given_sem)
    bring.start()
    occupied, width = chol_ref.shape[0], chol_ref.shape[2]
    virtuals = chol_ref.shape[1]
    size = occupied * virtuals
    span = occupied * 2 * virtuals
    part = occupied // PIECES
    chunks = 2 * n_col
    group = LANES // (2 * virtuals)
    blocks = occupied // group
    tall = group * virtuals
    partner = (row + 1 - 2 * core, col)
    beside = (row + 2 - 4 * side, col)
    across = (row + 4 - 8 * half, col)
    above = (row, col + 1)
    below = (row, col - 1)
    own_chunk = 2 * col + half

    def slot(chunk, owner, piece):
        return land.at[chunk, owner, pl.ds(piece * part, part), :, :]

    def move(source, chunk, target, piece, device):
        return pltpu.make_async_remote_copy(
            src_ref=source,
            dst_ref=slot(chunk, core, piece),
            send_sem=send_sem.at[chunk, target],
            recv_sem=pair_recv.at[chunk] if target == CORE else recv_sem.at[chunk, piece],
            device_id=device,
            device_id_type=MESH,
        )

    def landed(chunk, piece):
        pltpu.make_async_remote_copy(
            src_ref=slot(chunk, core, piece),
            dst_ref=slot(chunk, core, piece),
            send_sem=send_sem.at[chunk, CORE],
            recv_sem=recv_sem.at[chunk, piece],
            device_id=partner,
            device_id_type=MESH,
        ).wait_recv()

    def paired(chunk):
        pltpu.make_async_remote_copy(
            src_ref=land.at[chunk, 1 - core],
            dst_ref=land.at[chunk, 1 - core],
            send_sem=send_sem.at[chunk, CORE],
            recv_sem=pair_recv.at[chunk],
            device_id=partner,
            device_id_type=MESH,
        ).wait_recv()

    def sent(ref, chunk, target, device):
        pltpu.make_async_remote_copy(
            src_ref=ref, dst_ref=ref, send_sem=send_sem.at[chunk, target], recv_sem=pair_recv.at[chunk], device_id=device, device_id_type=MESH
        ).wait_send()

    def pieces_of(ref, piece):
        return ref.at[pl.ds(piece * part, part), :, :]

    def lend(source, step, piece):
        return pltpu.make_async_remote_copy(
            src_ref=pieces_of(source, piece), dst_ref=pieces_of(held.at[step], piece), send_sem=held_send, recv_sem=held_recv, device_id=beside, device_id_type=MESH
        )

    def lent(step):
        return pltpu.make_async_remote_copy(
            src_ref=factor, dst_ref=held.at[step], send_sem=held_send, recv_sem=held_recv, device_id=beside, device_id_type=MESH
        )

    def gave():
        return pltpu.make_async_remote_copy(
            src_ref=total.at[0], dst_ref=back, send_sem=back_send, recv_sem=back_recv.at[0], device_id=beside, device_id_type=MESH
        )

    def give(piece):
        return pltpu.make_async_remote_copy(
            src_ref=pieces_of(total.at[0], piece), dst_ref=pieces_of(back, piece), send_sem=back_send, recv_sem=back_recv.at[piece], device_id=beside, device_id_type=MESH
        )

    def stay(source, piece):
        return pltpu.make_async_copy(pieces_of(source, piece), slot(own_chunk, core, piece), local_sem)

    def take(value, start):
        high, low = split(value.reshape(-1, width))
        at = slice(start, start + high.shape[0])
        rows[at, :width] = low
        rows[at, width:] = high

    def offer(source, piece):
        move(pieces_of(source, piece), own_chunk, ACROSS, piece, across).start()

    def publish(source, step, piece):
        @pl.when(col < n_col - 1)
        def _():
            move(pieces_of(source, piece), own_chunk, UP, piece, above).start()

        @pl.when(col > 0)
        def _():
            move(pieces_of(source, piece), own_chunk, DOWN, piece, below).start()

        lend(source, step, piece).start()
        move(pieces_of(source, piece), own_chunk, CORE, piece, partner).start()
        stay(source, piece).start()

    def relay(distance, first, last):
        def of(position, target, device, more):
            near = 2 * position + half
            away = near + 1 - 2 * half

            def one(order, carry):
                piece = lax.rem(order + 1, PIECES)
                landed(near, piece)

                @pl.when(more)
                def _():
                    move(slot(near, core, piece), near, target, piece, device).start()

                @pl.when(piece > 0)
                def _():
                    move(slot(near, core, piece), near, ACROSS, piece, across).start()

                @pl.when(piece == 0)
                def _():
                    landed(away, piece)

                    @pl.when(more)
                    def _():
                        move(slot(away, core, piece), away, target, piece, device).start()

                    move(slot(away, core, piece), away, CORE, piece, partner).start()

                move(slot(near, core, piece), near, CORE, piece, partner).start()
                return carry

            lax.fori_loop(first, last, one, 0)

        @pl.when(col + distance < n_col)
        def _():
            of(col + distance, DOWN, below, col > 0)

        @pl.when(col >= distance)
        def _():
            of(col - distance, UP, above, col < n_col - 1)

    def turn():
        chunk = own_chunk + 1 - 2 * half
        landed(chunk, 0)

        @pl.when(col < n_col - 1)
        def _():
            move(slot(chunk, core, 0), chunk, UP, 0, above).start()

        @pl.when(col > 0)
        def _():
            move(slot(chunk, core, 0), chunk, DOWN, 0, below).start()

        move(slot(chunk, core, 0), chunk, CORE, 0, partner).start()

    def cross(chunk, first, last):
        def one(order, carry):
            piece = order + 1
            landed(chunk, piece)
            move(slot(chunk, core, piece), chunk, CORE, piece, partner).start()
            return carry

        lax.fori_loop(first, last, one, 0)

    def settle(step):
        def one(position, carry):
            near = 2 * position + half
            away = near + 1 - 2 * half
            sent(land.at[near, core], near, CORE, partner)
            sent(land.at[away, core], away, CORE, partner)

            @pl.when(position == col)
            def _():
                sent(land.at[near, core], near, ACROSS, across)

            @pl.when(position != col)
            def _():
                sent(land.at[near, core, pl.ds(part, occupied - part), :, :], near, ACROSS, across)

            @pl.when((position >= col) & (col > 0))
            def _():
                sent(land.at[near, core], near, DOWN, below)
                sent(slot(away, core, 0), away, DOWN, below)

            @pl.when((position <= col) & (col < n_col - 1))
            def _():
                sent(land.at[near, core], near, UP, above)
                sent(slot(away, core, 0), away, UP, above)

            return carry

        lax.fori_loop(0, n_col, one, 0)
        lent(0).wait_send()

        @pl.when(step == 0)
        def _():
            def thank(device):
                pl.semaphore_signal(credit, inc=1, device_id=device, device_id_type=MESH)

            thank(partner)
            thank(beside)
            thank(across)

            @pl.when(col < n_col - 1)
            def _():
                thank(above)

            @pl.when(col > 0)
            def _():
                thank(below)

    barrier = pltpu.get_barrier_semaphore()

    def same_side(other):
        return lax.rem(half + lax.div(other, 2), 2) * 4 + side * 2 + lax.rem(core + other, 2)

    def greet(device):
        pl.semaphore_signal(barrier, inc=1, device_id=device, device_id_type=MESH)

    greet(beside)
    for other in range(1, n_row // 2):
        greet((same_side(other), col))
    for other in range(1, n_col):
        greet((row, lax.rem(col + other, n_col)))
    bring.wait()
    for piece in range(PIECES):
        at = slice(piece * part, (piece + 1) * part)
        chol_ref[at] = jnp.transpose(given[:, at, :], (1, 0, 2))
    pl.semaphore_wait(barrier, n_row // 2 + n_col - 1)

    offer(chol_ref, 0)
    for order in range(PIECES):
        piece = (order + 1) % PIECES
        publish(chol_ref, 0, piece)
        if piece:
            offer(chol_ref, piece)
    take(chol_ref[...], size)

    scale = jnp.float32(occupied * virtuals * n_row * n_col)
    vertical = lax.broadcasted_iota(jnp.int32, (virtuals, LANES), 0)
    lateral = lax.broadcasted_iota(jnp.int32, (1, LANES), 1)

    for which in range(2):
        first = ((row + (1 - which) * (2 - 4 * side)) * n_col + col) * virtuals
        level = jnp.zeros((virtuals, LANES), jnp.float32)
        for index in range(virtuals):
            level = jnp.where(vertical == index, vir_ref[first + index], level)

        def lower(index, carry):
            bottoms[which, index] = scale * (level - occ_ref[index])
            return carry

        lax.fori_loop(0, occupied, lower, 0)

    def raised(chunk, carry):
        position, other = lax.div(chunk, 2), lax.rem(chunk, 2)
        level = jnp.zeros((1, LANES), jnp.float32)
        for index in range(2 * virtuals):
            source = (4 * other + 2 * side + index // virtuals) * n_col + position
            level = jnp.where(lax.rem(lateral, 2 * virtuals) == index, vir_ref[source * virtuals + index % virtuals], level)
        for block in range(blocks):
            deep = jnp.zeros((1, LANES), jnp.float32)
            for index in range(group):
                deep = jnp.where(lax.div(lateral, 2 * virtuals) == index, occ_ref[block * group + index], deep)
            tops[chunk, block : block + 1, :] = scale * (level - deep)
        return carry

    lax.fori_loop(0, chunks, raised, 0)

    def convert(step, chunk, place):
        def one(index, carry):
            high, low = split(jnp.concatenate([land[chunk, 0, index], land[chunk, 1, index]], axis=0))
            at = pl.ds(pl.multiple_of(index * 2 * virtuals, 2 * virtuals), 2 * virtuals)
            fresh[place, at, :width] = high
            fresh[place, at, width:] = low

            @pl.when(step == 0)
            def _():
                kept[chunk, at, :width] = high
                kept[chunk, at, width:] = low

            return carry

        lax.fori_loop(0, occupied, one, 0, unroll=8)

    lane = lax.broadcasted_iota(jnp.int32, (virtuals, LANES), 1) // (2 * virtuals)

    products = (direct, other_direct)
    highs, lows = (high_tile, other_high), (low_tile, other_low)

    def product(which, place, part, start, count):
        at = pl.ds(pl.multiple_of(start, LANES), count)
        whose = pl.ds(pl.multiple_of(which * size, size), size)
        value = lax.dot_general(rows[whose, :], fresh[place, at, :], NT, preferred_element_type=jnp.float32)
        value += lax.dot_general(rows[whose, width:], fresh[place, at, :width], NT, preferred_element_type=jnp.float32)
        products[part][:, at] = value

    def amplitude(which, chunk, part, first, second):
        at = pl.ds(pl.multiple_of(first * tall, tall), tall)
        to = slice(second * LANES, (second + 1) * LANES)
        plain = products[part][at, to]
        turned = products[part][second * tall : (second + 1) * tall, pl.ds(pl.multiple_of(first * LANES, LANES), LANES)]
        skew = [turned[(-m) % group * virtuals : ((-m) % group + 1) * virtuals] for m in range(group)]
        skew = [pltpu.roll(value, (-m) % group * 2 * virtuals, 1) if m else value for m, value in enumerate(skew)]
        stride = 1
        while stride < group:
            upper = (lane & stride) != 0
            skew = [jnp.where(upper, skew[(m - stride) % group], skew[m]) for m in range(group)]
            stride *= 2
        top = tops[chunk, second : second + 1, :]
        values = []
        for m in range(group):
            exchange = pltpu.roll(skew[m], LANES - m * 2 * virtuals, 1) if m else skew[m]
            bottom = bottoms[which, first * group + m]
            values.append((exchange - 2.0 * plain[m * virtuals : (m + 1) * virtuals]) / (bottom + top))
        high, low = split(jnp.concatenate(values, axis=0))
        highs[part][at, to] = high
        lows[part][at, to] = low

    def collect(chunk, part, start, count):
        at = pl.ds(pl.multiple_of(start, tall), count)
        both = jnp.dot(highs[part][at, :], kept[chunk], preferred_element_type=jnp.float32)
        value = both[:, :width] + both[:, width:]
        value += jnp.dot(lows[part][at, :], kept[chunk, :, :width], preferred_element_type=jnp.float32)
        return value.reshape(count // virtuals, virtuals, width)

    cuts = span // (2 * LANES)

    def alone(which, chunk, place):
        product(which, place, 0, 0, span)

        def rate(index, carry):
            for block in range(2 * blocks):
                amplitude(which, chunk, 0, index * 2 + block // blocks, block % blocks)
            return carry

        lax.fori_loop(0, blocks // 2, rate, 0)
        total[which] += collect(chunk, 0, 0, size)

    def contract(one, two, after, between):
        (which, chunk, place), (other, second_chunk, second_place) = one, two
        product(which, place, 0, 0, span)
        after()

        def begin(index, carry):
            for block in range(blocks * blocks // cuts):
                amplitude(which, chunk, 0, index * (blocks // cuts) + block // blocks, block % blocks)
            product(other, second_place, 1, index * 2 * LANES, 2 * LANES)
            return carry

        lax.fori_loop(0, cuts, begin, 0)
        between()

        def finish(index, carry):
            for block in range(blocks * blocks // 2):
                amplitude(other, second_chunk, 1, index * (blocks // 2) + block // blocks, block % blocks)
            at = pl.ds(index * (occupied // 2), occupied // 2)
            total[which, at] += collect(chunk, 0, index * (size // 2), size // 2)

            return carry

        lax.fori_loop(0, 2, finish, 0)
        total[other] += collect(second_chunk, 1, 0, size)

    def to_line(other):
        return pltpu.make_async_remote_copy(
            src_ref=mine, dst_ref=along.at[col], send_sem=line_send.at[other], recv_sem=line_recv.at[col], device_id=(row, lax.rem(col + other, n_col)), device_id_type=MESH
        )

    def from_line(other):
        source = lax.rem(col + other, n_col)
        return pltpu.make_async_remote_copy(
            src_ref=mine, dst_ref=along.at[source], send_sem=line_send.at[other], recv_sem=line_recv.at[source], device_id=(row, source), device_id_type=MESH
        )

    me = 2 * half + core

    def to_side(other):
        return pltpu.make_async_remote_copy(
            src_ref=around.at[me], dst_ref=around.at[me], send_sem=side_send.at[other], recv_sem=side_recv.at[me], device_id=(same_side(other), col), device_id_type=MESH
        )

    def from_side(other):
        source = 2 * lax.rem(half + lax.div(other, 2), 2) + lax.rem(core + other, 2)
        return pltpu.make_async_remote_copy(
            src_ref=around.at[source], dst_ref=around.at[source], send_sem=side_send.at[other], recv_sem=side_recv.at[source], device_id=(same_side(other), col), device_id_type=MESH
        )

    def to_beside():
        return pltpu.make_async_remote_copy(
            src_ref=facing.at[0], dst_ref=facing.at[1], send_sem=facing_sem.at[0], recv_sem=facing_sem.at[1], device_id=beside, device_id_type=MESH
        )

    def iterate(step, carry):
        total[...] = jnp.zeros_like(total)
        pltpu.make_async_copy(factor, land.at[own_chunk, core], local_sem).wait()

        def chunk_of(index):
            return 2 * nearest(col, n_col, lax.div(index, 2)) + half + lax.rem(index, 2) * (1 - 2 * half)

        def one(index, carry):
            chunk = chunk_of(jnp.where(index >= 4, jnp.minimum(index, chunks - 1) - 1, jnp.where((index == 1) | (index == 2), 1, 0)))

            def pass_on(event):
                @pl.when((event >= 0) & (event < (n_col - 2) * PIECES))
                def _():
                    piece = lax.rem(event, PIECES)
                    relay(2 + lax.div(event, PIECES), piece, piece + 1)

            first = jnp.where(index < 4, 2 * index - 3, 2 * index - 4)
            pass_on(first)

            @pl.when(index == chunks - 1)
            def _():
                pass_on(first + 1)

            @pl.when(index == 0)
            def _():
                paired(own_chunk)
                convert(step, own_chunk, 0)

            @pl.when(index == 1)
            def _():
                turn()
                relay(1, 0, PIECES)
                cross(chunk, 0, LAST)
                paired(chunk)
                convert(step, chunk, 1)
                paired(chunk_of(2))
                convert(step, chunk_of(2), 2)

            @pl.when(index == 2)
            def _():
                lent(step).wait_recv()
                take(held[step], 0)

            @pl.when(index == 3)
            def _():
                cross(chunk_of(3), 0, PIECES // 2)

            @pl.when(index == 4)
            def _():
                cross(chunk, PIECES // 2, LAST)

            @pl.when(index == 6)
            def _():
                cross(chunk, LAST - 1, LAST)

            @pl.when((index >= 4) & (index < chunks))
            def _():
                paired(chunk)
                convert(step, chunk, 1)

            @pl.when(index == chunks)
            def _():
                for piece in range(PIECES):
                    give(piece).start()
                settle(step)

            @pl.when(lax.rem(index, 3) == 0)
            def _():
                @pl.when(index < 4)
                def _():
                    alone(jnp.where(index == 0, 1, 0), own_chunk, 0)

            @pl.when((index == 1) | (index == 2) | (index >= 4))
            def _():
                def between():
                    @pl.when(index != chunks - 1)
                    def _():
                        pass_on(first + 1)

                    @pl.when(index == 5)
                    def _():
                        cross(chunk_of(5), 0, LAST - 1)

                    @pl.when(index == 6)
                    def _():
                        cross(chunk_of(7), 0, LAST - 2)

                def after():
                    @pl.when(index == chunks - 1)
                    def _():
                        cross(chunk_of(7), LAST - 2, LAST)
                        paired(chunk_of(7))
                        convert(step, chunk_of(7), 2)

                late = index >= chunks - 1
                which = jnp.where((index == 1) | (index == chunks), 1, 0)
                other = jnp.where((index == 2) | (index == chunks - 1), 0, 1)
                second = jnp.where(index < 4, 2, jnp.where(late, chunks - 1, index - 1))
                contract((which, chunk, 1), (other, chunk_of(second), jnp.where((index < 4) | late, 2, 1)), after, between)

            return carry

        lax.fori_loop(0, chunks + 1, one, 0)
        @pl.when(step == 0)
        def _():
            pl.semaphore_wait(credit, 3 + jnp.minimum(col, 1) + jnp.minimum(n_col - 1 - col, 1))

        def weigh(index, energy):
            return energy + chol_ref[index] * total[1, index] + held[0, index] * total[0, index]

        def tally():
            energy = lax.fori_loop(0, occupied, weigh, jnp.zeros((virtuals, width), jnp.float32), unroll=4)
            folded = energy[:, :LANES]
            for index in range(1, width // LANES):
                folded += energy[:, index * LANES : (index + 1) * LANES]
            mine[step] = folded

        @pl.when(step == ITERS - 1)
        def _():
            tally()
            along[col] = mine[...]
            for other in range(1, n_col):
                to_line(other).start()

        for piece in range(PIECES):
            if piece == PIECES // 3:

                @pl.when(step == ITERS - 1)
                def _():
                    for other in range(1, n_col):
                        from_line(other).wait_recv()
                    around[me] = sum(along[index] for index in range(n_col))
                    for other in range(1, n_row // 2):
                        to_side(other).start()

            if piece == 2 * PIECES // 3:

                @pl.when(step == ITERS - 1)
                def _():
                    for other in range(1, n_row // 2):
                        from_side(other).wait_recv()
                    facing[0] = sum(around[index] for index in range(n_row // 2))
                    to_beside().start()

            give(piece).wait_recv()
            at = slice(piece * part, (piece + 1) * part)
            value = total[1, at] + back[at]

            @pl.when(step == 0)
            def _():
                fresh_rows = chol_ref[at] + value
                factor[at] = fresh_rows
                publish(factor, 1, piece)
                offer(factor, piece)
                take(fresh_rows, size + piece * part * virtuals)

            @pl.when(step == ITERS - 1)
            def _():
                out_ref[:, at, :] = jnp.transpose(value, (1, 0, 2))

        gave().wait_send()

        @pl.when(step == 0)
        def _():
            tally()

        return carry

    lax.fori_loop(0, ITERS, iterate, 0)
    to_beside().wait_recv()
    both = facing[0] + facing[1]
    for step in range(ITERS):
        energy_ref[step] = jnp.sum(both[step]) / scale
    to_beside().wait_send()
    for other in range(1, n_col):
        to_line(other).wait_send()
    for other in range(1, n_row // 2):
        to_side(other).wait_send()


def fused(chol, eps_occ, eps_vir):
    n_col = lax.axis_size("col")
    n_row = lax.axis_size("row")
    shard, width = chol.shape
    occupied = eps_occ.shape[0]
    virtuals = shard // occupied
    size, span = shard, 2 * shard
    shape = (occupied, virtuals, width)
    dma = pltpu.SemaphoreType.DMA
    work, energies = pl.pallas_call(
        functools.partial(fused_kernel, n_col),
        out_shape=(pltpu.VMEM((virtuals, occupied, width), jnp.float32), jax.ShapeDtypeStruct((ITERS,), jnp.float32)),
        in_specs=[pl.BlockSpec(memory_space=pl.ANY), pl.BlockSpec(memory_space=pltpu.SMEM), pl.BlockSpec(memory_space=pltpu.SMEM)],
        out_specs=(pl.BlockSpec(memory_space=pltpu.VMEM), pl.BlockSpec(memory_space=pltpu.SMEM)),
        scratch_shapes=[
            pltpu.VMEM((virtuals, occupied, width), jnp.float32),
            pltpu.VMEM(shape, jnp.float32),
            pltpu.VMEM((2 * n_col, 2, occupied, virtuals, width), jnp.float32),
            pltpu.VMEM((ITERS,) + shape, jnp.float32),
            pltpu.VMEM(shape, jnp.float32),
            pltpu.VMEM(shape, jnp.float32),
            pltpu.VMEM((2 * size, 2 * width), jnp.bfloat16),
            pltpu.VMEM((3, span, 2 * width), jnp.bfloat16),
            pltpu.VMEM((2 * n_col, span, 2 * width), jnp.bfloat16),
            pltpu.VMEM((size, span), jnp.float32),
            pltpu.VMEM((size, span), jnp.float32),
            pltpu.VMEM((size, span), jnp.bfloat16),
            pltpu.VMEM((size, span), jnp.bfloat16),
            pltpu.VMEM((size, span), jnp.bfloat16),
            pltpu.VMEM((size, span), jnp.bfloat16),
            pltpu.VMEM((2,) + shape, jnp.float32),
            pltpu.VMEM((2, occupied, virtuals, LANES), jnp.float32),
            pltpu.VMEM((2 * n_col, 2 * occupied * virtuals // LANES, LANES), jnp.float32),
            pltpu.VMEM((ITERS, virtuals, LANES), jnp.float32),
            pltpu.VMEM((n_row // 2, ITERS, virtuals, LANES), jnp.float32),
            pltpu.VMEM((n_col, ITERS, virtuals, LANES), jnp.float32),
            pltpu.VMEM((2, ITERS, virtuals, LANES), jnp.float32),
            dma(()),
            dma((2 * n_col, 4)),
            dma((2 * n_col, PIECES)),
            dma(()),
            dma(()),
            dma(()),
            dma((PIECES,)),
            dma((n_row // 2,)),
            dma((n_row // 2,)),
            dma((n_col,)),
            dma((n_col,)),
            dma((2,)),
            dma(()),
            dma((2 * n_col,)),
            pltpu.SemaphoreType.REGULAR,
        ],
        compiler_params=pltpu.CompilerParams(collective_id=0, has_side_effects=True, vmem_limit_bytes=60 * 1000 * 1000),
    )(chol.reshape(virtuals, occupied, width), eps_occ, eps_vir)
    return work.reshape(shard, width), energies


def shards(chol, eps_occ, eps_vir):
    if lax.axis_size("row") == 8 and chol.shape[0] == 8 * eps_occ.shape[0] and eps_occ.shape[0] % 48 == 0:
        return fused(chol, eps_occ, eps_vir)
    n_row = lax.axis_size("row")
    n_col = lax.axis_size("col")
    row_index = lax.axis_index("row")
    col_index = lax.axis_index("col")
    shard, width = chol.shape
    occupied = eps_occ.shape[0]
    virtual = eps_vir.shape[0]
    shard_virtuals = shard // occupied
    block_virtuals = n_col * shard_virtuals
    total = virtual * occupied
    scale = jnp.float32(total)
    row_vir = lax.dynamic_slice_in_dim(eps_vir, row_index * block_virtuals, block_virtuals, 0)
    col_vir = lax.dynamic_slice_in_dim(
        eps_vir.reshape(n_row, block_virtuals), col_index * shard_virtuals, shard_virtuals, 1
    ).reshape(n_row * shard_virtuals)
    rpair = scale * (row_vir[None, :] - eps_occ[:, None])
    rpair = jnp.broadcast_to(rpair[:, :, None], (occupied, block_virtuals, LANES))
    cpair = (scale * (col_vir[None, :] - eps_occ[:, None])).reshape(-1, LANES)
    chol_t = jnp.transpose(chol.reshape(shard_virtuals, occupied, width), (1, 0, 2))
    chol_cols = gather(chol_t, "row")
    factor = chol_t
    sums = []
    for step in range(ITERS):
        if shard_virtuals % 8:
            rows = gather(factor, "col")
            turn = jnp.zeros((1,), jnp.int32)
        else:
            rows = passed(factor, "col")
            turn = jnp.full((1,), n_col - col_index, jnp.int32)
        cols = chol_cols if step == 0 else gather(factor, "row")
        partial_value = update(turn, rows, cols, chol_cols, rpair, cpair)
        if shard_virtuals % 8:
            partial_value = jnp.transpose(
                partial_value.reshape(occupied, n_col, shard_virtuals, width), (1, 0, 2, 3)
            )
        work = lax.psum_scatter(partial_value, "col", scatter_dimension=0, tiled=False)
        factor = chol_t + work
        sums.append(jnp.sum(chol_t * work))
    energies = lax.psum(jnp.stack(sums), ("row", "col"))
    return jnp.transpose(work, (1, 0, 2)).reshape(shard, width), energies / scale


def solution(mesh):
    placed = (P(("row", "col"), None), P(), P())
    return jax.shard_map(
        shards,
        mesh=mesh,
        in_specs=placed,
        out_specs=(P(("row", "col"), None), P()),
        check_vma=False,
    )
```

```python
import functools

import jax
import jax.numpy as jnp
from jax import lax
from jax.experimental import pallas as pl
from jax.experimental.pallas import tpu as pltpu
from jax.sharding import PartitionSpec as P

ITERS = 2
LANES = 128
NT = (((1,), (1,)), ((), ()))


def split(x):
    high = x.astype(jnp.bfloat16)
    low = (x - high.astype(jnp.float32)).astype(jnp.bfloat16)
    return high, low


def flat(ref, index, turn=None):
    parts = range(ref.shape[0])
    pieces = [ref[part if turn is None else (part + turn) % len(parts), index] for part in parts]
    return pieces[0] if len(pieces) == 1 else jnp.concatenate(pieces, axis=0)


def kernel(steps, turn_ref, rows_ref, cols_ref, chol_ref, rpair_ref, cpair_ref, out_ref, rows, cols, chol, direct, high_tile, low_tile):
    step = pl.program_id(0)
    parts, occupied, shard_virtuals, width = rows_ref.shape
    height = parts * shard_virtuals
    block = occupied // steps
    breadth = cols_ref.shape[0] * cols_ref.shape[2]
    span = block * breadth
    group = LANES // breadth

    @pl.when(step == 0)
    def _():
        def one(index, carry):
            high, low = split(flat(rows_ref, index, turn_ref[0]))
            at = pl.ds(pl.multiple_of(index * height, height), height)
            rows[at, :width] = high
            rows[at, width:] = low
            return carry

        lax.fori_loop(0, occupied, one, 0)

    @pl.when(step < steps)
    def _():
        for index in range(block):
            high, low = split(flat(cols_ref, index))
            cols[index * breadth : (index + 1) * breadth, :width] = low
            cols[index * breadth : (index + 1) * breadth, width:] = high
            high, low = split(flat(chol_ref, index))
            at = pl.ds(pl.multiple_of(step * span + index * breadth, breadth), breadth)
            chol[at, :width] = high
            chol[at, width:] = low

        def one(index, carry):
            at = pl.ds(pl.multiple_of(index * block * height, block * height), block * height)
            value = lax.dot_general(rows[at, :], cols[...], NT, preferred_element_type=jnp.float32)
            value += lax.dot_general(rows[at, :width], cols[:, width:], NT, preferred_element_type=jnp.float32)
            direct[at, pl.ds(pl.multiple_of(step * span, span), span)] = value
            return carry

        lax.fori_loop(0, steps, one, 0)

    @pl.when(step >= steps)
    def _():
        first = (step - steps) * block
        lane = lax.broadcasted_iota(jnp.int32, (height, LANES), 1) // breadth

        def one(index, carry):
            lead = first + index * group
            columns = pl.ds(pl.multiple_of(lead * breadth, LANES), LANES)
            bottoms = [rpair_ref[lead + own] for own in range(group)]
            for other in range(occupied // group):
                swapped = [direct[pl.ds((other * group + m) * height, height), columns] for m in range(group)]
                to = slice(other * LANES, (other + 1) * LANES)
                tops = cpair_ref[other : other + 1, :]
                for own in range(group):
                    exchange = swapped[0] if own == 0 else pltpu.roll(swapped[0], (LANES - own * breadth) % LANES, 1)
                    for m in range(1, group):
                        shift = ((m - own) * breadth) % LANES
                        moved = pltpu.roll(swapped[m], shift, 1) if shift else swapped[m]
                        exchange = jnp.where(lane == m, moved, exchange)
                    at = pl.ds(pl.multiple_of((lead + own) * height, height), height)
                    value = (exchange - 2.0 * direct[at, to]) / (bottoms[own] + tops)
                    high, low = split(value)
                    put = pl.ds(pl.multiple_of((index * group + own) * height, height), height)
                    high_tile[put, to] = high
                    low_tile[put, to] = low
            return carry

        lax.fori_loop(0, block // group, one, 0)
        both = jnp.dot(high_tile[...], chol[...], preferred_element_type=jnp.float32)
        value = both[:, :width] + both[:, width:]
        value += jnp.dot(low_tile[...], chol[:, :width], preferred_element_type=jnp.float32)
        value = value.reshape(block, parts, shard_virtuals, width)
        for part in range(parts):
            out_ref[part] = value[:, part]


def update(turn, rows, cols, chol, rpair, cpair):
    parts, occupied, shard_virtuals, width = rows.shape
    height = parts * shard_virtuals
    breadth = cols.shape[0] * cols.shape[2]
    steps = 6
    block = occupied // steps
    pair_columns = occupied * breadth
    column_block = (cols.shape[0], block, cols.shape[2], width)

    def of_columns(step):
        return (0, jnp.minimum(step, steps - 1), 0, 0)

    return pl.pallas_call(
        functools.partial(kernel, steps),
        grid=(2 * steps,),
        out_shape=jax.ShapeDtypeStruct(rows.shape, jnp.float32),
        in_specs=[
            pl.BlockSpec(memory_space=pltpu.SMEM),
            pl.BlockSpec(rows.shape, lambda step: (0, 0, 0, 0)),
            pl.BlockSpec(column_block, of_columns),
            pl.BlockSpec(column_block, of_columns),
            pl.BlockSpec(rpair.shape, lambda step: (0, 0, 0)),
            pl.BlockSpec(cpair.shape, lambda step: (0, 0)),
        ],
        out_specs=pl.BlockSpec((parts, block, shard_virtuals, width), lambda step: (0, jnp.maximum(step - steps, 0), 0, 0)),
        scratch_shapes=[
            pltpu.VMEM((occupied * height, 2 * width), jnp.bfloat16),
            pltpu.VMEM((block * breadth, 2 * width), jnp.bfloat16),
            pltpu.VMEM((pair_columns, 2 * width), jnp.bfloat16),
            pltpu.VMEM((occupied * height, pair_columns), jnp.float32),
            pltpu.VMEM((block * height, pair_columns), jnp.bfloat16),
            pltpu.VMEM((block * height, pair_columns), jnp.bfloat16),
        ],
        compiler_params=pltpu.CompilerParams(
            dimension_semantics=("arbitrary",), vmem_limit_bytes=66 * 1000 * 1000
        ),
        cost_estimate=pl.CostEstimate(
            flops=12 * occupied * height * pair_columns * width, bytes_accessed=4 * width * (2 * occupied * height + 2 * pair_columns), transcendentals=0
        ),
    )(turn, rows, cols, chol, rpair, cpair)


def gather(x, axis):
    parts = lax.all_gather(x, axis, axis=0)
    if x.shape[1] % 8:
        parts = jnp.transpose(parts, (1, 0, 2, 3)).reshape(1, x.shape[0], -1, x.shape[2])
    return parts


def passed(x, axis):
    n = lax.axis_size(axis)
    blocks = [x]
    for k in range(1, n):
        blocks.append(lax.ppermute(x, axis, [(j, (j - k) % n) for j in range(n)]))
    return jnp.stack(blocks)


PIECES = 6
LAST = PIECES - 1
CORE, ACROSS, UP, DOWN = 0, 1, 2, 3
MESH = pl.DeviceIdType.MESH


def place():
    row = lax.axis_index("row")
    core = lax.rem(row, 2)
    side = lax.rem(lax.div(row, 2), 2)
    half = lax.div(row, 4)
    return row, half, side, core, lax.axis_index("col")


def nearest(col, n_col, order):
    near = jnp.minimum(col, n_col - 1 - col)
    far = order - near
    away = jnp.where(col < n_col - 1 - col, far, -far)
    turn = lax.div(order + 1, 2) * (2 * lax.rem(order, 2) - 1)
    return col + jnp.where(order <= 2 * near, turn, away)


def fused_kernel(
    n_col, given_ref, occ_ref, vir_ref, out_ref, energy_ref, given, chol_ref, land, held, back, factor, rows, fresh, kept, direct, other_direct, high_tile, other_high, low_tile, other_low, total, bottoms, tops,
    mine, around, along, facing, local_sem, send_sem, recv_sem, held_send, held_recv, back_send, back_recv, side_send, side_recv, line_send, line_recv, facing_sem, given_sem, pair_recv, credit,
):
    row, half, side, core, col = place()
    n_row = 8
    bring = pltpu.make_async_copy(given_ref, given, given_sem)
    bring.start()
    occupied, width = chol_ref.shape[0], chol_ref.shape[2]
    virtuals = chol_ref.shape[1]
    size = occupied * virtuals
    span = occupied * 2 * virtuals
    part = occupied // PIECES
    chunks = 2 * n_col
    group = LANES // (2 * virtuals)
    blocks = occupied // group
    tall = group * virtuals
    partner = (row + 1 - 2 * core, col)
    beside = (row + 2 - 4 * side, col)
    across = (row + 4 - 8 * half, col)
    above = (row, col + 1)
    below = (row, col - 1)
    own_chunk = 2 * col + half

    def slot(chunk, owner, piece):
        return land.at[chunk, owner, pl.ds(piece * part, part), :, :]

    def move(source, chunk, target, piece, device):
        return pltpu.make_async_remote_copy(
            src_ref=source,
            dst_ref=slot(chunk, core, piece),
            send_sem=send_sem.at[chunk, target],
            recv_sem=pair_recv.at[chunk] if target == CORE else recv_sem.at[chunk, piece],
            device_id=device,
            device_id_type=MESH,
        )

    def landed(chunk, piece):
        pltpu.make_async_remote_copy(
            src_ref=slot(chunk, core, piece),
            dst_ref=slot(chunk, core, piece),
            send_sem=send_sem.at[chunk, CORE],
            recv_sem=recv_sem.at[chunk, piece],
            device_id=partner,
            device_id_type=MESH,
        ).wait_recv()

    def paired(chunk):
        pltpu.make_async_remote_copy(
            src_ref=land.at[chunk, 1 - core],
            dst_ref=land.at[chunk, 1 - core],
            send_sem=send_sem.at[chunk, CORE],
            recv_sem=pair_recv.at[chunk],
            device_id=partner,
            device_id_type=MESH,
        ).wait_recv()

    def sent(ref, chunk, target, device):
        pltpu.make_async_remote_copy(
            src_ref=ref, dst_ref=ref, send_sem=send_sem.at[chunk, target], recv_sem=pair_recv.at[chunk], device_id=device, device_id_type=MESH
        ).wait_send()

    def pieces_of(ref, piece):
        return ref.at[pl.ds(piece * part, part), :, :]

    def lend(source, step, piece):
        return pltpu.make_async_remote_copy(
            src_ref=pieces_of(source, piece), dst_ref=pieces_of(held.at[step], piece), send_sem=held_send, recv_sem=held_recv, device_id=beside, device_id_type=MESH
        )

    def lent(step):
        return pltpu.make_async_remote_copy(
            src_ref=factor, dst_ref=held.at[step], send_sem=held_send, recv_sem=held_recv, device_id=beside, device_id_type=MESH
        )

    def gave():
        return pltpu.make_async_remote_copy(
            src_ref=total.at[0], dst_ref=back, send_sem=back_send, recv_sem=back_recv.at[0], device_id=beside, device_id_type=MESH
        )

    def give(piece):
        return pltpu.make_async_remote_copy(
            src_ref=pieces_of(total.at[0], piece), dst_ref=pieces_of(back, piece), send_sem=back_send, recv_sem=back_recv.at[piece], device_id=beside, device_id_type=MESH
        )

    def stay(source, piece):
        return pltpu.make_async_copy(pieces_of(source, piece), slot(own_chunk, core, piece), local_sem)

    def take(value, start):
        high, low = split(value.reshape(-1, width))
        at = slice(start, start + high.shape[0])
        rows[at, :width] = low
        rows[at, width:] = high

    def offer(source, piece):
        move(pieces_of(source, piece), own_chunk, ACROSS, piece, across).start()

    def publish(source, step, piece):
        @pl.when(col < n_col - 1)
        def _():
            move(pieces_of(source, piece), own_chunk, UP, piece, above).start()

        @pl.when(col > 0)
        def _():
            move(pieces_of(source, piece), own_chunk, DOWN, piece, below).start()

        lend(source, step, piece).start()
        move(pieces_of(source, piece), own_chunk, CORE, piece, partner).start()
        stay(source, piece).start()

    def relay(distance, first, last):
        def of(position, target, device, more):
            near = 2 * position + half
            away = near + 1 - 2 * half

            def one(order, carry):
                piece = lax.rem(order + 1, PIECES)
                landed(near, piece)

                @pl.when(more)
                def _():
                    move(slot(near, core, piece), near, target, piece, device).start()

                @pl.when(piece > 0)
                def _():
                    move(slot(near, core, piece), near, ACROSS, piece, across).start()

                @pl.when(piece == 0)
                def _():
                    landed(away, piece)

                    @pl.when(more)
                    def _():
                        move(slot(away, core, piece), away, target, piece, device).start()

                    move(slot(away, core, piece), away, CORE, piece, partner).start()

                move(slot(near, core, piece), near, CORE, piece, partner).start()
                return carry

            lax.fori_loop(first, last, one, 0)

        @pl.when(col + distance < n_col)
        def _():
            of(col + distance, DOWN, below, col > 0)

        @pl.when(col >= distance)
        def _():
            of(col - distance, UP, above, col < n_col - 1)

    def turn():
        chunk = own_chunk + 1 - 2 * half
        landed(chunk, 0)

        @pl.when(col < n_col - 1)
        def _():
            move(slot(chunk, core, 0), chunk, UP, 0, above).start()

        @pl.when(col > 0)
        def _():
            move(slot(chunk, core, 0), chunk, DOWN, 0, below).start()

        move(slot(chunk, core, 0), chunk, CORE, 0, partner).start()

    def cross(chunk, first, last):
        def one(order, carry):
            piece = order + 1
            landed(chunk, piece)
            move(slot(chunk, core, piece), chunk, CORE, piece, partner).start()
            return carry

        lax.fori_loop(first, last, one, 0)

    def settle(step):
        def one(position, carry):
            near = 2 * position + half
            away = near + 1 - 2 * half
            sent(land.at[near, core], near, CORE, partner)
            sent(land.at[away, core], away, CORE, partner)

            @pl.when(position == col)
            def _():
                sent(land.at[near, core], near, ACROSS, across)

            @pl.when(position != col)
            def _():
                sent(land.at[near, core, pl.ds(part, occupied - part), :, :], near, ACROSS, across)

            @pl.when((position >= col) & (col > 0))
            def _():
                sent(land.at[near, core], near, DOWN, below)
                sent(slot(away, core, 0), away, DOWN, below)

            @pl.when((position <= col) & (col < n_col - 1))
            def _():
                sent(land.at[near, core], near, UP, above)
                sent(slot(away, core, 0), away, UP, above)

            return carry

        lax.fori_loop(0, n_col, one, 0)
        lent(0).wait_send()

        @pl.when(step == 0)
        def _():
            def thank(device):
                pl.semaphore_signal(credit, inc=1, device_id=device, device_id_type=MESH)

            thank(partner)
            thank(beside)
            thank(across)

            @pl.when(col < n_col - 1)
            def _():
                thank(above)

            @pl.when(col > 0)
            def _():
                thank(below)

    barrier = pltpu.get_barrier_semaphore()

    def same_side(other):
        return lax.rem(half + lax.div(other, 2), 2) * 4 + side * 2 + lax.rem(core + other, 2)

    def greet(device):
        pl.semaphore_signal(barrier, inc=1, device_id=device, device_id_type=MESH)

    greet(beside)
    for other in range(1, n_row // 2):
        greet((same_side(other), col))
    for other in range(1, n_col):
        greet((row, lax.rem(col + other, n_col)))
    bring.wait()
    for piece in range(PIECES):
        at = slice(piece * part, (piece + 1) * part)
        chol_ref[at] = jnp.transpose(given[:, at, :], (1, 0, 2))
    pl.semaphore_wait(barrier, n_row // 2 + n_col - 1)

    offer(chol_ref, 0)
    for order in range(PIECES):
        piece = (order + 1) % PIECES
        publish(chol_ref, 0, piece)
        if piece:
            offer(chol_ref, piece)
    take(chol_ref[...], size)

    scale = jnp.float32(occupied * virtuals * n_row * n_col)
    vertical = lax.broadcasted_iota(jnp.int32, (virtuals, LANES), 0)
    lateral = lax.broadcasted_iota(jnp.int32, (1, LANES), 1)

    for which in range(2):
        first = ((row + (1 - which) * (2 - 4 * side)) * n_col + col) * virtuals
        level = jnp.zeros((virtuals, LANES), jnp.float32)
        for index in range(virtuals):
            level = jnp.where(vertical == index, vir_ref[first + index], level)

        def lower(index, carry):
            bottoms[which, index] = scale * (level - occ_ref[index])
            return carry

        lax.fori_loop(0, occupied, lower, 0)

    def raised(chunk, carry):
        position, other = lax.div(chunk, 2), lax.rem(chunk, 2)
        level = jnp.zeros((1, LANES), jnp.float32)
        for index in range(2 * virtuals):
            source = (4 * other + 2 * side + index // virtuals) * n_col + position
            level = jnp.where(lax.rem(lateral, 2 * virtuals) == index, vir_ref[source * virtuals + index % virtuals], level)
        for block in range(blocks):
            deep = jnp.zeros((1, LANES), jnp.float32)
            for index in range(group):
                deep = jnp.where(lax.div(lateral, 2 * virtuals) == index, occ_ref[block * group + index], deep)
            tops[chunk, block : block + 1, :] = scale * (level - deep)
        return carry

    lax.fori_loop(0, chunks, raised, 0)

    def convert(step, chunk, place):
        def one(index, carry):
            high, low = split(jnp.concatenate([land[chunk, 0, index], land[chunk, 1, index]], axis=0))
            at = pl.ds(pl.multiple_of(index * 2 * virtuals, 2 * virtuals), 2 * virtuals)
            fresh[place, at, :width] = high
            fresh[place, at, width:] = low

            @pl.when(step == 0)
            def _():
                kept[chunk, at, :width] = high
                kept[chunk, at, width:] = low

            return carry

        lax.fori_loop(0, occupied, one, 0, unroll=8)

    lane = lax.broadcasted_iota(jnp.int32, (virtuals, LANES), 1) // (2 * virtuals)

    products = (direct, other_direct)
    highs, lows = (high_tile, other_high), (low_tile, other_low)

    def product(which, place, part, start, count):
        at = pl.ds(pl.multiple_of(start, LANES), count)
        whose = pl.ds(pl.multiple_of(which * size, size), size)
        value = lax.dot_general(rows[whose, :], fresh[place, at, :], NT, preferred_element_type=jnp.float32)
        value += lax.dot_general(rows[whose, width:], fresh[place, at, :width], NT, preferred_element_type=jnp.float32)
        products[part][:, at] = value

    def amplitude(which, chunk, part, first, second):
        at = pl.ds(pl.multiple_of(first * tall, tall), tall)
        to = slice(second * LANES, (second + 1) * LANES)
        plain = products[part][at, to]
        turned = products[part][second * tall : (second + 1) * tall, pl.ds(pl.multiple_of(first * LANES, LANES), LANES)]
        skew = [turned[(-m) % group * virtuals : ((-m) % group + 1) * virtuals] for m in range(group)]
        skew = [pltpu.roll(value, (-m) % group * 2 * virtuals, 1) if m else value for m, value in enumerate(skew)]
        stride = 1
        while stride < group:
            upper = (lane & stride) != 0
            skew = [jnp.where(upper, skew[(m - stride) % group], skew[m]) for m in range(group)]
            stride *= 2
        top = tops[chunk, second : second + 1, :]
        values = []
        for m in range(group):
            exchange = pltpu.roll(skew[m], LANES - m * 2 * virtuals, 1) if m else skew[m]
            bottom = bottoms[which, first * group + m]
            values.append((exchange - 2.0 * plain[m * virtuals : (m + 1) * virtuals]) / (bottom + top))
        high, low = split(jnp.concatenate(values, axis=0))
        highs[part][at, to] = high
        lows[part][at, to] = low

    def collect(chunk, part, start, count):
        at = pl.ds(pl.multiple_of(start, tall), count)
        both = jnp.dot(highs[part][at, :], kept[chunk], preferred_element_type=jnp.float32)
        value = both[:, :width] + both[:, width:]
        value += jnp.dot(lows[part][at, :], kept[chunk, :, :width], preferred_element_type=jnp.float32)
        return value.reshape(count // virtuals, virtuals, width)

    cuts = span // (2 * LANES)

    def alone(which, chunk, place):
        product(which, place, 0, 0, span)

        def rate(index, carry):
            for block in range(2 * blocks):
                amplitude(which, chunk, 0, index * 2 + block // blocks, block % blocks)
            return carry

        lax.fori_loop(0, blocks // 2, rate, 0)
        total[which] += collect(chunk, 0, 0, size)

    def contract(one, two, after, between):
        (which, chunk, place), (other, second_chunk, second_place) = one, two
        product(which, place, 0, 0, span)
        after()

        def begin(index, carry):
            for block in range(blocks * blocks // cuts):
                amplitude(which, chunk, 0, index * (blocks // cuts) + block // blocks, block % blocks)
            product(other, second_place, 1, index * 2 * LANES, 2 * LANES)
            return carry

        lax.fori_loop(0, cuts, begin, 0)
        between()

        def finish(index, carry):
            for block in range(blocks * blocks // 2):
                amplitude(other, second_chunk, 1, index * (blocks // 2) + block // blocks, block % blocks)
            at = pl.ds(index * (occupied // 2), occupied // 2)
            total[which, at] += collect(chunk, 0, index * (size // 2), size // 2)

            return carry

        lax.fori_loop(0, 2, finish, 0)
        total[other] += collect(second_chunk, 1, 0, size)

    def to_line(other):
        return pltpu.make_async_remote_copy(
            src_ref=mine, dst_ref=along.at[col], send_sem=line_send.at[other], recv_sem=line_recv.at[col], device_id=(row, lax.rem(col + other, n_col)), device_id_type=MESH
        )

    def from_line(other):
        source = lax.rem(col + other, n_col)
        return pltpu.make_async_remote_copy(
            src_ref=mine, dst_ref=along.at[source], send_sem=line_send.at[other], recv_sem=line_recv.at[source], device_id=(row, source), device_id_type=MESH
        )

    me = 2 * half + core

    def to_side(other):
        return pltpu.make_async_remote_copy(
            src_ref=around.at[me], dst_ref=around.at[me], send_sem=side_send.at[other], recv_sem=side_recv.at[me], device_id=(same_side(other), col), device_id_type=MESH
        )

    def from_side(other):
        source = 2 * lax.rem(half + lax.div(other, 2), 2) + lax.rem(core + other, 2)
        return pltpu.make_async_remote_copy(
            src_ref=around.at[source], dst_ref=around.at[source], send_sem=side_send.at[other], recv_sem=side_recv.at[source], device_id=(same_side(other), col), device_id_type=MESH
        )

    def to_beside():
        return pltpu.make_async_remote_copy(
            src_ref=facing.at[0], dst_ref=facing.at[1], send_sem=facing_sem.at[0], recv_sem=facing_sem.at[1], device_id=beside, device_id_type=MESH
        )

    def iterate(step, carry):
        total[...] = jnp.zeros_like(total)
        pltpu.make_async_copy(factor, land.at[own_chunk, core], local_sem).wait()

        def chunk_of(index):
            return 2 * nearest(col, n_col, lax.div(index, 2)) + half + lax.rem(index, 2) * (1 - 2 * half)

        def one(index, carry):
            chunk = chunk_of(jnp.where(index >= 4, jnp.minimum(index, chunks - 1) - 1, jnp.where((index == 1) | (index == 2), 1, 0)))

            def pass_on(event):
                @pl.when((event >= 0) & (event < (n_col - 2) * PIECES))
                def _():
                    piece = lax.rem(event, PIECES)
                    relay(2 + lax.div(event, PIECES), piece, piece + 1)

            first = jnp.where(index < 4, 2 * index - 3, 2 * index - 4)
            pass_on(first)

            @pl.when(index == chunks - 1)
            def _():
                pass_on(first + 1)

            @pl.when(index == 0)
            def _():
                paired(own_chunk)
                convert(step, own_chunk, 0)

            @pl.when(index == 1)
            def _():
                turn()
                relay(1, 0, PIECES)
                cross(chunk, 0, LAST)
                paired(chunk)
                convert(step, chunk, 1)
                paired(chunk_of(2))
                convert(step, chunk_of(2), 2)

            @pl.when(index == 2)
            def _():
                lent(step).wait_recv()
                take(held[step], 0)

            @pl.when(index == 3)
            def _():
                cross(chunk_of(3), 0, PIECES // 2)

            @pl.when(index == 4)
            def _():
                cross(chunk, PIECES // 2, LAST)

            @pl.when(index == 6)
            def _():
                cross(chunk, LAST - 1, LAST)

            @pl.when((index >= 4) & (index < chunks))
            def _():
                paired(chunk)
                convert(step, chunk, 1)

            @pl.when(index == chunks)
            def _():
                for piece in range(PIECES):
                    give(piece).start()
                settle(step)

            @pl.when(lax.rem(index, 3) == 0)
            def _():
                @pl.when(index < 4)
                def _():
                    alone(jnp.where(index == 0, 1, 0), own_chunk, 0)

            @pl.when((index == 1) | (index == 2) | (index >= 4))
            def _():
                def between():
                    @pl.when(index != chunks - 1)
                    def _():
                        pass_on(first + 1)

                    @pl.when(index == 5)
                    def _():
                        cross(chunk_of(5), 0, LAST - 1)

                    @pl.when(index == 6)
                    def _():
                        cross(chunk_of(7), 0, LAST - 2)

                def after():
                    @pl.when(index == chunks - 1)
                    def _():
                        cross(chunk_of(7), LAST - 2, LAST)
                        paired(chunk_of(7))
                        convert(step, chunk_of(7), 2)

                late = index >= chunks - 1
                which = jnp.where((index == 1) | (index == chunks), 1, 0)
                other = jnp.where((index == 2) | (index == chunks - 1), 0, 1)
                second = jnp.where(index < 4, 2, jnp.where(late, chunks - 1, index - 1))
                contract((which, chunk, 1), (other, chunk_of(second), jnp.where((index < 4) | late, 2, 1)), after, between)

            return carry

        lax.fori_loop(0, chunks + 1, one, 0)
        @pl.when(step == 0)
        def _():
            pl.semaphore_wait(credit, 3 + jnp.minimum(col, 1) + jnp.minimum(n_col - 1 - col, 1))

        def weigh(index, energy):
            return energy + chol_ref[index] * total[1, index] + held[0, index] * total[0, index]

        def tally():
            energy = lax.fori_loop(0, occupied, weigh, jnp.zeros((virtuals, width), jnp.float32), unroll=4)
            folded = energy[:, :LANES]
            for index in range(1, width // LANES):
                folded += energy[:, index * LANES : (index + 1) * LANES]
            mine[step] = folded

        @pl.when(step == ITERS - 1)
        def _():
            tally()
            along[col] = mine[...]
            for other in range(1, n_col):
                to_line(other).start()

        for piece in range(PIECES):
            if piece == PIECES // 3:

                @pl.when(step == ITERS - 1)
                def _():
                    for other in range(1, n_col):
                        from_line(other).wait_recv()
                    around[me] = sum(along[index] for index in range(n_col))
                    for other in range(1, n_row // 2):
                        to_side(other).start()

            if piece == 2 * PIECES // 3:

                @pl.when(step == ITERS - 1)
                def _():
                    for other in range(1, n_row // 2):
                        from_side(other).wait_recv()
                    facing[0] = sum(around[index] for index in range(n_row // 2))
                    to_beside().start()

            give(piece).wait_recv()
            at = slice(piece * part, (piece + 1) * part)
            value = total[1, at] + back[at]

            @pl.when(step == 0)
            def _():
                fresh_rows = chol_ref[at] + value
                factor[at] = fresh_rows
                publish(factor, 1, piece)
                offer(factor, piece)
                take(fresh_rows, size + piece * part * virtuals)

            @pl.when(step == ITERS - 1)
            def _():
                out_ref[:, at, :] = jnp.transpose(value, (1, 0, 2))

        gave().wait_send()

        @pl.when(step == 0)
        def _():
            tally()

        return carry

    lax.fori_loop(0, ITERS, iterate, 0)
    to_beside().wait_recv()
    both = facing[0] + facing[1]
    for step in range(ITERS):
        energy_ref[step] = jnp.sum(both[step]) / scale
    to_beside().wait_send()
    for other in range(1, n_col):
        to_line(other).wait_send()
    for other in range(1, n_row // 2):
        to_side(other).wait_send()


def fused(chol, eps_occ, eps_vir):
    n_col = lax.axis_size("col")
    n_row = lax.axis_size("row")
    shard, width = chol.shape
    occupied = eps_occ.shape[0]
    virtuals = shard // occupied
    size, span = shard, 2 * shard
    shape = (occupied, virtuals, width)
    dma = pltpu.SemaphoreType.DMA
    work, energies = pl.pallas_call(
        functools.partial(fused_kernel, n_col),
        out_shape=(pltpu.VMEM((virtuals, occupied, width), jnp.float32), jax.ShapeDtypeStruct((ITERS,), jnp.float32)),
        in_specs=[pl.BlockSpec(memory_space=pl.ANY), pl.BlockSpec(memory_space=pltpu.SMEM), pl.BlockSpec(memory_space=pltpu.SMEM)],
        out_specs=(pl.BlockSpec(memory_space=pltpu.VMEM), pl.BlockSpec(memory_space=pltpu.SMEM)),
        scratch_shapes=[
            pltpu.VMEM((virtuals, occupied, width), jnp.float32),
            pltpu.VMEM(shape, jnp.float32),
            pltpu.VMEM((2 * n_col, 2, occupied, virtuals, width), jnp.float32),
            pltpu.VMEM((ITERS,) + shape, jnp.float32),
            pltpu.VMEM(shape, jnp.float32),
            pltpu.VMEM(shape, jnp.float32),
            pltpu.VMEM((2 * size, 2 * width), jnp.bfloat16),
            pltpu.VMEM((3, span, 2 * width), jnp.bfloat16),
            pltpu.VMEM((2 * n_col, span, 2 * width), jnp.bfloat16),
            pltpu.VMEM((size, span), jnp.float32),
            pltpu.VMEM((size, span), jnp.float32),
            pltpu.VMEM((size, span), jnp.bfloat16),
            pltpu.VMEM((size, span), jnp.bfloat16),
            pltpu.VMEM((size, span), jnp.bfloat16),
            pltpu.VMEM((size, span), jnp.bfloat16),
            pltpu.VMEM((2,) + shape, jnp.float32),
            pltpu.VMEM((2, occupied, virtuals, LANES), jnp.float32),
            pltpu.VMEM((2 * n_col, 2 * occupied * virtuals // LANES, LANES), jnp.float32),
            pltpu.VMEM((ITERS, virtuals, LANES), jnp.float32),
            pltpu.VMEM((n_row // 2, ITERS, virtuals, LANES), jnp.float32),
            pltpu.VMEM((n_col, ITERS, virtuals, LANES), jnp.float32),
            pltpu.VMEM((2, ITERS, virtuals, LANES), jnp.float32),
            dma(()),
            dma((2 * n_col, 4)),
            dma((2 * n_col, PIECES)),
            dma(()),
            dma(()),
            dma(()),
            dma((PIECES,)),
            dma((n_row // 2,)),
            dma((n_row // 2,)),
            dma((n_col,)),
            dma((n_col,)),
            dma((2,)),
            dma(()),
            dma((2 * n_col,)),
            pltpu.SemaphoreType.REGULAR,
        ],
        compiler_params=pltpu.CompilerParams(collective_id=0, has_side_effects=True, vmem_limit_bytes=60 * 1000 * 1000),
    )(chol.reshape(virtuals, occupied, width), eps_occ, eps_vir)
    return work.reshape(shard, width), energies


def shards(chol, eps_occ, eps_vir):
    if (lax.axis_size("row"), lax.axis_size("col")) == (8, 4) and chol.shape[0] == 8 * eps_occ.shape[0] and eps_occ.shape[0] % 48 == 0 and chol.shape[1] % LANES == 0:
        return fused(chol, eps_occ, eps_vir)
    n_row = lax.axis_size("row")
    n_col = lax.axis_size("col")
    row_index = lax.axis_index("row")
    col_index = lax.axis_index("col")
    shard, width = chol.shape
    occupied = eps_occ.shape[0]
    virtual = eps_vir.shape[0]
    shard_virtuals = shard // occupied
    block_virtuals = n_col * shard_virtuals
    total = virtual * occupied
    scale = jnp.float32(total)
    row_vir = lax.dynamic_slice_in_dim(eps_vir, row_index * block_virtuals, block_virtuals, 0)
    col_vir = lax.dynamic_slice_in_dim(
        eps_vir.reshape(n_row, block_virtuals), col_index * shard_virtuals, shard_virtuals, 1
    ).reshape(n_row * shard_virtuals)
    rpair = scale * (row_vir[None, :] - eps_occ[:, None])
    rpair = jnp.broadcast_to(rpair[:, :, None], (occupied, block_virtuals, LANES))
    cpair = (scale * (col_vir[None, :] - eps_occ[:, None])).reshape(-1, LANES)
    chol_t = jnp.transpose(chol.reshape(shard_virtuals, occupied, width), (1, 0, 2))
    chol_cols = gather(chol_t, "row")
    factor = chol_t
    sums = []
    for step in range(ITERS):
        if shard_virtuals % 8:
            rows = gather(factor, "col")
            turn = jnp.zeros((1,), jnp.int32)
        else:
            rows = passed(factor, "col")
            turn = jnp.full((1,), n_col - col_index, jnp.int32)
        cols = chol_cols if step == 0 else gather(factor, "row")
        partial_value = update(turn, rows, cols, chol_cols, rpair, cpair)
        if shard_virtuals % 8:
            partial_value = jnp.transpose(
                partial_value.reshape(occupied, n_col, shard_virtuals, width), (1, 0, 2, 3)
            )
        work = lax.psum_scatter(partial_value, "col", scatter_dimension=0, tiled=False)
        factor = chol_t + work
        sums.append(jnp.sum(chol_t * work))
    energies = lax.psum(jnp.stack(sums), ("row", "col"))
    return jnp.transpose(work, (1, 0, 2)).reshape(shard, width), energies / scale


def solution(mesh):
    placed = (P(("row", "col"), None), P(), P())
    return jax.shard_map(
        shards,
        mesh=mesh,
        in_specs=placed,
        out_specs=(P(("row", "col"), None), P()),
        check_vma=False,
    )
```

```python
import functools

import jax
import jax.numpy as jnp
from jax import lax
from jax.experimental import pallas as pl
from jax.experimental.pallas import tpu as pltpu
from jax.sharding import PartitionSpec as P

ITERS = 2
LANES = 128
NT = (((1,), (1,)), ((), ()))


def split(x):
    high = x.astype(jnp.bfloat16)
    low = (x - high.astype(jnp.float32)).astype(jnp.bfloat16)
    return high, low


def flat(ref, index, turn=None):
    parts = range(ref.shape[0])
    pieces = [ref[part if turn is None else (part + turn) % len(parts), index] for part in parts]
    return pieces[0] if len(pieces) == 1 else jnp.concatenate(pieces, axis=0)


def kernel(steps, turn_ref, rows_ref, cols_ref, chol_ref, rpair_ref, cpair_ref, out_ref, rows, cols, chol, direct, high_tile, low_tile):
    step = pl.program_id(0)
    parts, occupied, shard_virtuals, width = rows_ref.shape
    height = parts * shard_virtuals
    block = occupied // steps
    breadth = cols_ref.shape[0] * cols_ref.shape[2]
    span = block * breadth
    group = LANES // breadth

    @pl.when(step == 0)
    def _():
        def one(index, carry):
            high, low = split(flat(rows_ref, index, turn_ref[0]))
            at = pl.ds(pl.multiple_of(index * height, height), height)
            rows[at, :width] = high
            rows[at, width:] = low
            return carry

        lax.fori_loop(0, occupied, one, 0)

    @pl.when(step < steps)
    def _():
        for index in range(block):
            high, low = split(flat(cols_ref, index))
            cols[index * breadth : (index + 1) * breadth, :width] = low
            cols[index * breadth : (index + 1) * breadth, width:] = high
            high, low = split(flat(chol_ref, index))
            at = pl.ds(pl.multiple_of(step * span + index * breadth, breadth), breadth)
            chol[at, :width] = high
            chol[at, width:] = low

        def one(index, carry):
            at = pl.ds(pl.multiple_of(index * block * height, block * height), block * height)
            value = lax.dot_general(rows[at, :], cols[...], NT, preferred_element_type=jnp.float32)
            value += lax.dot_general(rows[at, :width], cols[:, width:], NT, preferred_element_type=jnp.float32)
            direct[at, pl.ds(pl.multiple_of(step * span, span), span)] = value
            return carry

        lax.fori_loop(0, steps, one, 0)

    @pl.when(step >= steps)
    def _():
        first = (step - steps) * block
        lane = lax.broadcasted_iota(jnp.int32, (height, LANES), 1) // breadth

        def one(index, carry):
            lead = first + index * group
            columns = pl.ds(pl.multiple_of(lead * breadth, LANES), LANES)
            bottoms = [rpair_ref[lead + own] for own in range(group)]
            for other in range(occupied // group):
                swapped = [direct[pl.ds((other * group + m) * height, height), columns] for m in range(group)]
                to = slice(other * LANES, (other + 1) * LANES)
                tops = cpair_ref[other : other + 1, :]
                for own in range(group):
                    exchange = swapped[0] if own == 0 else pltpu.roll(swapped[0], (LANES - own * breadth) % LANES, 1)
                    for m in range(1, group):
                        shift = ((m - own) * breadth) % LANES
                        moved = pltpu.roll(swapped[m], shift, 1) if shift else swapped[m]
                        exchange = jnp.where(lane == m, moved, exchange)
                    at = pl.ds(pl.multiple_of((lead + own) * height, height), height)
                    value = (exchange - 2.0 * direct[at, to]) / (bottoms[own] + tops)
                    high, low = split(value)
                    put = pl.ds(pl.multiple_of((index * group + own) * height, height), height)
                    high_tile[put, to] = high
                    low_tile[put, to] = low
            return carry

        lax.fori_loop(0, block // group, one, 0)
        both = jnp.dot(high_tile[...], chol[...], preferred_element_type=jnp.float32)
        value = both[:, :width] + both[:, width:]
        value += jnp.dot(low_tile[...], chol[:, :width], preferred_element_type=jnp.float32)
        value = value.reshape(block, parts, shard_virtuals, width)
        for part in range(parts):
            out_ref[part] = value[:, part]


def update(turn, rows, cols, chol, rpair, cpair):
    parts, occupied, shard_virtuals, width = rows.shape
    height = parts * shard_virtuals
    breadth = cols.shape[0] * cols.shape[2]
    steps = 6
    block = occupied // steps
    pair_columns = occupied * breadth
    column_block = (cols.shape[0], block, cols.shape[2], width)

    def of_columns(step):
        return (0, jnp.minimum(step, steps - 1), 0, 0)

    return pl.pallas_call(
        functools.partial(kernel, steps),
        grid=(2 * steps,),
        out_shape=jax.ShapeDtypeStruct(rows.shape, jnp.float32),
        in_specs=[
            pl.BlockSpec(memory_space=pltpu.SMEM),
            pl.BlockSpec(rows.shape, lambda step: (0, 0, 0, 0)),
            pl.BlockSpec(column_block, of_columns),
            pl.BlockSpec(column_block, of_columns),
            pl.BlockSpec(rpair.shape, lambda step: (0, 0, 0)),
            pl.BlockSpec(cpair.shape, lambda step: (0, 0)),
        ],
        out_specs=pl.BlockSpec((parts, block, shard_virtuals, width), lambda step: (0, jnp.maximum(step - steps, 0), 0, 0)),
        scratch_shapes=[
            pltpu.VMEM((occupied * height, 2 * width), jnp.bfloat16),
            pltpu.VMEM((block * breadth, 2 * width), jnp.bfloat16),
            pltpu.VMEM((pair_columns, 2 * width), jnp.bfloat16),
            pltpu.VMEM((occupied * height, pair_columns), jnp.float32),
            pltpu.VMEM((block * height, pair_columns), jnp.bfloat16),
            pltpu.VMEM((block * height, pair_columns), jnp.bfloat16),
        ],
        compiler_params=pltpu.CompilerParams(
            dimension_semantics=("arbitrary",), vmem_limit_bytes=66 * 1000 * 1000
        ),
        cost_estimate=pl.CostEstimate(
            flops=12 * occupied * height * pair_columns * width, bytes_accessed=4 * width * (2 * occupied * height + 2 * pair_columns), transcendentals=0
        ),
    )(turn, rows, cols, chol, rpair, cpair)


def gather(x, axis):
    parts = lax.all_gather(x, axis, axis=0)
    if x.shape[1] % 8:
        parts = jnp.transpose(parts, (1, 0, 2, 3)).reshape(1, x.shape[0], -1, x.shape[2])
    return parts


def passed(x, axis):
    n = lax.axis_size(axis)
    blocks = [x]
    for k in range(1, n):
        blocks.append(lax.ppermute(x, axis, [(j, (j - k) % n) for j in range(n)]))
    return jnp.stack(blocks)


PIECES = 6
LAST = PIECES - 1
CORE, ACROSS, UP, DOWN = 0, 1, 2, 3
MESH = pl.DeviceIdType.MESH


def place():
    row = lax.axis_index("row")
    core = lax.rem(row, 2)
    side = lax.rem(lax.div(row, 2), 2)
    half = lax.div(row, 4)
    return row, half, side, core, lax.axis_index("col")


def nearest(col, n_col, order):
    near = jnp.minimum(col, n_col - 1 - col)
    far = order - near
    away = jnp.where(col < n_col - 1 - col, far, -far)
    turn = lax.div(order + 1, 2) * (2 * lax.rem(order, 2) - 1)
    return col + jnp.where(order <= 2 * near, turn, away)


def fused_kernel(
    n_col, given_ref, occ_ref, vir_ref, out_ref, energy_ref, given, chol_ref, land, held, back, factor, rows, fresh, kept, direct, other_direct, high_tile, other_high, low_tile, other_low, total, bottoms, tops,
    mine, around, along, facing, local_sem, send_sem, recv_sem, held_send, held_recv, back_send, back_recv, side_send, side_recv, line_send, line_recv, facing_sem, given_sem, pair_recv, credit,
):
    row, half, side, core, col = place()
    n_row = 8
    bring = pltpu.make_async_copy(given_ref, given, given_sem)
    bring.start()
    occupied, width = chol_ref.shape[0], chol_ref.shape[2]
    virtuals = chol_ref.shape[1]
    size = occupied * virtuals
    span = occupied * 2 * virtuals
    part = occupied // PIECES
    chunks = 2 * n_col
    group = LANES // (2 * virtuals)
    blocks = occupied // group
    tall = group * virtuals
    partner = (row + 1 - 2 * core, col)
    beside = (row + 2 - 4 * side, col)
    across = (row + 4 - 8 * half, col)
    above = (row, col + 1)
    below = (row, col - 1)
    own_chunk = 2 * col + half

    def slot(chunk, owner, piece):
        return land.at[chunk, owner, pl.ds(piece * part, part), :, :]

    def move(source, chunk, target, piece, device):
        return pltpu.make_async_remote_copy(
            src_ref=source,
            dst_ref=slot(chunk, core, piece),
            send_sem=send_sem.at[chunk, target],
            recv_sem=pair_recv.at[chunk] if target == CORE else recv_sem.at[chunk, piece],
            device_id=device,
            device_id_type=MESH,
        )

    def landed(chunk, piece):
        pltpu.make_async_remote_copy(
            src_ref=slot(chunk, core, piece),
            dst_ref=slot(chunk, core, piece),
            send_sem=send_sem.at[chunk, CORE],
            recv_sem=recv_sem.at[chunk, piece],
            device_id=partner,
            device_id_type=MESH,
        ).wait_recv()

    def paired(chunk):
        pltpu.make_async_remote_copy(
            src_ref=land.at[chunk, 1 - core],
            dst_ref=land.at[chunk, 1 - core],
            send_sem=send_sem.at[chunk, CORE],
            recv_sem=pair_recv.at[chunk],
            device_id=partner,
            device_id_type=MESH,
        ).wait_recv()

    def sent(ref, chunk, target, device):
        pltpu.make_async_remote_copy(
            src_ref=ref, dst_ref=ref, send_sem=send_sem.at[chunk, target], recv_sem=pair_recv.at[chunk], device_id=device, device_id_type=MESH
        ).wait_send()

    def pieces_of(ref, piece):
        return ref.at[pl.ds(piece * part, part), :, :]

    def lend(source, step, piece):
        return pltpu.make_async_remote_copy(
            src_ref=pieces_of(source, piece), dst_ref=pieces_of(held.at[step], piece), send_sem=held_send, recv_sem=held_recv, device_id=beside, device_id_type=MESH
        )

    def lent(step):
        return pltpu.make_async_remote_copy(
            src_ref=factor, dst_ref=held.at[step], send_sem=held_send, recv_sem=held_recv, device_id=beside, device_id_type=MESH
        )

    def gave():
        return pltpu.make_async_remote_copy(
            src_ref=total.at[0], dst_ref=back, send_sem=back_send, recv_sem=back_recv.at[0], device_id=beside, device_id_type=MESH
        )

    def give(piece):
        return pltpu.make_async_remote_copy(
            src_ref=pieces_of(total.at[0], piece), dst_ref=pieces_of(back, piece), send_sem=back_send, recv_sem=back_recv.at[piece], device_id=beside, device_id_type=MESH
        )

    def stay(source, piece):
        return pltpu.make_async_copy(pieces_of(source, piece), slot(own_chunk, core, piece), local_sem)

    def take(value, start):
        high, low = split(value.reshape(-1, width))
        at = slice(start, start + high.shape[0])
        rows[at, :width] = low
        rows[at, width:] = high

    def offer(source, piece):
        move(pieces_of(source, piece), own_chunk, ACROSS, piece, across).start()

    def publish(source, step, piece):
        @pl.when(col < n_col - 1)
        def _():
            move(pieces_of(source, piece), own_chunk, UP, piece, above).start()

        @pl.when(col > 0)
        def _():
            move(pieces_of(source, piece), own_chunk, DOWN, piece, below).start()

        lend(source, step, piece).start()
        move(pieces_of(source, piece), own_chunk, CORE, piece, partner).start()
        stay(source, piece).start()

    def relay(distance, first, last):
        def of(position, target, device, more):
            near = 2 * position + half
            away = near + 1 - 2 * half

            def one(order, carry):
                piece = lax.rem(order + 1, PIECES)
                landed(near, piece)

                @pl.when(piece > 0)
                def _():
                    move(slot(near, core, piece), near, ACROSS, piece, across).start()

                @pl.when(more)
                def _():
                    move(slot(near, core, piece), near, target, piece, device).start()

                @pl.when(piece == 0)
                def _():
                    landed(away, piece)

                    @pl.when(more)
                    def _():
                        move(slot(away, core, piece), away, target, piece, device).start()

                    move(slot(away, core, piece), away, CORE, piece, partner).start()

                move(slot(near, core, piece), near, CORE, piece, partner).start()
                return carry

            lax.fori_loop(first, last, one, 0)

        @pl.when(col + distance < n_col)
        def _():
            of(col + distance, DOWN, below, col > 0)

        @pl.when(col >= distance)
        def _():
            of(col - distance, UP, above, col < n_col - 1)

    def turn():
        chunk = own_chunk + 1 - 2 * half
        landed(chunk, 0)

        @pl.when(col < n_col - 1)
        def _():
            move(slot(chunk, core, 0), chunk, UP, 0, above).start()

        @pl.when(col > 0)
        def _():
            move(slot(chunk, core, 0), chunk, DOWN, 0, below).start()

        move(slot(chunk, core, 0), chunk, CORE, 0, partner).start()

    def cross(chunk, first, last):
        def one(order, carry):
            piece = order + 1
            landed(chunk, piece)
            move(slot(chunk, core, piece), chunk, CORE, piece, partner).start()
            return carry

        lax.fori_loop(first, last, one, 0)

    def settle(step):
        def one(position, carry):
            near = 2 * position + half
            away = near + 1 - 2 * half
            sent(land.at[near, core], near, CORE, partner)
            sent(land.at[away, core], away, CORE, partner)

            @pl.when(position == col)
            def _():
                sent(land.at[near, core], near, ACROSS, across)

            @pl.when(position != col)
            def _():
                sent(land.at[near, core, pl.ds(part, occupied - part), :, :], near, ACROSS, across)

            @pl.when((position >= col) & (col > 0))
            def _():
                sent(land.at[near, core], near, DOWN, below)
                sent(slot(away, core, 0), away, DOWN, below)

            @pl.when((position <= col) & (col < n_col - 1))
            def _():
                sent(land.at[near, core], near, UP, above)
                sent(slot(away, core, 0), away, UP, above)

            return carry

        lax.fori_loop(0, n_col, one, 0)
        lent(0).wait_send()

        @pl.when(step == 0)
        def _():
            def thank(device):
                pl.semaphore_signal(credit, inc=1, device_id=device, device_id_type=MESH)

            thank(partner)
            thank(beside)
            thank(across)

            @pl.when(col < n_col - 1)
            def _():
                thank(above)

            @pl.when(col > 0)
            def _():
                thank(below)

    barrier = pltpu.get_barrier_semaphore()

    def same_side(other):
        return lax.rem(half + lax.div(other, 2), 2) * 4 + side * 2 + lax.rem(core + other, 2)

    def greet(device):
        pl.semaphore_signal(barrier, inc=1, device_id=device, device_id_type=MESH)

    greet(beside)
    for other in range(1, n_row // 2):
        greet((same_side(other), col))
    for other in range(1, n_col):
        greet((row, lax.rem(col + other, n_col)))
    bring.wait()
    for piece in range(PIECES):
        at = slice(piece * part, (piece + 1) * part)
        chol_ref[at] = jnp.transpose(given[:, at, :], (1, 0, 2))
    pl.semaphore_wait(barrier, n_row // 2 + n_col - 1)

    offer(chol_ref, 0)
    for order in range(PIECES):
        piece = (order + 1) % PIECES
        if piece:
            offer(chol_ref, piece)
        publish(chol_ref, 0, piece)
    take(chol_ref[...], size)

    scale = jnp.float32(occupied * virtuals * n_row * n_col)
    vertical = lax.broadcasted_iota(jnp.int32, (virtuals, LANES), 0)
    lateral = lax.broadcasted_iota(jnp.int32, (1, LANES), 1)

    for which in range(2):
        first = ((row + (1 - which) * (2 - 4 * side)) * n_col + col) * virtuals
        level = jnp.zeros((virtuals, LANES), jnp.float32)
        for index in range(virtuals):
            level = jnp.where(vertical == index, vir_ref[first + index], level)

        def lower(index, carry):
            bottoms[which, index] = scale * (level - occ_ref[index])
            return carry

        lax.fori_loop(0, occupied, lower, 0)

    def raised(chunk, carry):
        position, other = lax.div(chunk, 2), lax.rem(chunk, 2)
        level = jnp.zeros((1, LANES), jnp.float32)
        for index in range(2 * virtuals):
            source = (4 * other + 2 * side + index // virtuals) * n_col + position
            level = jnp.where(lax.rem(lateral, 2 * virtuals) == index, vir_ref[source * virtuals + index % virtuals], level)
        for block in range(blocks):
            deep = jnp.zeros((1, LANES), jnp.float32)
            for index in range(group):
                deep = jnp.where(lax.div(lateral, 2 * virtuals) == index, occ_ref[block * group + index], deep)
            tops[chunk, block : block + 1, :] = scale * (level - deep)
        return carry

    lax.fori_loop(0, chunks, raised, 0)

    def convert(step, chunk, place):
        def one(index, carry):
            high, low = split(jnp.concatenate([land[chunk, 0, index], land[chunk, 1, index]], axis=0))
            at = pl.ds(pl.multiple_of(index * 2 * virtuals, 2 * virtuals), 2 * virtuals)
            fresh[place, at, :width] = high
            fresh[place, at, width:] = low

            @pl.when(step == 0)
            def _():
                kept[chunk, at, :width] = high
                kept[chunk, at, width:] = low

            return carry

        lax.fori_loop(0, occupied, one, 0, unroll=8)

    lane = lax.broadcasted_iota(jnp.int32, (virtuals, LANES), 1) // (2 * virtuals)

    products = (direct, other_direct)
    highs, lows = (high_tile, other_high), (low_tile, other_low)

    def product(which, place, part, start, count):
        at = pl.ds(pl.multiple_of(start, LANES), count)
        whose = pl.ds(pl.multiple_of(which * size, size), size)
        value = lax.dot_general(rows[whose, :], fresh[place, at, :], NT, preferred_element_type=jnp.float32)
        value += lax.dot_general(rows[whose, width:], fresh[place, at, :width], NT, preferred_element_type=jnp.float32)
        products[part][:, at] = value

    def amplitude(which, chunk, part, first, second):
        at = pl.ds(pl.multiple_of(first * tall, tall), tall)
        to = slice(second * LANES, (second + 1) * LANES)
        plain = products[part][at, to]
        turned = products[part][second * tall : (second + 1) * tall, pl.ds(pl.multiple_of(first * LANES, LANES), LANES)]
        skew = [turned[(-m) % group * virtuals : ((-m) % group + 1) * virtuals] for m in range(group)]
        skew = [pltpu.roll(value, (-m) % group * 2 * virtuals, 1) if m else value for m, value in enumerate(skew)]
        stride = 1
        while stride < group:
            upper = (lane & stride) != 0
            skew = [jnp.where(upper, skew[(m - stride) % group], skew[m]) for m in range(group)]
            stride *= 2
        top = tops[chunk, second : second + 1, :]
        values = []
        for m in range(group):
            exchange = pltpu.roll(skew[m], LANES - m * 2 * virtuals, 1) if m else skew[m]
            bottom = bottoms[which, first * group + m]
            values.append((exchange - 2.0 * plain[m * virtuals : (m + 1) * virtuals]) / (bottom + top))
        high, low = split(jnp.concatenate(values, axis=0))
        highs[part][at, to] = high
        lows[part][at, to] = low

    def collect(chunk, part, start, count):
        at = pl.ds(pl.multiple_of(start, tall), count)
        both = jnp.dot(highs[part][at, :], kept[chunk], preferred_element_type=jnp.float32)
        value = both[:, :width] + both[:, width:]
        value += jnp.dot(lows[part][at, :], kept[chunk, :, :width], preferred_element_type=jnp.float32)
        return value.reshape(count // virtuals, virtuals, width)

    cuts = span // (2 * LANES)

    def alone(which, chunk, place):
        product(which, place, 0, 0, span)

        def rate(index, carry):
            for block in range(2 * blocks):
                amplitude(which, chunk, 0, index * 2 + block // blocks, block % blocks)
            return carry

        lax.fori_loop(0, blocks // 2, rate, 0)
        total[which] += collect(chunk, 0, 0, size)

    def contract(one, two, after, between):
        (which, chunk, place), (other, second_chunk, second_place) = one, two
        product(which, place, 0, 0, span)
        after()

        def begin(index, carry):
            for block in range(blocks * blocks // cuts):
                amplitude(which, chunk, 0, index * (blocks // cuts) + block // blocks, block % blocks)
            product(other, second_place, 1, index * 2 * LANES, 2 * LANES)
            return carry

        lax.fori_loop(0, cuts, begin, 0)
        between()

        def finish(index, carry):
            for block in range(blocks * blocks // 2):
                amplitude(other, second_chunk, 1, index * (blocks // 2) + block // blocks, block % blocks)
            at = pl.ds(index * (occupied // 2), occupied // 2)
            total[which, at] += collect(chunk, 0, index * (size // 2), size // 2)

            return carry

        lax.fori_loop(0, 2, finish, 0)
        total[other] += collect(second_chunk, 1, 0, size)

    def to_line(other):
        return pltpu.make_async_remote_copy(
            src_ref=mine, dst_ref=along.at[col], send_sem=line_send.at[other], recv_sem=line_recv.at[col], device_id=(row, lax.rem(col + other, n_col)), device_id_type=MESH
        )

    def from_line(other):
        source = lax.rem(col + other, n_col)
        return pltpu.make_async_remote_copy(
            src_ref=mine, dst_ref=along.at[source], send_sem=line_send.at[other], recv_sem=line_recv.at[source], device_id=(row, source), device_id_type=MESH
        )

    me = 2 * half + core

    def to_side(other):
        return pltpu.make_async_remote_copy(
            src_ref=around.at[me], dst_ref=around.at[me], send_sem=side_send.at[other], recv_sem=side_recv.at[me], device_id=(same_side(other), col), device_id_type=MESH
        )

    def from_side(other):
        source = 2 * lax.rem(half + lax.div(other, 2), 2) + lax.rem(core + other, 2)
        return pltpu.make_async_remote_copy(
            src_ref=around.at[source], dst_ref=around.at[source], send_sem=side_send.at[other], recv_sem=side_recv.at[source], device_id=(same_side(other), col), device_id_type=MESH
        )

    def to_beside():
        return pltpu.make_async_remote_copy(
            src_ref=facing.at[0], dst_ref=facing.at[1], send_sem=facing_sem.at[0], recv_sem=facing_sem.at[1], device_id=beside, device_id_type=MESH
        )

    def iterate(step, carry):
        total[...] = jnp.zeros_like(total)
        pltpu.make_async_copy(factor, land.at[own_chunk, core], local_sem).wait()

        def chunk_of(index):
            return 2 * nearest(col, n_col, lax.div(index, 2)) + half + lax.rem(index, 2) * (1 - 2 * half)

        def one(index, carry):
            chunk = chunk_of(jnp.where(index >= 4, jnp.minimum(index, chunks - 1) - 1, jnp.where((index == 1) | (index == 2), 1, 0)))

            def pass_on(event):
                @pl.when((event >= 0) & (event < (n_col - 2) * PIECES))
                def _():
                    piece = lax.rem(event, PIECES)
                    relay(2 + lax.div(event, PIECES), piece, piece + 1)

            first = jnp.where(index < 4, 2 * index - 3, 2 * index - 4)
            pass_on(first)

            @pl.when(index == chunks - 1)
            def _():
                pass_on(first + 1)

            @pl.when(index == 0)
            def _():
                paired(own_chunk)
                convert(step, own_chunk, 0)

            @pl.when(index == 1)
            def _():
                turn()
                relay(1, 0, PIECES)
                cross(chunk, 0, LAST)
                paired(chunk)
                convert(step, chunk, 1)
                paired(chunk_of(2))
                convert(step, chunk_of(2), 2)

            @pl.when(index == 2)
            def _():
                lent(step).wait_recv()
                take(held[step], 0)

            @pl.when(index == 3)
            def _():
                cross(chunk_of(3), 0, PIECES // 2)

            @pl.when(index == 4)
            def _():
                cross(chunk, PIECES // 2, LAST)

            @pl.when(index == 6)
            def _():
                cross(chunk, LAST - 1, LAST)

            @pl.when((index >= 4) & (index < chunks))
            def _():
                paired(chunk)
                convert(step, chunk, 1)

            @pl.when(index == chunks)
            def _():
                for piece in range(PIECES):
                    give(piece).start()
                settle(step)

            @pl.when(lax.rem(index, 3) == 0)
            def _():
                @pl.when(index < 4)
                def _():
                    alone(jnp.where(index == 0, 1, 0), own_chunk, 0)

            @pl.when((index == 1) | (index == 2) | (index >= 4))
            def _():
                def between():
                    @pl.when(index != chunks - 1)
                    def _():
                        pass_on(first + 1)

                    @pl.when(index == 5)
                    def _():
                        cross(chunk_of(5), 0, LAST - 1)

                    @pl.when(index == 6)
                    def _():
                        cross(chunk_of(7), 0, LAST - 2)

                def after():
                    @pl.when(index == chunks - 1)
                    def _():
                        cross(chunk_of(7), LAST - 2, LAST)
                        paired(chunk_of(7))
                        convert(step, chunk_of(7), 2)

                late = index >= chunks - 1
                which = jnp.where((index == 1) | (index == chunks), 1, 0)
                other = jnp.where((index == 2) | (index == chunks - 1), 0, 1)
                second = jnp.where(index < 4, 2, jnp.where(late, chunks - 1, index - 1))
                contract((which, chunk, 1), (other, chunk_of(second), jnp.where((index < 4) | late, 2, 1)), after, between)

            return carry

        lax.fori_loop(0, chunks + 1, one, 0)
        @pl.when(step == 0)
        def _():
            pl.semaphore_wait(credit, 3 + jnp.minimum(col, 1) + jnp.minimum(n_col - 1 - col, 1))

        def weigh(index, energy):
            return energy + chol_ref[index] * total[1, index] + held[0, index] * total[0, index]

        def tally():
            energy = lax.fori_loop(0, occupied, weigh, jnp.zeros((virtuals, width), jnp.float32), unroll=4)
            folded = energy[:, :LANES]
            for index in range(1, width // LANES):
                folded += energy[:, index * LANES : (index + 1) * LANES]
            mine[step] = folded

        @pl.when(step == ITERS - 1)
        def _():
            tally()
            along[col] = mine[...]
            for other in range(1, n_col):
                to_line(other).start()

        for piece in range(PIECES):
            if piece == PIECES // 3:

                @pl.when(step == ITERS - 1)
                def _():
                    for other in range(1, n_col):
                        from_line(other).wait_recv()
                    around[me] = sum(along[index] for index in range(n_col))
                    for other in range(1, n_row // 2):
                        to_side(other).start()

            if piece == 2 * PIECES // 3:

                @pl.when(step == ITERS - 1)
                def _():
                    for other in range(1, n_row // 2):
                        from_side(other).wait_recv()
                    facing[0] = sum(around[index] for index in range(n_row // 2))
                    to_beside().start()

            give(piece).wait_recv()
            at = slice(piece * part, (piece + 1) * part)
            value = total[1, at] + back[at]

            @pl.when(step == 0)
            def _():
                fresh_rows = chol_ref[at] + value
                factor[at] = fresh_rows
                offer(factor, piece)
                publish(factor, 1, piece)
                take(fresh_rows, size + piece * part * virtuals)

            @pl.when(step == ITERS - 1)
            def _():
                out_ref[:, at, :] = jnp.transpose(value, (1, 0, 2))

        gave().wait_send()

        @pl.when(step == 0)
        def _():
            tally()

        return carry

    lax.fori_loop(0, ITERS, iterate, 0)
    to_beside().wait_recv()
    both = facing[0] + facing[1]
    for step in range(ITERS):
        energy_ref[step] = jnp.sum(both[step]) / scale
    to_beside().wait_send()
    for other in range(1, n_col):
        to_line(other).wait_send()
    for other in range(1, n_row // 2):
        to_side(other).wait_send()


def fused(chol, eps_occ, eps_vir):
    n_col = lax.axis_size("col")
    n_row = lax.axis_size("row")
    shard, width = chol.shape
    occupied = eps_occ.shape[0]
    virtuals = shard // occupied
    size, span = shard, 2 * shard
    shape = (occupied, virtuals, width)
    dma = pltpu.SemaphoreType.DMA
    work, energies = pl.pallas_call(
        functools.partial(fused_kernel, n_col),
        out_shape=(pltpu.VMEM((virtuals, occupied, width), jnp.float32), jax.ShapeDtypeStruct((ITERS,), jnp.float32)),
        in_specs=[pl.BlockSpec(memory_space=pl.ANY), pl.BlockSpec(memory_space=pltpu.SMEM), pl.BlockSpec(memory_space=pltpu.SMEM)],
        out_specs=(pl.BlockSpec(memory_space=pltpu.VMEM), pl.BlockSpec(memory_space=pltpu.SMEM)),
        scratch_shapes=[
            pltpu.VMEM((virtuals, occupied, width), jnp.float32),
            pltpu.VMEM(shape, jnp.float32),
            pltpu.VMEM((2 * n_col, 2, occupied, virtuals, width), jnp.float32),
            pltpu.VMEM((ITERS,) + shape, jnp.float32),
            pltpu.VMEM(shape, jnp.float32),
            pltpu.VMEM(shape, jnp.float32),
            pltpu.VMEM((2 * size, 2 * width), jnp.bfloat16),
            pltpu.VMEM((3, span, 2 * width), jnp.bfloat16),
            pltpu.VMEM((2 * n_col, span, 2 * width), jnp.bfloat16),
            pltpu.VMEM((size, span), jnp.float32),
            pltpu.VMEM((size, span), jnp.float32),
            pltpu.VMEM((size, span), jnp.bfloat16),
            pltpu.VMEM((size, span), jnp.bfloat16),
            pltpu.VMEM((size, span), jnp.bfloat16),
            pltpu.VMEM((size, span), jnp.bfloat16),
            pltpu.VMEM((2,) + shape, jnp.float32),
            pltpu.VMEM((2, occupied, virtuals, LANES), jnp.float32),
            pltpu.VMEM((2 * n_col, 2 * occupied * virtuals // LANES, LANES), jnp.float32),
            pltpu.VMEM((ITERS, virtuals, LANES), jnp.float32),
            pltpu.VMEM((n_row // 2, ITERS, virtuals, LANES), jnp.float32),
            pltpu.VMEM((n_col, ITERS, virtuals, LANES), jnp.float32),
            pltpu.VMEM((2, ITERS, virtuals, LANES), jnp.float32),
            dma(()),
            dma((2 * n_col, 4)),
            dma((2 * n_col, PIECES)),
            dma(()),
            dma(()),
            dma(()),
            dma((PIECES,)),
            dma((n_row // 2,)),
            dma((n_row // 2,)),
            dma((n_col,)),
            dma((n_col,)),
            dma((2,)),
            dma(()),
            dma((2 * n_col,)),
            pltpu.SemaphoreType.REGULAR,
        ],
        compiler_params=pltpu.CompilerParams(collective_id=0, has_side_effects=True, vmem_limit_bytes=60 * 1000 * 1000),
    )(chol.reshape(virtuals, occupied, width), eps_occ, eps_vir)
    return work.reshape(shard, width), energies


def shards(chol, eps_occ, eps_vir):
    if (lax.axis_size("row"), lax.axis_size("col")) == (8, 4) and chol.shape[0] == 8 * eps_occ.shape[0] and eps_occ.shape[0] % 48 == 0 and chol.shape[1] % LANES == 0:
        return fused(chol, eps_occ, eps_vir)
    n_row = lax.axis_size("row")
    n_col = lax.axis_size("col")
    row_index = lax.axis_index("row")
    col_index = lax.axis_index("col")
    shard, width = chol.shape
    occupied = eps_occ.shape[0]
    virtual = eps_vir.shape[0]
    shard_virtuals = shard // occupied
    block_virtuals = n_col * shard_virtuals
    total = virtual * occupied
    scale = jnp.float32(total)
    row_vir = lax.dynamic_slice_in_dim(eps_vir, row_index * block_virtuals, block_virtuals, 0)
    col_vir = lax.dynamic_slice_in_dim(
        eps_vir.reshape(n_row, block_virtuals), col_index * shard_virtuals, shard_virtuals, 1
    ).reshape(n_row * shard_virtuals)
    rpair = scale * (row_vir[None, :] - eps_occ[:, None])
    rpair = jnp.broadcast_to(rpair[:, :, None], (occupied, block_virtuals, LANES))
    cpair = (scale * (col_vir[None, :] - eps_occ[:, None])).reshape(-1, LANES)
    chol_t = jnp.transpose(chol.reshape(shard_virtuals, occupied, width), (1, 0, 2))
    chol_cols = gather(chol_t, "row")
    factor = chol_t
    sums = []
    for step in range(ITERS):
        if shard_virtuals % 8:
            rows = gather(factor, "col")
            turn = jnp.zeros((1,), jnp.int32)
        else:
            rows = passed(factor, "col")
            turn = jnp.full((1,), n_col - col_index, jnp.int32)
        cols = chol_cols if step == 0 else gather(factor, "row")
        partial_value = update(turn, rows, cols, chol_cols, rpair, cpair)
        if shard_virtuals % 8:
            partial_value = jnp.transpose(
                partial_value.reshape(occupied, n_col, shard_virtuals, width), (1, 0, 2, 3)
            )
        work = lax.psum_scatter(partial_value, "col", scatter_dimension=0, tiled=False)
        factor = chol_t + work
        sums.append(jnp.sum(chol_t * work))
    energies = lax.psum(jnp.stack(sums), ("row", "col"))
    return jnp.transpose(work, (1, 0, 2)).reshape(shard, width), energies / scale


def solution(mesh):
    placed = (P(("row", "col"), None), P(), P())
    return jax.shard_map(
        shards,
        mesh=mesh,
        in_specs=placed,
        out_specs=(P(("row", "col"), None), P()),
        check_vma=False,
    )
```
